256 devices in a mesh: pb: 8 (over x, core), ka: 32 (over z, y).
Axes of the slice: x: 4, y: 4, z: 8, core: 2. Of those that a mesh axis runs over, the one named last changes fastest.
Arguments:
- queries: bfloat16 [32768, 512], P(('pb', 'ka')), may hold values from -9 to 9
- keys: bfloat16 [32768, 512], P(('ka', 'pb')), may hold values from -6 to 6
- values: bfloat16 [32768, 512], P(('ka', 'pb')), may hold values from -6 to 6
- block_pairs: int32 [6400, 2], replicated, may hold values from 0 to 255, as said below
- doc_lengths: int32 [16], replicated, may hold values from 1 to 8192, 32768 in all
Outputs:
- attended: bfloat16 [32768, 512], P(('pb', 'ka'))
The draws below stay inside these ranges and needn't reach their ends.
Inputs may be any that keep to these rules, and one draw needn't show every extreme that they name: `block_pairs`: each row is (query block, key block) with the key block at most the query block; rows come grouped by query block, 25 rows each, and the first row of each group is the block with itself; a pair may appear more than once.
All inputs are finite; a program needn't handle non-finite values.
Results may differ from the reference program's by a relative error of at most 0.02.
Values may be sent and summed in bfloat16 or wider, within the bound.
No kernel may reach another device: no remote copies, remote signals or barrier semaphores. Data moves between devices by JAX's collectives and lax.ppermute only.
A program may use at most 64 MiB of HBM per device.

```python
import math
import jax
import jax.numpy as jnp
import numpy as np
from jax import lax

H = 4
DH = 128
BLK = 128
NDOC = 16
SEQ = 32768
KROWS = 1024
PER_ROW = 25
NPAIRS = 6400
DOC_MOST = 8192
N_KA = 32


def shared_fields(key):
    base = jnp.clip(jax.random.normal(jax.random.fold_in(key, 11), (SEQ, H * DH), jnp.float32), -6.0, 6.0)
    column_sign = jnp.where(jax.random.normal(jax.random.fold_in(key, 14), (H * DH,), jnp.float32) >= 0.0, 1.0, -1.0)[None, :]
    position = jnp.arange(SEQ, dtype=jnp.int32)[:, None]
    block_of = position // BLK
    anchor = (position % BLK == BLK // 8) & (block_of % 4 == 0)
    return (base, column_sign, anchor, position, block_of)


def draw_keys(key, part):
    base, column_sign, anchor, position, block_of = shared_fields(key)
    result = base
    result = jnp.where(anchor, 6.0 * column_sign, result)
    return result.astype(jnp.bfloat16)


def draw_queries(key, part):
    base, column_sign, anchor, position, block_of = shared_fields(key)
    fresh = jnp.clip(jax.random.normal(jax.random.fold_in(key, 13), (SEQ, H * DH), jnp.float32), -6.0, 6.0)
    other = jax.random.normal(jax.random.fold_in(key, 16), (SEQ, H * DH), jnp.float32)
    toward = (position % BLK == BLK // 2) & (block_of % 4 == 0)
    strong = position % BLK == 3 * BLK // 4
    result = jnp.where(toward, jnp.clip(2.0 * column_sign + fresh, -9.0, 9.0), jnp.where(strong, jnp.clip(4.0 * other, -9.0, 9.0), fresh))
    return result.astype(jnp.bfloat16)


def draw_block_pairs(key, part):
    row_index = jnp.arange(NPAIRS, dtype=jnp.int32)
    query_block = row_index // PER_ROW
    within = row_index % PER_ROW
    random_block = jax.random.randint(key, (NPAIRS,), 0, query_block + 1, dtype=jnp.int32)
    previous = jnp.maximum(query_block - 1, 0)
    key_block = jnp.where(within == 0, query_block, jnp.where(within == 1, previous, random_block))
    return jnp.stack([query_block, key_block], axis=1).astype(jnp.int32)


def levels(key, extent, split, low, largest):
    def one(dim, parts):
        steps = jax.random.uniform(jax.random.fold_in(jax.random.fold_in(key, 6), dim), (parts,), jnp.float32, low / len(split), largest / len(split))
        return jnp.repeat(jnp.exp(steps), extent[dim] // parts).reshape((-1,) + (1,) * (len(extent) - dim - 1))

    loudness = one(*split[0])
    for cut in split[1:]:
        loudness = loudness * one(*cut)
    return loudness


def length_profile(count, total, most, skew):
    loads = [(1 << 20) // math.isqrt(rank ** skew) + 1 for rank in range(2, count + 1)]
    surplus, holding = total - most - (count - 1), [1] * (count - 1)
    while surplus > 0:
        movable = [i for i in range(count - 1) if holding[i] < most]
        mass, budget = sum([loads[i] for i in movable]), surplus
        for i in movable:
            more = min(most - holding[i], max(1, budget * loads[i] // mass), surplus)
            holding[i] = holding[i] + more
            surplus = surplus - more
    return np.array([most] + holding)


def uneven_parts(key, number_of, total, reach, skew):
    if number_of == 2:
        one = jax.random.randint(key, (), max(1, total - reach), min(reach, total - 1) + 1)
        return jnp.stack([one, total - one])
    lengths = jnp.asarray(length_profile(number_of, total, reach, skew), jnp.int32)
    couples = (number_of - 1) // 2
    giver, sink = lengths[1:1 + 2 * couples:2], lengths[2:2 + 2 * couples:2]
    room = jnp.minimum(giver - 1, reach - sink)
    moved = jax.random.randint(jax.random.fold_in(key, 1), (couples,), 0, 1 << 20) % (room + 1)
    lengths = lengths.at[1:1 + 2 * couples:2].set(giver - moved).at[2:2 + 2 * couples:2].set(sink + moved)
    return lengths[jax.random.permutation(jax.random.fold_in(key, 2), number_of)]


def scatter_about(key, shape, deviation, most, cuts=(), held_as=jnp.bfloat16):
    values = jax.random.normal(key, shape, jnp.float32) * deviation
    if len(cuts) > 0:
        values = levels(key, shape, cuts, -0.22, 0.18) * values
    return jnp.clip(values, min=-most, max=most).astype(held_as)


def setup_inputs(seed: int = 0) -> dict:
    seeds = jax.random.split(jax.random.key(seed), 6)
    queries = draw_queries(jax.random.fold_in(seeds[5], 71), 0)
    keys = draw_keys(jax.random.fold_in(seeds[5], 71), 0)
    values = scatter_about(seeds[2], (SEQ, H * DH), 1.0, 6.0, ((0, 256),))
    block_pairs = draw_block_pairs(jax.random.fold_in(seeds[5], 71), 0)
    doc_lengths = uneven_parts(seeds[4], NDOC, SEQ, DOC_MOST, 2).astype(jnp.int32)
    return {"queries": queries, "keys": keys, "values": values, "block_pairs": block_pairs, "doc_lengths": doc_lengths}


masked_fill = -1e+30

def document_of(positions, doc_lengths):
    doc_ends = jnp.cumsum(doc_lengths)
    return lax.optimization_barrier(jnp.sum((positions[:, None] >= doc_ends[None, :]).astype(jnp.int32), axis=1))

def reference(queries, keys, values, block_pairs, doc_lengths):
    seq_len = queries.shape[0]
    blocks = seq_len // BLK
    block_mask = jnp.zeros((blocks, blocks), jnp.int32).at[block_pairs[:, 0], block_pairs[:, 1]].set(1)
    key_pos = jnp.arange(seq_len, dtype=jnp.int32)
    key_doc = document_of(key_pos, doc_lengths)
    keys_wide = keys.astype(jnp.float32).reshape(seq_len, H, DH)
    values_wide = values.astype(jnp.float32).reshape(N_KA, KROWS, H, DH)
    group_rows = min(512, seq_len)
    scale = 1.0 / math.sqrt(DH)

    def per_group(group_index):
        offset = (group_index * group_rows).astype(jnp.int32)
        query_part = lax.dynamic_slice_in_dim(queries, offset, group_rows, 0).astype(jnp.float32).reshape(group_rows, H, DH)
        query_pos = offset + jnp.arange(group_rows, dtype=jnp.int32)
        query_doc = document_of(query_pos, doc_lengths)
        block_rows = lax.dynamic_slice_in_dim(block_mask, (offset // BLK).astype(jnp.int32), group_rows // BLK, 0)
        expanded = jnp.repeat(jnp.repeat(block_rows, BLK, axis=0), BLK, axis=1) > 0
        allowed = expanded & (query_doc[:, None] == key_doc[None, :]) & (key_pos[None, :] <= query_pos[:, None])
        scores = jnp.einsum('ghd,khd->hgk', query_part, keys_wide) * scale
        scores = jnp.where(allowed[None], scores, masked_fill).reshape(H, group_rows, N_KA, KROWS)
        allowed_four = allowed.reshape(group_rows, N_KA, KROWS)[None]
        shard_max = lax.optimization_barrier(jnp.max(scores, axis=3))
        highest = lax.optimization_barrier(jnp.max(shard_max, axis=2))
        factor = jnp.exp(shard_max - highest[:, :, None])
        weights = jnp.where(allowed_four, jnp.exp(scores - shard_max[:, :, :, None]), 0.0).astype(jnp.bfloat16)
        weights = lax.optimization_barrier(weights).astype(jnp.float32)
        part_num = jnp.einsum('hgsk,skhd->sghd', weights, values_wide)
        part_num = (part_num * jnp.transpose(factor, (2, 1, 0))[:, :, :, None]).astype(jnp.bfloat16)
        part_den = (lax.optimization_barrier(jnp.sum(weights, axis=3)) * factor).astype(jnp.bfloat16)
        part_num = lax.optimization_barrier(part_num).astype(jnp.float32)
        part_den = lax.optimization_barrier(part_den).astype(jnp.float32)
        numer = lax.optimization_barrier(jnp.sum(part_num, axis=0))
        denom = lax.optimization_barrier(jnp.sum(part_den, axis=2))
        result = numer / jnp.transpose(denom)[:, :, None]
        return result.reshape(group_rows, H * DH).astype(jnp.bfloat16)
    outputs = lax.map(per_group, jnp.arange(seq_len // group_rows, dtype=jnp.int32))
    return outputs.reshape(seq_len, H * DH)
```

```python
import functools
import math

import jax
import jax.numpy as jnp
from jax import lax
from jax.experimental import pallas as pl
from jax.experimental.pallas import tpu as pltpu
from jax.sharding import Mesh
from jax.sharding import PartitionSpec as P

H = 4
DH = 128
BLK = 128
NX, NC, NZ, NY = 4, 2, 8, 4
PLANE = 32
NQ = NX * NY
PLANES = 3
NK = PLANES * NY * NC
STAT_ROWS = 16
ROWS = DH + STAT_ROWS
UNROLL = 4
LIST = NQ * NK + UNROLL
NEG = -1e30
SCALE = math.log2(math.e) / math.sqrt(DH)


def device(x, c, z, y):
    return ((x * NC + c) * NZ + z) * NY + y


def transpose_pairs():
    pairs = []
    for x in range(NX):
        for c in range(NC):
            for z in range(NZ):
                for y in range(NY):
                    pairs.append((device(x, c, z, y), device(z // 2, z % 2, 2 * x + c, y)))
    return pairs


def pack_queries_kernel(q_ref, out_ref):
    for h in range(H):
        part = q_ref[:, h * DH : (h + 1) * DH].astype(jnp.float32).T.astype(jnp.bfloat16)
        for x in range(NX):
            out_ref[x * H + h] = part


def pack_keys_kernel(k_ref, v_ref, out_ref):
    for h in range(H):
        out_ref[h, 0] = k_ref[:, h * DH : (h + 1) * DH]
        out_ref[h, 1] = (
            v_ref[:, h * DH : (h + 1) * DH].astype(jnp.float32).T.astype(jnp.bfloat16)
        )


def attend_kernel(
    need_ref, qblk_ref, kblk_ref, start_ref, q_ref, *refs
):
    kv_refs, (out_ref, kv, acc, top, total, pairs, sems) = refs[: 2 * PLANES], refs[2 * PLANES :]
    copies = []
    for n, ref in enumerate(kv_refs):
        copy = pltpu.make_async_copy(ref, kv.at[pl.ds(n * NY, NY)], sems.at[n])
        copy.start()
        copies.append(copy)

    acc[...] = jnp.zeros_like(acc)
    top[...] = jnp.full_like(top, NEG)
    total[...] = jnp.zeros_like(total)

    def list_row(j, count):
        for s in range(NK):
            pairs[count] = j * NK + s
            count = count + jnp.where(need_ref[j, s] > 0, 1, 0)
        return count

    count = lax.fori_loop(0, NQ, list_row, jnp.int32(0))
    for u in range(UNROLL):
        pairs[count + u] = NQ * NK
    for copy in copies:
        copy.wait()

    key_row = lax.broadcasted_iota(jnp.int32, (BLK, BLK), 0)
    lane = lax.broadcasted_iota(jnp.int32, (1, BLK), 1)

    def step(i, carry):
        done = []
        for u in range(UNROLL):
            pair = pairs[i * UNROLL + u]
            j = pair // NK
            s = pair - j * NK
            jq = jnp.minimum(j, NQ - 1)
            base = kblk_ref[s] * BLK
            low = start_ref[jq] - base
            high = qblk_ref[jq] * BLK + lane - base
            scores = jnp.dot(kv[s, 0], q_ref[jq], preferred_element_type=jnp.float32)
            allowed = (key_row >= low) & (key_row <= high)
            scores = jnp.where(allowed, scores * SCALE, NEG)
            peak = jnp.max(scores, axis=0, keepdims=True)
            weights = jnp.exp2(scores - peak)
            mass = jnp.sum(weights, axis=0, keepdims=True)
            part = jnp.dot(
                kv[s, 1], weights.astype(jnp.bfloat16), preferred_element_type=jnp.float32
            )
            done.append((j, peak, mass, part))
        for j, peak, mass, part in done:
            old = top[j]
            new = jnp.maximum(old, peak)
            keep = jnp.exp2(old - new)
            gain = jnp.exp2(peak - new)
            top[j] = new
            total[j] = total[j] * keep + mass * gain
            acc[j] = acc[j] * keep + part * gain
        return carry

    lax.fori_loop(0, (count + UNROLL - 1) // UNROLL, step, 0)

    row = lax.broadcasted_iota(jnp.int32, (STAT_ROWS, BLK), 0)

    def finish(j, carry):
        mass = total[j]
        some = mass > 0.0
        safe = jnp.where(some, mass, 1.0)
        out_ref[j, pl.ds(0, DH), :] = (acc[j] * (1.0 / safe)).astype(jnp.bfloat16)
        level = jnp.where(some, top[j] + jnp.log2(safe), NEG)
        first = level.astype(jnp.bfloat16).astype(jnp.float32)
        second = (level - first).astype(jnp.bfloat16).astype(jnp.float32)
        third = level - first - second
        stat = jnp.where(row == 0, first, jnp.where(row == 1, second, jnp.where(row == 2, third, 0.0)))
        out_ref[j, pl.ds(DH, STAT_ROWS), :] = stat.astype(jnp.bfloat16)
        return carry

    lax.fori_loop(0, NQ, finish, 0)


def combine_kernel(parts_ref, out_ref):
    for h in range(H):
        levels = []
        for r in range(NX):
            stat = parts_ref[r * H + h, DH:, :].astype(jnp.float32)
            levels.append(stat[0:1] + stat[1:2] + stat[2:3])
        peak = functools.reduce(jnp.maximum, levels)
        shares = [jnp.exp2(level - peak) for level in levels]
        inverse = 1.0 / functools.reduce(jnp.add, shares)
        value = functools.reduce(
            jnp.add,
            [
                parts_ref[r * H + h, :DH, :].astype(jnp.float32) * (shares[r] * inverse)
                for r in range(NX)
            ],
        )
        out_ref[:, h * DH : (h + 1) * DH] = value.T.astype(jnp.bfloat16)


VMEM = pl.BlockSpec(memory_space=pltpu.VMEM)
SMEM = pl.BlockSpec(memory_space=pltpu.SMEM)
ANY = pl.BlockSpec(memory_space=pl.ANY)


def on_device(queries, keys, values, block_pairs, doc_lengths):
    x, c, z, y = (lax.axis_index(name) for name in ("x", "c", "z", "y"))
    bf16 = jnp.bfloat16

    packed = pl.pallas_call(
        pack_keys_kernel,
        out_shape=jax.ShapeDtypeStruct((H, 2, BLK, DH), bf16),
        in_specs=[VMEM, VMEM],
        out_specs=VMEM,
    )(keys, values)
    moved = lax.ppermute(queries, ("x", "c", "z", "y"), transpose_pairs())
    here = lax.all_to_all(packed, "y", 0, 0, tiled=True)
    below = [here] + [
        lax.ppermute(here, "z", [(n, n + d) for n in range(NZ - d)]) for d in range(1, PLANES)
    ]
    other = [lax.ppermute(b, "c", [(0, 1), (1, 0)]) for b in below]

    spread = pl.pallas_call(
        pack_queries_kernel,
        out_shape=jax.ShapeDtypeStruct((NQ, DH, BLK), bf16),
        in_specs=[VMEM],
        out_specs=VMEM,
    )(moved)
    mine = lax.all_to_all(spread, ("x", "y"), 0, 0, tiled=True)

    slot = jnp.arange(NQ, dtype=jnp.int32)
    query_block = PLANE * z + 4 * (2 * (slot // NY) + c) + slot % NY
    slot = jnp.arange(NK, dtype=jnp.int32)
    plane = (slot // NY) % PLANES
    core = jnp.where(slot < PLANES * NY, c, 1 - c)
    key_block = PLANE * (z - plane) + 8 * (slot % NY) + 2 * x + core
    ends = jnp.sum(
        jnp.where(
            jnp.arange(16)[:, None] <= jnp.arange(16)[None, :], doc_lengths[:, None], 0
        ),
        axis=0,
    )
    token = query_block[:, None] * BLK + jnp.arange(BLK, dtype=jnp.int32)[None, :]
    start = jnp.max(jnp.where(ends[:, None, None] <= token[None], ends[:, None, None], 0), axis=0)
    first = jnp.max(
        jnp.where(ends[:, None] <= query_block[None] * BLK, ends[:, None], 0), axis=0
    )
    hit_query = (block_pairs[:, 0][None, :] == query_block[:, None]).astype(bf16)
    hit_key = (block_pairs[:, 1][None, :] == key_block[:, None]).astype(bf16)
    listed = lax.dot_general(
        hit_query, hit_key, (((1,), (1,)), ((), ())), preferred_element_type=jnp.float32
    )
    need = (
        (listed > 0.5)
        & (key_block[None, :] * BLK + (BLK - 1) >= first[:, None])
        & (key_block[None, :] <= query_block[:, None])
    ).astype(jnp.int32)

    parts = pl.pallas_call(
        attend_kernel,
        out_shape=jax.ShapeDtypeStruct((NQ, ROWS, BLK), bf16),
        in_specs=[SMEM, SMEM, SMEM, VMEM, VMEM] + [ANY] * (2 * PLANES),
        out_specs=VMEM,
        scratch_shapes=[
            pltpu.VMEM((NK, 2, BLK, DH), bf16),
            pltpu.VMEM((NQ + 1, DH, BLK), jnp.float32),
            pltpu.VMEM((NQ + 1, 1, BLK), jnp.float32),
            pltpu.VMEM((NQ + 1, 1, BLK), jnp.float32),
            pltpu.SMEM((LIST,), jnp.int32),
            pltpu.SemaphoreType.DMA((2 * PLANES,)),
        ],
        compiler_params=pltpu.CompilerParams(vmem_limit_bytes=24 << 20),
    )(need, query_block, key_block, start.reshape(NQ, 1, BLK), mine, *below, *other)

    gathered = lax.all_to_all(parts, ("x", "y"), 0, 0, tiled=True)
    result = pl.pallas_call(
        combine_kernel,
        out_shape=jax.ShapeDtypeStruct((BLK, H * DH), bf16),
        in_specs=[VMEM],
        out_specs=VMEM,
    )(gathered)
    return lax.ppermute(result, ("x", "c", "z", "y"), transpose_pairs())


def solution(mesh):
    fine = Mesh(mesh.devices.reshape(NX, NC, NZ, NY), ("x", "c", "z", "y"))
    return jax.shard_map(
        on_device,
        mesh=fine,
        in_specs=(
            P(("x", "c", "z", "y"), None),
            P(("z", "y", "x", "c"), None),
            P(("z", "y", "x", "c"), None),
            P(),
            P(),
        ),
        out_specs=P(("x", "c", "z", "y"), None),
        check_vma=False,
    )
```

```python
import functools
import math

import jax
import jax.numpy as jnp
from jax import lax
from jax.experimental import pallas as pl
from jax.experimental.pallas import tpu as pltpu
from jax.sharding import Mesh
from jax.sharding import PartitionSpec as P

H = 4
DH = 128
BLK = 128
NX, NC, NZ, NY = 4, 2, 8, 4
PLANE = 32
NQ = NX * NY
PLANES = 3
NK = PLANES * NY * NC
STAT_ROWS = 16
ROWS = DH + STAT_ROWS
UNROLL = 4
LIST = NQ * NK + UNROLL
NEG = -1e30
SCALE = math.log2(math.e) / math.sqrt(DH)


def device(x, c, z, y):
    return ((x * NC + c) * NZ + z) * NY + y


PLACE = [list(range(NZ)) for _ in range(NZ)]
LIVES = [
    [[PLACE[(z + 1) % NZ].index(2 * x + c) for c in range(NC)] for x in range(NX)] for z in range(NZ)
]


def transpose_pairs(back):
    pairs = []
    for x in range(NX):
        for c in range(NC):
            for z in range(NZ):
                for y in range(NY):
                    p = 2 * x + c
                    home = device(x, c, z, y)
                    work = device(PLACE[p][z] // 2, PLACE[p][z] % 2, (p - 1) % NZ, y)
                    pairs.append((work, home) if back else (home, work))
    return pairs


def ring(n, d):
    return [(i, (i + d) % n) for i in range(n)]


def pack_queries_kernel(q_ref, out_ref):
    for h in range(H):
        part = q_ref[:, h * DH : (h + 1) * DH].astype(jnp.float32).T.astype(jnp.bfloat16)
        for x in range(NX):
            out_ref[x * H + h] = part


def pack_keys_kernel(y_ref, k_ref, v_ref, *out_refs):
    for d, out_ref in enumerate(out_refs):
        at = pl.ds(pl.multiple_of(lax.rem(y_ref[0] + d, H) * DH, DH), DH)
        out_ref[0] = k_ref[:, at]
        out_ref[1] = v_ref[:, at].astype(jnp.float32).T.astype(jnp.bfloat16)


def attend_kernel(
    need_ref, qblk_ref, kblk_ref, start_ref, q_ref, *refs
):
    kv_refs, (out_ref, kv, acc, top, total, pairs, sems) = refs[: 2 * PLANES], refs[2 * PLANES :]
    copies = []
    for n, ref in enumerate(kv_refs):
        copy = pltpu.make_async_copy(ref, kv.at[pl.ds(n * NY, NY)], sems.at[n])
        copy.start()
        copies.append(copy)

    acc[...] = jnp.zeros_like(acc)
    top[...] = jnp.full_like(top, NEG)
    total[...] = jnp.zeros_like(total)

    def list_row(j, count):
        for s in range(NK):
            pairs[count] = j * NK + s
            count = count + jnp.where(need_ref[j, s] > 0, 1, 0)
        return count

    count = lax.fori_loop(0, NQ, list_row, jnp.int32(0))
    for u in range(UNROLL):
        pairs[count + u] = NQ * NK
    for copy in copies:
        copy.wait()

    key_row = lax.broadcasted_iota(jnp.int32, (BLK, BLK), 0)
    lane = lax.broadcasted_iota(jnp.int32, (1, BLK), 1)

    def step(i, carry):
        done = []
        for u in range(UNROLL):
            pair = pairs[i * UNROLL + u]
            j = pair // NK
            s = pair - j * NK
            jq = jnp.minimum(j, NQ - 1)
            base = kblk_ref[s] * BLK
            low = start_ref[jq] - base
            high = qblk_ref[jq] * BLK + lane - base
            scores = jnp.dot(kv[s, 0], q_ref[jq], preferred_element_type=jnp.float32)
            allowed = (key_row >= low) & (key_row <= high)
            scores = jnp.where(allowed, scores * SCALE, NEG)
            peak = jnp.max(scores, axis=0, keepdims=True)
            weights = jnp.exp2(scores - peak)
            mass = jnp.sum(weights, axis=0, keepdims=True)
            part = jnp.dot(
                kv[s, 1], weights.astype(jnp.bfloat16), preferred_element_type=jnp.float32
            )
            done.append((j, peak, mass, part))
        for j, peak, mass, part in done:
            old = top[j]
            new = jnp.maximum(old, peak)
            keep = jnp.exp2(old - new)
            gain = jnp.exp2(peak - new)
            top[j] = new
            total[j] = total[j] * keep + mass * gain
            acc[j] = acc[j] * keep + part * gain
        return carry

    lax.fori_loop(0, (count + UNROLL - 1) // UNROLL, step, 0)

    row = lax.broadcasted_iota(jnp.int32, (STAT_ROWS, BLK), 0)

    def finish(j, carry):
        mass = total[j]
        some = mass > 0.0
        safe = jnp.where(some, mass, 1.0)
        out_ref[j, pl.ds(0, DH), :] = (acc[j] * (1.0 / safe)).astype(jnp.bfloat16)
        level = jnp.where(some, top[j] + jnp.log2(safe), NEG)
        first = level.astype(jnp.bfloat16).astype(jnp.float32)
        second = (level - first).astype(jnp.bfloat16).astype(jnp.float32)
        third = level - first - second
        stat = jnp.where(row == 0, first, jnp.where(row == 1, second, jnp.where(row == 2, third, 0.0)))
        out_ref[j, pl.ds(DH, STAT_ROWS), :] = stat.astype(jnp.bfloat16)
        return carry

    lax.fori_loop(0, NQ, finish, 0)


def combine_kernel(parts_ref, out_ref):
    for h in range(H):
        levels = []
        for r in range(NX):
            stat = parts_ref[r * H + h, DH:, :].astype(jnp.float32)
            levels.append(stat[0:1] + stat[1:2] + stat[2:3])
        peak = functools.reduce(jnp.maximum, levels)
        shares = [jnp.exp2(level - peak) for level in levels]
        inverse = 1.0 / functools.reduce(jnp.add, shares)
        value = functools.reduce(
            jnp.add,
            [
                parts_ref[r * H + h, :DH, :].astype(jnp.float32) * (shares[r] * inverse)
                for r in range(NX)
            ],
        )
        out_ref[:, h * DH : (h + 1) * DH] = value.T.astype(jnp.bfloat16)


VMEM = pl.BlockSpec(memory_space=pltpu.VMEM)
SMEM = pl.BlockSpec(memory_space=pltpu.SMEM)
ANY = pl.BlockSpec(memory_space=pl.ANY)
SMALL = pltpu.CompilerParams(vmem_limit_bytes=4 << 20)


def on_device(queries, keys, values, block_pairs, doc_lengths):
    x, c, z, y = (lax.axis_index(name) for name in ("x", "c", "z", "y"))
    bf16 = jnp.bfloat16

    piece = jax.ShapeDtypeStruct((2, BLK, DH), bf16)
    split = pl.pallas_call(
        pack_keys_kernel,
        out_shape=[piece] * NY,
        in_specs=[SMEM, VMEM, VMEM],
        out_specs=[VMEM] * NY,
        compiler_params=SMALL,
    )(y.reshape(1), keys, values)
    moved = lax.ppermute(queries, ("x", "c", "z", "y"), transpose_pairs(False))
    pieces = [split[0]] + [lax.ppermute(split[d], "y", ring(NY, d)) for d in range(1, NY)]

    spread = pl.pallas_call(
        pack_queries_kernel,
        out_shape=jax.ShapeDtypeStruct((NQ, DH, BLK), bf16),
        in_specs=[VMEM],
        out_specs=VMEM,
        compiler_params=SMALL,
    )(moved)
    spread, *pieces = lax.optimization_barrier((spread, *pieces))
    mine = lax.all_to_all(spread, ("x", "y"), 0, 0, tiled=True)

    here = jnp.stack(pieces)
    near = [here, lax.ppermute(here, "z", ring(NZ, 1)), lax.ppermute(here, "z", ring(NZ, -1))]
    other = [lax.ppermute(b, "c", ring(NC, 1)) for b in near]

    slot = jnp.arange(NQ, dtype=jnp.int32)
    lives = jnp.repeat(jnp.asarray(LIVES, jnp.int32)[z, :, c], NY)
    query_block = PLANE * lax.rem(z + 1, NZ) + NY * lives + slot % NY
    slot = jnp.arange(NK, dtype=jnp.int32)
    group = (slot // NY) % PLANES
    plane = lax.rem(z + jnp.where(group == 0, 0, jnp.where(group == 1, NZ - 1, 1)), NZ)
    row = lax.rem(y + NY - slot % NY, NY)
    core = jnp.where(slot < PLANES * NY, c, 1 - c)
    key_block = PLANE * plane + 8 * row + 2 * x + core
    ends = jnp.sum(
        jnp.where(
            jnp.arange(16)[:, None] <= jnp.arange(16)[None, :], doc_lengths[:, None], 0
        ),
        axis=0,
    )
    token = query_block[:, None] * BLK + jnp.arange(BLK, dtype=jnp.int32)[None, :]
    start = jnp.max(jnp.where(ends[:, None, None] <= token[None], ends[:, None, None], 0), axis=0)
    first = jnp.max(
        jnp.where(ends[:, None] <= query_block[None] * BLK, ends[:, None], 0), axis=0
    )
    hit_query = (block_pairs[:, 0][None, :] == query_block[:, None]).astype(bf16)
    hit_key = (block_pairs[:, 1][None, :] == key_block[:, None]).astype(bf16)
    listed = lax.dot_general(
        hit_query, hit_key, (((1,), (1,)), ((), ())), preferred_element_type=jnp.float32
    )
    need = (
        (listed > 0.5)
        & (key_block[None, :] * BLK + (BLK - 1) >= first[:, None])
        & (key_block[None, :] <= query_block[:, None])
    ).astype(jnp.int32)

    parts = pl.pallas_call(
        attend_kernel,
        out_shape=jax.ShapeDtypeStruct((NQ, ROWS, BLK), bf16),
        in_specs=[SMEM, SMEM, SMEM, VMEM, VMEM] + [ANY] * (2 * PLANES),
        out_specs=VMEM,
        scratch_shapes=[
            pltpu.VMEM((NK, 2, BLK, DH), bf16),
            pltpu.VMEM((NQ + 1, DH, BLK), jnp.float32),
            pltpu.VMEM((NQ + 1, 1, BLK), jnp.float32),
            pltpu.VMEM((NQ + 1, 1, BLK), jnp.float32),
            pltpu.SMEM((LIST,), jnp.int32),
            pltpu.SemaphoreType.DMA((2 * PLANES,)),
        ],
        compiler_params=pltpu.CompilerParams(vmem_limit_bytes=24 << 20),
    )(need, query_block, key_block, start.reshape(NQ, 1, BLK), mine, *near, *other)

    gathered = lax.all_to_all(parts, ("x", "y"), 0, 0, tiled=True)
    result = pl.pallas_call(
        combine_kernel,
        out_shape=jax.ShapeDtypeStruct((BLK, H * DH), bf16),
        in_specs=[VMEM],
        out_specs=VMEM,
        compiler_params=SMALL,
    )(gathered)
    return lax.ppermute(result, ("x", "c", "z", "y"), transpose_pairs(True))


def solution(mesh):
    fine = Mesh(mesh.devices.reshape(NX, NC, NZ, NY), ("x", "c", "z", "y"))
    return jax.shard_map(
        on_device,
        mesh=fine,
        in_specs=(
            P(("x", "c", "z", "y"), None),
            P(("z", "y", "x", "c"), None),
            P(("z", "y", "x", "c"), None),
            P(),
            P(),
        ),
        out_specs=P(("x", "c", "z", "y"), None),
        check_vma=False,
    )
```

```python
import functools
import math

import jax
import jax.numpy as jnp
from jax import lax
from jax.experimental import pallas as pl
from jax.experimental.pallas import tpu as pltpu
from jax.sharding import Mesh
from jax.sharding import PartitionSpec as P

H = 4
DH = 128
BLK = 128
NX, NC, NZ, NY = 4, 2, 8, 4
PLANE = 32
NS = 2
NQ = NS * NY
PLANES = 3
GROUP = 2 * NY
GROUPS = PLANES * NC
NK = GROUP * GROUPS
STAT_ROWS = 16
ROWS = DH + STAT_ROWS
UNROLL = 4
LIST = NQ * GROUP + UNROLL
NEG = -1e30
SCALE = math.log2(math.e) / math.sqrt(DH)


AXES = ("high", "low", "c", "z", "y")


def device(x, c, z, y):
    return ((x * NC + c) * NZ + z) * NY + y


PLACE = [list(range(NZ)) for _ in range(NZ)]
LIVES = [
    [[PLACE[(z + 1) % NZ].index(2 * x + c) for c in range(NC)] for x in range(NX)] for z in range(NZ)
]


def transpose_pairs(back):
    pairs = []
    for x in range(NX):
        for c in range(NC):
            for z in range(NZ):
                for y in range(NY):
                    p = 2 * x + c
                    home = device(x, c, z, y)
                    work = device(PLACE[p][z] // 2, PLACE[p][z] % 2, (p - 1) % NZ, y)
                    pairs.append((work, home) if back else (home, work))
    return pairs


def ring(n, d):
    return [(i, (i + d) % n) for i in range(n)]


def pack_queries_kernel(q_ref, out_ref):
    for h in range(H):
        part = q_ref[:, h * DH : (h + 1) * DH].astype(jnp.float32).T.astype(jnp.bfloat16)
        for n in range(NS):
            out_ref[n * H + h] = part


def pack_keys_kernel(y_ref, k_ref, v_ref, *out_refs):
    for d, out_ref in enumerate(out_refs):
        at = pl.ds(pl.multiple_of(lax.rem(y_ref[0] + d, H) * DH, DH), DH)
        out_ref[0] = k_ref[:, at]
        out_ref[1] = v_ref[:, at].astype(jnp.float32).T.astype(jnp.bfloat16)


def join_kernel(*refs):
    out_ref = refs[-1]
    at = 0
    for ref in refs[:-1]:
        out_ref[at : at + ref.shape[0]] = ref[...]
        at += ref.shape[0]


def join(parts):
    count = sum(p.shape[0] for p in parts)
    return pl.pallas_call(
        join_kernel,
        out_shape=jax.ShapeDtypeStruct((count,) + parts[0].shape[1:], parts[0].dtype),
        in_specs=[VMEM] * len(parts),
        out_specs=VMEM,
        compiler_params=SMALL,
    )(*parts)


def attend_kernel(need_ref, qblk_ref, kblk_ref, start_ref, q_ref, *refs):
    kv_refs, (out_ref, acc, top, total, pairs) = refs[:GROUPS], refs[GROUPS:]
    acc[...] = jnp.zeros_like(acc)
    top[...] = jnp.full_like(top, NEG)
    total[...] = jnp.zeros_like(total)
    key_row = lax.broadcasted_iota(jnp.int32, (BLK, BLK), 0)
    lane = lax.broadcasted_iota(jnp.int32, (1, BLK), 1)

    for g, kv in enumerate(kv_refs):

        def list_row(j, count, g=g):
            for s in range(GROUP):
                pairs[count] = j * GROUP + s
                count = count + need_ref[j, g * GROUP + s]
            return count

        count = lax.fori_loop(0, NQ, list_row, jnp.int32(0))
        for u in range(UNROLL):
            pairs[count + u] = NQ * GROUP

        def step(i, carry, g=g, kv=kv):
            done = []
            for u in range(UNROLL):
                pair = pairs[i * UNROLL + u]
                j = pair // GROUP
                s = pair - j * GROUP
                jq = jnp.minimum(j, NQ - 1)
                base = kblk_ref[g * GROUP + s] * BLK
                low = start_ref[jq] - base
                high = qblk_ref[jq] * BLK + lane - base
                scores = jnp.dot(kv[s, 0], q_ref[jq], preferred_element_type=jnp.float32)
                allowed = (key_row >= low) & (key_row <= high)
                scores = jnp.where(allowed, scores * SCALE, NEG)
                peak = jnp.max(scores, axis=0, keepdims=True)
                weights = jnp.exp2(scores - peak)
                mass = jnp.sum(weights, axis=0, keepdims=True)
                part = jnp.dot(
                    kv[s, 1], weights.astype(jnp.bfloat16), preferred_element_type=jnp.float32
                )
                done.append((j, peak, mass, part))
            for j, peak, mass, part in done:
                old = top[j]
                new = jnp.maximum(old, peak)
                keep = jnp.exp2(old - new)
                gain = jnp.exp2(peak - new)
                top[j] = new
                total[j] = total[j] * keep + mass * gain
                acc[j] = acc[j] * keep + part * gain
            return carry

        lax.fori_loop(0, (count + UNROLL - 1) // UNROLL, step, 0)

    row = lax.broadcasted_iota(jnp.int32, (STAT_ROWS, BLK), 0)

    def finish(j, carry):
        mass = total[j]
        some = mass > 0.0
        safe = jnp.where(some, mass, 1.0)
        out_ref[j, pl.ds(0, DH), :] = (acc[j] * (1.0 / safe)).astype(jnp.bfloat16)
        level = jnp.where(some, top[j] + jnp.log2(safe), NEG)
        first = level.astype(jnp.bfloat16).astype(jnp.float32)
        second = (level - first).astype(jnp.bfloat16).astype(jnp.float32)
        third = level - first - second
        stat = jnp.where(row == 0, first, jnp.where(row == 1, second, jnp.where(row == 2, third, 0.0)))
        out_ref[j, pl.ds(DH, STAT_ROWS), :] = stat.astype(jnp.bfloat16)
        return carry

    lax.fori_loop(0, NQ, finish, 0)


def combine_kernel(parts_ref, out_ref):
    for h in range(H):
        levels = []
        for r in range(NS):
            stat = parts_ref[r * H + h, DH:, :].astype(jnp.float32)
            levels.append(stat[0:1] + stat[1:2] + stat[2:3])
        peak = functools.reduce(jnp.maximum, levels)
        shares = [jnp.exp2(level - peak) for level in levels]
        inverse = 1.0 / functools.reduce(jnp.add, shares)
        value = functools.reduce(
            jnp.add,
            [
                parts_ref[r * H + h, :DH, :].astype(jnp.float32) * (shares[r] * inverse)
                for r in range(NS)
            ],
        )
        out_ref[:, h * DH : (h + 1) * DH] = value.T.astype(jnp.bfloat16)


VMEM = pl.BlockSpec(memory_space=pltpu.VMEM)
SMEM = pl.BlockSpec(memory_space=pltpu.SMEM)
SMALL = pltpu.CompilerParams(vmem_limit_bytes=4 << 20)


def on_device(queries, keys, values, block_pairs, doc_lengths):
    high, low, c, z, y = (lax.axis_index(name) for name in AXES)
    x = 2 * high + low
    bf16 = jnp.bfloat16

    piece = jax.ShapeDtypeStruct((2, BLK, DH), bf16)
    split = pl.pallas_call(
        pack_keys_kernel,
        out_shape=[piece] * NY,
        in_specs=[SMEM, VMEM, VMEM],
        out_specs=[VMEM] * NY,
        compiler_params=SMALL,
    )(y.reshape(1), keys, values)
    moved = lax.ppermute(queries, AXES, transpose_pairs(False))
    pieces = [split[0]] + [lax.ppermute(split[d], "y", ring(NY, d)) for d in range(1, NY)]
    moved, *pieces = lax.optimization_barrier((moved, *pieces))

    spread = pl.pallas_call(
        pack_queries_kernel,
        out_shape=jax.ShapeDtypeStruct((NQ, DH, BLK), bf16),
        in_specs=[VMEM],
        out_specs=VMEM,
        compiler_params=SMALL,
    )(moved)
    here = join([p[None] for p in pieces])
    there = lax.ppermute(here, ("high", "low"), [(i, NX - 1 - i) for i in range(NX)])
    spread, there = lax.optimization_barrier((spread, there))
    mine = lax.all_to_all(spread, ("low", "y"), 0, 0, tiled=True)
    here = join([here, there])
    near = [here, lax.ppermute(here, "z", ring(NZ, 1)), lax.ppermute(here, "z", ring(NZ, -1))]
    mine, *near = lax.optimization_barrier((mine, *near))
    other = [lax.ppermute(b, "c", ring(NC, 1)) for b in near]

    slot = jnp.arange(NQ, dtype=jnp.int32)
    lives = jnp.asarray(LIVES, jnp.int32)[z, :, c].reshape(NX // NS, NS)[high]
    lives = jnp.repeat(lives, NY)
    query_block = PLANE * lax.rem(z + 1, NZ) + NY * lives + slot % NY
    slot = jnp.arange(NK, dtype=jnp.int32)
    group = (slot // GROUP) % PLANES
    plane = lax.rem(z + jnp.where(group == 0, 0, jnp.where(group == 1, NZ - 1, 1)), NZ)
    row = lax.rem(y + NY - slot % NY, NY)
    core = jnp.where(slot < PLANES * GROUP, c, 1 - c)
    column = jnp.where(slot // NY % 2 == 0, x, NX - 1 - x)
    key_block = PLANE * plane + 8 * row + 2 * column + core
    ends = jnp.sum(
        jnp.where(
            jnp.arange(16)[:, None] <= jnp.arange(16)[None, :], doc_lengths[:, None], 0
        ),
        axis=0,
    )
    token = query_block[:, None] * BLK + jnp.arange(BLK, dtype=jnp.int32)[None, :]
    start = jnp.max(jnp.where(ends[:, None, None] <= token[None], ends[:, None, None], 0), axis=0)
    first = jnp.max(
        jnp.where(ends[:, None] <= query_block[None] * BLK, ends[:, None], 0), axis=0
    )
    hit_query = (block_pairs[:, 0][None, :] == query_block[:, None]).astype(bf16)
    hit_key = (block_pairs[:, 1][None, :] == key_block[:, None]).astype(bf16)
    listed = lax.dot_general(
        hit_query, hit_key, (((1,), (1,)), ((), ())), preferred_element_type=jnp.float32
    )
    need = (
        (listed > 0.5)
        & (key_block[None, :] * BLK + (BLK - 1) >= first[:, None])
        & (key_block[None, :] <= query_block[:, None])
    ).astype(jnp.int32)

    parts = pl.pallas_call(
        attend_kernel,
        out_shape=jax.ShapeDtypeStruct((NQ, ROWS, BLK), bf16),
        in_specs=[SMEM, SMEM, SMEM] + [VMEM] * (2 + GROUPS),
        out_specs=VMEM,
        scratch_shapes=[
            pltpu.VMEM((NQ + 1, DH, BLK), jnp.float32),
            pltpu.VMEM((NQ + 1, 1, BLK), jnp.float32),
            pltpu.VMEM((NQ + 1, 1, BLK), jnp.float32),
            pltpu.SMEM((LIST,), jnp.int32),
        ],
        compiler_params=pltpu.CompilerParams(vmem_limit_bytes=24 << 20),
    )(need, query_block, key_block, start.reshape(NQ, 1, BLK), mine, *near, *other)

    gathered = lax.all_to_all(parts, ("low", "y"), 0, 0, tiled=True)
    result = pl.pallas_call(
        combine_kernel,
        out_shape=jax.ShapeDtypeStruct((BLK, H * DH), bf16),
        in_specs=[VMEM],
        out_specs=VMEM,
        compiler_params=SMALL,
    )(gathered)
    return lax.ppermute(result, AXES, transpose_pairs(True))


def solution(mesh):
    fine = Mesh(mesh.devices.reshape(NX // NS, NS, NC, NZ, NY), AXES)
    return jax.shard_map(
        on_device,
        mesh=fine,
        in_specs=(
            P(AXES, None),
            P(("z", "y", "high", "low", "c"), None),
            P(("z", "y", "high", "low", "c"), None),
            P(),
            P(),
        ),
        out_specs=P(AXES, None),
        check_vma=False,
    )
```

```python
import functools
import math

import jax
import jax.numpy as jnp
from jax import lax
from jax.experimental import pallas as pl
from jax.experimental.pallas import tpu as pltpu
from jax.sharding import Mesh
from jax.sharding import PartitionSpec as P

H = 4
DH = 128
BLK = 128
NX, NC, NZ, NY = 4, 2, 8, 4
PLANE = 32
NQ = NX * NY
PLANES = 3
NK = PLANES * NY * NC
STAT_ROWS = 16
ROWS = DH + STAT_ROWS
UNROLL = 4
LIST = NQ * NK + UNROLL
NEG = -1e30
SCALE = math.log2(math.e) / math.sqrt(DH)


AXES = ("x", "c", "z", "y")


def device(x, c, z, y):
    return ((x * NC + c) * NZ + z) * NY + y


PLACE = [list(range(NZ)) for _ in range(NZ)]
LIVES = [
    [[PLACE[(z + 1) % NZ].index(2 * x + c) for c in range(NC)] for x in range(NX)] for z in range(NZ)
]


def transpose_pairs(d, back=False):
    pairs = []
    for x in range(NX):
        for c in range(NC):
            for z in range(NZ):
                for y in range(NY):
                    p = 2 * x + c
                    home = device(x, c, z, y)
                    work = device(PLACE[p][z] // 2, PLACE[p][z] % 2, (p - 1) % NZ, (y + d) % NY)
                    pairs.append((work, home) if back else (home, work))
    return pairs


def ring(n, d):
    return [(i, (i + d) % n) for i in range(n)]


def head_at(y_ref, d):
    return pl.ds(pl.multiple_of(lax.rem(y_ref[0] + d, H) * DH, DH), DH)


def flip(block):
    return block.astype(jnp.float32).T.astype(jnp.bfloat16)


def pack_queries_kernel(y_ref, q_hbm, *refs):
    out_refs, (q_ref, sem) = refs[:NY], refs[NY:]
    copy = pltpu.make_async_copy(q_hbm, q_ref, sem)
    copy.start()
    copy.wait()
    for d, out_ref in enumerate(out_refs):
        out_ref[...] = flip(q_ref[:, head_at(y_ref, d)])


def pack_keys_kernel(y_ref, k_hbm, v_hbm, *refs):
    out_refs, (k_ref, v_ref, sems) = refs[:NY], refs[NY:]
    copies = [
        pltpu.make_async_copy(k_hbm, k_ref, sems.at[0]),
        pltpu.make_async_copy(v_hbm, v_ref, sems.at[1]),
    ]
    for copy in copies:
        copy.start()
    for copy in copies:
        copy.wait()
    for d, out_ref in enumerate(out_refs):
        out_ref[0] = k_ref[:, head_at(y_ref, d)]
        out_ref[1] = flip(v_ref[:, head_at(y_ref, d)])


def join_kernel(*refs):
    for n, ref in enumerate(refs[:-1]):
        refs[-1][n] = ref[...]


def join(parts):
    return pl.pallas_call(
        join_kernel,
        out_shape=jax.ShapeDtypeStruct((len(parts),) + parts[0].shape, parts[0].dtype),
        in_specs=[VMEM] * len(parts),
        out_specs=VMEM,
        compiler_params=SMALL,
    )(*parts)


def attend_kernel(
    need_ref, qblk_ref, kblk_ref, start_ref, *refs
):
    q_refs, refs = refs[:NX], refs[NX:]
    kv_refs, refs = refs[: 2 * PLANES], refs[2 * PLANES :]
    out_refs, (queries, kv, acc, top, total, pairs, sems) = refs[:NX], refs[NX:]
    copies = []
    for n, ref in enumerate(kv_refs):
        copy = pltpu.make_async_copy(ref, kv.at[pl.ds(n * NY, NY)], sems.at[n])
        copy.start()
        copies.append(copy)

    for n, ref in enumerate(q_refs):
        queries[n * NY : (n + 1) * NY] = ref[...]
    acc[...] = jnp.zeros_like(acc)
    top[...] = jnp.full_like(top, NEG)
    total[...] = jnp.zeros_like(total)

    def list_row(j, count):
        for s in range(NK):
            pairs[count] = j * 32 + s
            count = count + need_ref[j, s]
        return count

    count = lax.fori_loop(0, NQ, list_row, jnp.int32(0))
    for u in range(UNROLL):
        pairs[count + u] = NQ * 32
    for copy in copies:
        copy.wait()

    key_row = lax.broadcasted_iota(jnp.int32, (BLK, BLK), 0)
    lane = lax.broadcasted_iota(jnp.int32, (1, BLK), 1)

    def step(i, carry):
        done = []
        for u in range(UNROLL):
            pair = pairs[i * UNROLL + u]
            j = lax.shift_right_logical(pair, 5)
            s = pair & 31
            jq = jnp.minimum(j, NQ - 1)
            base = kblk_ref[s] * BLK
            low = start_ref[jq] - base
            high = qblk_ref[jq] * BLK + lane - base
            scores = jnp.dot(kv[s, 0], queries[jq], preferred_element_type=jnp.float32)
            allowed = (key_row >= low) & (key_row <= high)
            scores = jnp.where(allowed, scores * SCALE, NEG)
            peak = jnp.max(scores, axis=0, keepdims=True)
            weights = jnp.exp2(scores - peak)
            mass = jnp.sum(weights, axis=0, keepdims=True)
            part = jnp.dot(
                kv[s, 1], weights.astype(jnp.bfloat16), preferred_element_type=jnp.float32
            )
            done.append((j, peak, mass, part))
        for j, peak, mass, part in done:
            old = top[j]
            new = jnp.maximum(old, peak)
            keep = jnp.exp2(old - new)
            gain = jnp.exp2(peak - new)
            top[j] = new
            total[j] = total[j] * keep + mass * gain
            acc[j] = acc[j] * keep + part * gain
        return carry

    lax.fori_loop(0, (count + UNROLL - 1) // UNROLL, step, 0)

    row = lax.broadcasted_iota(jnp.int32, (STAT_ROWS, BLK), 0)

    for n, out_ref in enumerate(out_refs):

        def finish(d, carry, n=n, out_ref=out_ref):
            j = n * NY + d
            mass = total[j]
            some = mass > 0.0
            safe = jnp.where(some, mass, 1.0)
            out_ref[d, pl.ds(0, DH), :] = (acc[j] * (1.0 / safe)).astype(jnp.bfloat16)
            level = jnp.where(some, top[j] + jnp.log2(safe), NEG)
            first = level.astype(jnp.bfloat16).astype(jnp.float32)
            second = (level - first).astype(jnp.bfloat16).astype(jnp.float32)
            third = level - first - second
            stat = jnp.where(
                row == 0, first, jnp.where(row == 1, second, jnp.where(row == 2, third, 0.0))
            )
            out_ref[d, pl.ds(DH, STAT_ROWS), :] = stat.astype(jnp.bfloat16)
            return carry

        lax.fori_loop(0, NY, finish, 0)


def merge_kernel(*refs):
    part_refs, out_refs = refs[:NX], refs[NX:]
    for d, out_ref in enumerate(out_refs):
        levels = []
        for ref in part_refs:
            stat = ref[d, DH:, :].astype(jnp.float32)
            levels.append(stat[0:1] + stat[1:2] + stat[2:3])
        peak = functools.reduce(jnp.maximum, levels)
        shares = [jnp.exp2(level - peak) for level in levels]
        inverse = 1.0 / functools.reduce(jnp.add, shares)
        value = functools.reduce(
            jnp.add,
            [
                ref[d, :DH, :].astype(jnp.float32) * (share * inverse)
                for ref, share in zip(part_refs, shares)
            ],
        )
        out_ref[...] = value.T.astype(jnp.bfloat16)


def place_kernel(y_ref, *refs):
    for d, ref in enumerate(refs[:-1]):
        refs[-1][:, head_at(y_ref, d)] = ref[...]


VMEM = pl.BlockSpec(memory_space=pltpu.VMEM)
SMEM = pl.BlockSpec(memory_space=pltpu.SMEM)
ANY = pl.BlockSpec(memory_space=pl.ANY)
HBM = pl.BlockSpec(memory_space=pltpu.HBM)
SMALL = pltpu.CompilerParams(vmem_limit_bytes=4 << 20)


def on_device(queries, keys, values, block_pairs, doc_lengths):
    x, c, z, y = (lax.axis_index(name) for name in ("x", "c", "z", "y"))
    bf16 = jnp.bfloat16

    mine = y.reshape(1)
    block = jax.ShapeDtypeStruct((BLK, DH), bf16)
    heads = pl.pallas_call(
        pack_queries_kernel,
        out_shape=[block] * NY,
        in_specs=[SMEM, HBM],
        out_specs=[VMEM] * NY,
        scratch_shapes=[pltpu.VMEM((BLK, H * DH), bf16), pltpu.SemaphoreType.DMA],
        compiler_params=SMALL,
    )(mine, queries)
    asked = join([lax.ppermute(heads[d], AXES, transpose_pairs(d)) for d in range(NY)])
    asking = [asked] + [lax.ppermute(asked, "x", ring(NX, n)) for n in range(1, NX)]

    split = pl.pallas_call(
        pack_keys_kernel,
        out_shape=[jax.ShapeDtypeStruct((2, BLK, DH), bf16)] * NY,
        in_specs=[SMEM, HBM, HBM],
        out_specs=[VMEM] * NY,
        scratch_shapes=[pltpu.VMEM((BLK, H * DH), bf16)] * 2 + [pltpu.SemaphoreType.DMA((2,))],
        compiler_params=SMALL,
    )(mine, keys, values)
    here = join([split[0]] + [lax.ppermute(split[d], "y", ring(NY, d)) for d in range(1, NY)])
    near = [here, lax.ppermute(here, "z", ring(NZ, 1)), lax.ppermute(here, "z", ring(NZ, -1))]
    other = [lax.ppermute(b, "c", ring(NC, 1)) for b in near]

    slot = jnp.arange(NQ, dtype=jnp.int32)
    table = jnp.asarray(LIVES, jnp.int32)[z, :, c]
    column = lax.rem(x + NX - slot // NY, NX)
    lives = jnp.sum(
        jnp.where(column[:, None] == jnp.arange(NX)[None, :], table[None, :], 0), axis=1
    )
    query_block = PLANE * lax.rem(z + 1, NZ) + NY * lives + lax.rem(y + NY - slot % NY, NY)
    slot = jnp.arange(NK, dtype=jnp.int32)
    group = (slot // NY) % PLANES
    plane = lax.rem(z + jnp.where(group == 0, 0, jnp.where(group == 1, NZ - 1, 1)), NZ)
    row = lax.rem(y + NY - slot % NY, NY)
    core = jnp.where(slot < PLANES * NY, c, 1 - c)
    key_block = PLANE * plane + 8 * row + 2 * x + core
    ends = jnp.sum(
        jnp.where(
            jnp.arange(16)[:, None] <= jnp.arange(16)[None, :], doc_lengths[:, None], 0
        ),
        axis=0,
    )
    token = query_block[:, None] * BLK + jnp.arange(BLK, dtype=jnp.int32)[None, :]
    start = jnp.max(jnp.where(ends[:, None, None] <= token[None], ends[:, None, None], 0), axis=0)
    first = jnp.max(
        jnp.where(ends[:, None] <= query_block[None] * BLK, ends[:, None], 0), axis=0
    )
    hit_query = (block_pairs[:, 0][None, :] == query_block[:, None]).astype(bf16)
    hit_key = (block_pairs[:, 1][None, :] == key_block[:, None]).astype(bf16)
    listed = lax.dot_general(
        hit_query, hit_key, (((1,), (1,)), ((), ())), preferred_element_type=jnp.float32
    )
    need = (
        (listed > 0.5)
        & (key_block[None, :] * BLK + (BLK - 1) >= first[:, None])
        & (key_block[None, :] <= query_block[:, None])
    ).astype(jnp.int32)

    parts = pl.pallas_call(
        attend_kernel,
        out_shape=[jax.ShapeDtypeStruct((NY, ROWS, BLK), bf16)] * NX,
        in_specs=[SMEM, SMEM, SMEM] + [VMEM] * (1 + NX) + [ANY] * (2 * PLANES),
        out_specs=[VMEM] * NX,
        scratch_shapes=[
            pltpu.VMEM((NQ, DH, BLK), bf16),
            pltpu.VMEM((NK, 2, BLK, DH), bf16),
            pltpu.VMEM((NQ + 1, DH, BLK), jnp.float32),
            pltpu.VMEM((NQ + 1, 1, BLK), jnp.float32),
            pltpu.VMEM((NQ + 1, 1, BLK), jnp.float32),
            pltpu.SMEM((LIST,), jnp.int32),
            pltpu.SemaphoreType.DMA((2 * PLANES,)),
        ],
        compiler_params=pltpu.CompilerParams(vmem_limit_bytes=24 << 20),
    )(need, query_block, key_block, start.reshape(NQ, 1, BLK), *asking, *near, *other)

    back = [parts[0]] + [lax.ppermute(parts[n], "x", ring(NX, -n)) for n in range(1, NX)]
    merged = pl.pallas_call(
        merge_kernel,
        out_shape=[block] * NY,
        in_specs=[VMEM] * NX,
        out_specs=[VMEM] * NY,
        compiler_params=SMALL,
    )(*back)
    home = [lax.ppermute(merged[d], AXES, transpose_pairs(d, True)) for d in range(NY)]
    return pl.pallas_call(
        place_kernel,
        out_shape=jax.ShapeDtypeStruct((BLK, H * DH), bf16),
        in_specs=[SMEM] + [VMEM] * NY,
        out_specs=VMEM,
        compiler_params=SMALL,
    )(mine, *home)


def solution(mesh):
    fine = Mesh(mesh.devices.reshape(NX, NC, NZ, NY), ("x", "c", "z", "y"))
    return jax.shard_map(
        on_device,
        mesh=fine,
        in_specs=(
            P(("x", "c", "z", "y"), None),
            P(("z", "y", "x", "c"), None),
            P(("z", "y", "x", "c"), None),
            P(),
            P(),
        ),
        out_specs=P(("x", "c", "z", "y"), None),
        check_vma=False,
    )
```

```python
import functools
import math

import jax
import jax.numpy as jnp
from jax import lax
from jax.experimental import pallas as pl
from jax.experimental.pallas import tpu as pltpu
from jax.sharding import Mesh
from jax.sharding import PartitionSpec as P

H = 4
DH = 128
BLK = 128
NX, NC, NZ, NY = 4, 2, 8, 4
PLANE = 32
NQ = NX * NY
PLANES = 3
NK = PLANES * NY * NC
STAT_ROWS = 16
ROWS = DH + STAT_ROWS
UNROLL = 2
COUNT_AT = NQ * NK // 2 + UNROLL
QUERY_AT = COUNT_AT + 1
KEY_AT = QUERY_AT + NQ
PLAN = KEY_AT + NK + 1
NOWHERE = 1 << 20
NEG = -1e30
SCALE = math.log2(math.e) / math.sqrt(DH)


def device(x, c, z, y):
    return ((x * NC + c) * NZ + z) * NY + y


PLACE = [
    [7, 3, 4, 0, 5, 6, 2, 1],
    [3, 5, 1, 2, 6, 0, 7, 4],
    [1, 6, 2, 5, 0, 3, 4, 7],
    [2, 7, 4, 6, 0, 5, 3, 1],
    [6, 2, 0, 5, 3, 7, 4, 1],
    [5, 4, 2, 0, 6, 1, 7, 3],
    [1, 6, 0, 7, 2, 4, 3, 5],
    [1, 7, 5, 3, 0, 6, 4, 2],
]
LIVES = [
    [[PLACE[(z + 1) % NZ].index(2 * x + c) for c in range(NC)] for x in range(NX)] for z in range(NZ)
]


def transpose_pairs(back):
    pairs = []
    for x in range(NX):
        for c in range(NC):
            for z in range(NZ):
                for y in range(NY):
                    p = 2 * x + c
                    home = device(x, c, z, y)
                    work = device(PLACE[p][z] // 2, PLACE[p][z] % 2, (p - 1) % NZ, y)
                    pairs.append((work, home) if back else (home, work))
    return pairs


def ring(n, d):
    return [(i, (i + d) % n) for i in range(n)]


def pack_queries_kernel(q_ref, out_ref):
    for h in range(H):
        part = q_ref[:, h * DH : (h + 1) * DH].astype(jnp.float32).T.astype(jnp.bfloat16)
        for x in range(NX):
            out_ref[x * H + h] = part


def pack_keys_kernel(y_ref, k_ref, v_ref, *out_refs):
    for d, out_ref in enumerate(out_refs):
        at = pl.ds(pl.multiple_of(lax.rem(y_ref[0] + d, H) * DH, DH), DH)
        out_ref[0] = k_ref[:, at]
        out_ref[1] = v_ref[:, at].astype(jnp.float32).T.astype(jnp.bfloat16)


def join_kernel(*refs):
    at = 0
    for ref in refs[:-1]:
        refs[-1][at : at + ref.shape[0]] = ref[...]
        at += ref.shape[0]


def join(parts):
    count = sum(p.shape[0] for p in parts)
    return pl.pallas_call(
        join_kernel,
        out_shape=jax.ShapeDtypeStruct((count,) + parts[0].shape[1:], parts[0].dtype),
        in_specs=[VMEM] * len(parts),
        out_specs=VMEM,
        compiler_params=SMALL,
        cost_estimate=LIGHT,
    )(*parts)


def plan_kernel(need_ref, qblk_ref, kblk_ref, plan_ref):
    def list_row(j, count):
        plan_ref[QUERY_AT + j] = qblk_ref[j]
        held, has = jnp.int32(0), jnp.int32(0)
        for s in range(NK):
            want = need_ref[j, s]
            plan_ref[count] = j * 1024 + held * 32 + s
            count = count + want * has
            held = jnp.where(want > has, s, held)
            has = has ^ want
        plan_ref[count] = j * 1024 + held * 32 + NK
        return count + has

    count = lax.fori_loop(0, NQ, list_row, jnp.int32(0))
    for u in range(UNROLL):
        plan_ref[count + u] = NQ * 1024 + NK * 32 + NK
    plan_ref[COUNT_AT] = count
    for s in range(NK):
        plan_ref[KEY_AT + s] = kblk_ref[s]
    plan_ref[KEY_AT + NK] = NOWHERE


def attend_kernel(plan_ref, start_ref, q_ref, kv_ref, out_ref, acc, top, total):
    acc[...] = jnp.zeros_like(acc)
    top[...] = jnp.full_like(top, NEG)
    total[...] = jnp.zeros_like(total)
    key_row = lax.broadcasted_iota(jnp.int32, (BLK, BLK), 0)
    lane = lax.broadcasted_iota(jnp.int32, (1, BLK), 1)

    def step(i, carry):
        done = []
        for u in range(UNROLL):
            entry = plan_ref[i * UNROLL + u]
            j = lax.shift_right_logical(entry, 10)
            jq = jnp.minimum(j, NQ - 1)
            slots = (lax.shift_right_logical(entry, 5) & 31, entry & 31)
            held = [jnp.minimum(s, NK - 1) for s in slots]
            scores = jnp.dot(
                jnp.concatenate([kv_ref[s, 0] for s in held], axis=0),
                q_ref[jq],
                preferred_element_type=jnp.float32,
            )
            masked = []
            for n, s in enumerate(slots):
                base = plan_ref[KEY_AT + s] * BLK
                low = start_ref[jq] - base
                high = plan_ref[QUERY_AT + jq] * BLK + lane - base
                allowed = (key_row >= low) & (key_row <= high)
                part = scores[n * BLK : (n + 1) * BLK]
                masked.append(jnp.where(allowed, part * SCALE, NEG))
            scores = jnp.concatenate(masked, axis=0)
            peak = jnp.max(scores, axis=0, keepdims=True)
            weights = jnp.exp2(scores - peak)
            mass = jnp.sum(weights, axis=0, keepdims=True)
            part = jnp.dot(
                jnp.concatenate([kv_ref[s, 1] for s in held], axis=1),
                weights.astype(jnp.bfloat16),
                preferred_element_type=jnp.float32,
            )
            done.append((j, peak, mass, part))
        for j, peak, mass, part in done:
            old = top[j]
            new = jnp.maximum(old, peak)
            keep = jnp.exp2(old - new)
            gain = jnp.exp2(peak - new)
            top[j] = new
            total[j] = total[j] * keep + mass * gain
            acc[j] = acc[j] * keep + part * gain
        return carry

    lax.fori_loop(0, (plan_ref[COUNT_AT] + UNROLL - 1) // UNROLL, step, 0)

    row = lax.broadcasted_iota(jnp.int32, (STAT_ROWS, BLK), 0)

    def finish(j, carry):
        mass = total[j]
        some = mass > 0.0
        safe = jnp.where(some, mass, 1.0)
        out_ref[j, pl.ds(0, DH), :] = (acc[j] * (1.0 / safe)).astype(jnp.bfloat16)
        level = jnp.where(some, top[j] + jnp.log2(safe), NEG)
        first = level.astype(jnp.bfloat16).astype(jnp.float32)
        second = (level - first).astype(jnp.bfloat16).astype(jnp.float32)
        third = level - first - second
        stat = jnp.where(row == 0, first, jnp.where(row == 1, second, jnp.where(row == 2, third, 0.0)))
        out_ref[j, pl.ds(DH, STAT_ROWS), :] = stat.astype(jnp.bfloat16)
        return carry

    lax.fori_loop(0, NQ, finish, 0, unroll=4)


def combine_kernel(parts_ref, out_ref):
    for h in range(H):
        levels = []
        for r in range(NX):
            stat = parts_ref[r * H + h, DH:, :].astype(jnp.float32)
            levels.append(stat[0:1] + stat[1:2] + stat[2:3])
        peak = functools.reduce(jnp.maximum, levels)
        shares = [jnp.exp2(level - peak) for level in levels]
        inverse = 1.0 / functools.reduce(jnp.add, shares)
        value = functools.reduce(
            jnp.add,
            [
                parts_ref[r * H + h, :DH, :].astype(jnp.float32) * (shares[r] * inverse)
                for r in range(NX)
            ],
        )
        out_ref[:, h * DH : (h + 1) * DH] = value.T.astype(jnp.bfloat16)


VMEM = pl.BlockSpec(memory_space=pltpu.VMEM)
SMEM = pl.BlockSpec(memory_space=pltpu.SMEM)
LIGHT = pl.CostEstimate(flops=1024, bytes_accessed=1024, transcendentals=0)
SMALL = pltpu.CompilerParams(vmem_limit_bytes=8 << 20)


def on_device(queries, keys, values, block_pairs, doc_lengths):
    x, c, z, y = (lax.axis_index(name) for name in ("x", "c", "z", "y"))
    bf16 = jnp.bfloat16

    piece = jax.ShapeDtypeStruct((2, BLK, DH), bf16)
    split = pl.pallas_call(
        pack_keys_kernel,
        out_shape=[piece] * NY,
        in_specs=[SMEM, VMEM, VMEM],
        out_specs=[VMEM] * NY,
        compiler_params=SMALL,
        cost_estimate=LIGHT,
    )(y.reshape(1), keys, values)
    moved = lax.ppermute(queries, ("x", "c", "z", "y"), transpose_pairs(False))
    pieces = [split[0]] + [lax.ppermute(split[d], "y", ring(NY, d)) for d in range(1, NY)]

    spread = pl.pallas_call(
        pack_queries_kernel,
        out_shape=jax.ShapeDtypeStruct((NQ, DH, BLK), bf16),
        in_specs=[VMEM],
        out_specs=VMEM,
        compiler_params=SMALL,
        cost_estimate=LIGHT,
    )(moved)
    spread, *pieces = lax.optimization_barrier((spread, *pieces))
    mine = lax.all_to_all(spread, ("x", "y"), 0, 0, tiled=True)

    here = jnp.stack(pieces)
    near = [here, lax.ppermute(here, "z", ring(NZ, 1)), lax.ppermute(here, "z", ring(NZ, -1))]
    near[0], near[1], block_pairs, doc_lengths, x, c, z, y = lax.optimization_barrier(
        (near[0], near[1], block_pairs, doc_lengths, x, c, z, y)
    )
    other = [lax.ppermute(b, "c", ring(NC, 1)) for b in near]

    slot = jnp.arange(NQ, dtype=jnp.int32)
    lives = jnp.repeat(jnp.asarray(LIVES, jnp.int32)[z, :, c], NY)
    query_block = PLANE * lax.rem(z + 1, NZ) + NY * lives + slot % NY
    slot = jnp.arange(NK, dtype=jnp.int32)
    group = (slot // NY) % PLANES
    plane = lax.rem(z + jnp.where(group == 0, 0, jnp.where(group == 1, NZ - 1, 1)), NZ)
    row = lax.rem(y + NY - slot % NY, NY)
    core = jnp.where(slot < PLANES * NY, c, 1 - c)
    key_block = PLANE * plane + 8 * row + 2 * x + core
    ends = jnp.sum(
        jnp.where(
            jnp.arange(16)[:, None] <= jnp.arange(16)[None, :], doc_lengths[:, None], 0
        ),
        axis=0,
    )
    token = query_block[:, None] * BLK + jnp.arange(BLK, dtype=jnp.int32)[None, :]
    start = jnp.max(jnp.where(ends[:, None, None] <= token[None], ends[:, None, None], 0), axis=0)
    first = jnp.max(
        jnp.where(ends[:, None] <= query_block[None] * BLK, ends[:, None], 0), axis=0
    )
    hit_query = (block_pairs[:, 0][None, :] == query_block[:, None]).astype(bf16)
    hit_key = (block_pairs[:, 1][None, :] == key_block[:, None]).astype(bf16)
    listed = lax.dot_general(
        hit_query, hit_key, (((1,), (1,)), ((), ())), preferred_element_type=jnp.float32
    )
    need = (
        (listed > 0.5)
        & (key_block[None, :] * BLK + (BLK - 1) >= first[:, None])
        & (key_block[None, :] <= query_block[:, None])
    ).astype(jnp.int32)

    plan = pl.pallas_call(
        plan_kernel,
        out_shape=jax.ShapeDtypeStruct((PLAN,), jnp.int32),
        in_specs=[SMEM] * 3,
        out_specs=SMEM,
        compiler_params=SMALL,
        cost_estimate=LIGHT,
    )(need, query_block, key_block)
    parts = pl.pallas_call(
        attend_kernel,
        out_shape=jax.ShapeDtypeStruct((NQ, ROWS, BLK), bf16),
        in_specs=[SMEM, VMEM, VMEM, VMEM],
        out_specs=VMEM,
        scratch_shapes=[
            pltpu.VMEM((NQ + 1, DH, BLK), jnp.float32),
            pltpu.VMEM((NQ + 1, 1, BLK), jnp.float32),
            pltpu.VMEM((NQ + 1, 1, BLK), jnp.float32),
        ],
        compiler_params=pltpu.CompilerParams(vmem_limit_bytes=24 << 20),
    )(plan, start.reshape(NQ, 1, BLK), mine, join([*near, *other]))

    gathered = lax.all_to_all(parts, ("x", "y"), 0, 0, tiled=True)
    result = pl.pallas_call(
        combine_kernel,
        out_shape=jax.ShapeDtypeStruct((BLK, H * DH), bf16),
        in_specs=[VMEM],
        out_specs=VMEM,
        compiler_params=SMALL,
        cost_estimate=LIGHT,
    )(gathered)
    return lax.ppermute(result, ("x", "c", "z", "y"), transpose_pairs(True))


def solution(mesh):
    fine = Mesh(mesh.devices.reshape(NX, NC, NZ, NY), ("x", "c", "z", "y"))
    return jax.shard_map(
        on_device,
        mesh=fine,
        in_specs=(
            P(("x", "c", "z", "y"), None),
            P(("z", "y", "x", "c"), None),
            P(("z", "y", "x", "c"), None),
            P(),
            P(),
        ),
        out_specs=P(("x", "c", "z", "y"), None),
        check_vma=False,
    )
```

```python
import functools
import math

import jax
import jax.numpy as jnp
from jax import lax
from jax.experimental import pallas as pl
from jax.experimental.pallas import tpu as pltpu
from jax.sharding import Mesh
from jax.sharding import PartitionSpec as P

H = 4
DH = 128
BLK = 128
NX, NC, NZ, NY = 4, 2, 8, 4
PLANE = 32
NQ = NX * NY
PLANES = 3
NK = PLANES * NY * NC
STAT_ROWS = 16
ROWS = DH + STAT_ROWS
UNROLL = 8
COUNT_AT = NQ * NK // 2 + UNROLL
QUERY_AT = COUNT_AT + 1
KEY_AT = QUERY_AT + NQ
PLAN = KEY_AT + NK + 1
NOWHERE = 1 << 20
NEG = -1e30
SCALE = math.log2(math.e) / math.sqrt(DH)


def device(x, c, z, y):
    return ((x * NC + c) * NZ + z) * NY + y


PLACE = [
    [7, 3, 4, 0, 5, 6, 2, 1],
    [3, 5, 1, 2, 6, 0, 7, 4],
    [1, 6, 2, 5, 0, 3, 4, 7],
    [2, 7, 4, 6, 0, 5, 3, 1],
    [6, 2, 0, 5, 3, 7, 4, 1],
    [5, 4, 2, 0, 6, 1, 7, 3],
    [1, 6, 0, 7, 2, 4, 3, 5],
    [1, 7, 5, 3, 0, 6, 4, 2],
]
LIVES = [
    [
        sum(PLACE[(z + 1) % NZ].index(2 * x + c) << (3 * z) for z in range(NZ))
        for c in range(NC)
    ]
    for x in range(NX)
]


def transpose_pairs(back):
    pairs = []
    for x in range(NX):
        for c in range(NC):
            for z in range(NZ):
                for y in range(NY):
                    p = 2 * x + c
                    home = device(x, c, z, y)
                    work = device(PLACE[p][z] // 2, PLACE[p][z] % 2, (p - 1) % NZ, y)
                    pairs.append((work, home) if back else (home, work))
    return pairs


def ring(n, d):
    return [(i, (i + d) % n) for i in range(n)]


def pack_queries_kernel(q_ref, out_ref):
    for h in range(H):
        part = q_ref[:, h * DH : (h + 1) * DH].astype(jnp.float32).T.astype(jnp.bfloat16)
        for x in range(NX):
            out_ref[x * H + h] = part


def pack_keys_kernel(y_ref, k_ref, v_ref, *out_refs):
    for d, out_ref in enumerate(out_refs):
        at = pl.ds(pl.multiple_of(lax.rem(y_ref[0] + d, H) * DH, DH), DH)
        out_ref[0] = k_ref[:, at]
        out_ref[1] = v_ref[:, at].astype(jnp.float32).T.astype(jnp.bfloat16)


def join_kernel(*refs):
    at = 0
    for ref in refs[:-1]:
        refs[-1][at : at + ref.shape[0]] = ref[...]
        at += ref.shape[0]


def join(parts):
    count = sum(p.shape[0] for p in parts)
    return pl.pallas_call(
        join_kernel,
        out_shape=jax.ShapeDtypeStruct((count,) + parts[0].shape[1:], parts[0].dtype),
        in_specs=[VMEM] * len(parts),
        out_specs=VMEM,
        compiler_params=SMALL,
        cost_estimate=LIGHT,
    )(*parts)


def lowest_bit(mask):
    return 31 - lax.clz(mask & -mask)


def plan_kernel(need_ref, qblk_ref, kblk_ref, plan_ref):
    def list_row(j, count):
        plan_ref[QUERY_AT + j] = qblk_ref[j]

        def entry(carry):
            mask, count = carry
            rest = mask & (mask - 1)
            second = jnp.where(rest == 0, NK, lowest_bit(rest))
            plan_ref[count] = j * 1024 + lowest_bit(mask) * 32 + second
            return rest & (rest - 1), count + 1

        return lax.while_loop(lambda c: c[0] != 0, entry, (need_ref[j], count))[1]

    count = lax.fori_loop(0, NQ, list_row, jnp.int32(0))
    for u in range(UNROLL):
        plan_ref[count + u] = NQ * 1024 + NK * 32 + NK
    plan_ref[COUNT_AT] = count
    for s in range(NK):
        plan_ref[KEY_AT + s] = kblk_ref[s]
    plan_ref[KEY_AT + NK] = NOWHERE


def attend_kernel(plan_ref, start_ref, q_ref, kv_ref, out_ref, acc, top, total):
    acc[...] = jnp.zeros_like(acc)
    top[...] = jnp.full_like(top, NEG)
    total[...] = jnp.zeros_like(total)
    key_row = lax.broadcasted_iota(jnp.int32, (BLK, BLK), 0)
    lane = lax.broadcasted_iota(jnp.int32, (1, BLK), 1)

    def step(i, carry):
        done = []
        for u in range(UNROLL):
            entry = plan_ref[i * UNROLL + u]
            j = lax.shift_right_logical(entry, 10)
            jq = jnp.minimum(j, NQ - 1)
            slots = (lax.shift_right_logical(entry, 5) & 31, entry & 31)
            held = [jnp.minimum(s, NK - 1) for s in slots]
            scores = jnp.dot(
                jnp.concatenate([kv_ref[s, 0] for s in held], axis=0),
                q_ref[jq],
                preferred_element_type=jnp.float32,
            )
            masked = []
            for n, s in enumerate(slots):
                base = plan_ref[KEY_AT + s] * BLK
                low = start_ref[pl.ds(jq, 1), :] - base
                high = plan_ref[QUERY_AT + jq] * BLK + lane - base
                allowed = (key_row >= low) & (key_row <= high)
                part = scores[n * BLK : (n + 1) * BLK]
                masked.append(jnp.where(allowed, part * SCALE, NEG))
            scores = jnp.concatenate(masked, axis=0)
            peak = jnp.max(scores, axis=0, keepdims=True)
            weights = jnp.exp2(scores - peak)
            mass = jnp.sum(weights, axis=0, keepdims=True)
            part = jnp.dot(
                jnp.concatenate([kv_ref[s, 1] for s in held], axis=1),
                weights.astype(jnp.bfloat16),
                preferred_element_type=jnp.float32,
            )
            done.append((j, peak, mass, part))
        for j, peak, mass, part in done:
            at = pl.ds(j, 1)
            old = top[at, :]
            new = jnp.maximum(old, peak)
            keep = jnp.exp2(old - new)
            gain = jnp.exp2(peak - new)
            top[at, :] = new
            total[at, :] = total[at, :] * keep + mass * gain
            acc[j] = acc[j] * keep + part * gain
        return carry

    lax.fori_loop(0, (plan_ref[COUNT_AT] + UNROLL - 1) // UNROLL, step, 0)

    mass = total[:NQ, :]
    some = mass > 0.0
    safe = jnp.where(some, mass, 1.0)
    inverse = 1.0 / safe
    level = jnp.where(some, top[:NQ, :] + jnp.log2(safe), NEG)
    first = level.astype(jnp.bfloat16).astype(jnp.float32)
    second = (level - first).astype(jnp.bfloat16).astype(jnp.float32)
    third = level - first - second
    row = lax.broadcasted_iota(jnp.int32, (STAT_ROWS, BLK), 0)
    for j in range(NQ):
        one = slice(j, j + 1)
        out_ref[j, :DH, :] = (acc[j] * inverse[one]).astype(jnp.bfloat16)
        stat = jnp.where(
            row == 0, first[one], jnp.where(row == 1, second[one], third[one])
        )
        out_ref[j, DH:, :] = jnp.where(row < 3, stat, 0.0).astype(jnp.bfloat16)


def combine_kernel(parts_ref, out_ref):
    for h in range(H):
        levels = []
        for r in range(NX):
            stat = parts_ref[r * H + h, DH:, :].astype(jnp.float32)
            levels.append(stat[0:1] + stat[1:2] + stat[2:3])
        peak = functools.reduce(jnp.maximum, levels)
        shares = [jnp.exp2(level - peak) for level in levels]
        inverse = 1.0 / functools.reduce(jnp.add, shares)
        value = functools.reduce(
            jnp.add,
            [
                parts_ref[r * H + h, :DH, :].astype(jnp.float32) * (shares[r] * inverse)
                for r in range(NX)
            ],
        )
        out_ref[:, h * DH : (h + 1) * DH] = value.T.astype(jnp.bfloat16)


VMEM = pl.BlockSpec(memory_space=pltpu.VMEM)
SMEM = pl.BlockSpec(memory_space=pltpu.SMEM)
LIGHT = pl.CostEstimate(flops=1024, bytes_accessed=1024, transcendentals=0)
SMALL = pltpu.CompilerParams(vmem_limit_bytes=8 << 20)


def on_device(queries, keys, values, block_pairs, doc_lengths):
    x, c, z, y = (lax.axis_index(name) for name in ("x", "c", "z", "y"))
    bf16 = jnp.bfloat16

    piece = jax.ShapeDtypeStruct((2, BLK, DH), bf16)
    split = pl.pallas_call(
        pack_keys_kernel,
        out_shape=[piece] * NY,
        in_specs=[SMEM, VMEM, VMEM],
        out_specs=[VMEM] * NY,
        compiler_params=pltpu.CompilerParams(vmem_limit_bytes=63 << 20),
        cost_estimate=LIGHT,
    )(y.reshape(1), keys, values)
    moved = lax.ppermute(queries, ("x", "c", "z", "y"), transpose_pairs(False))
    pieces = [split[0]] + [lax.ppermute(split[d], "y", ring(NY, d)) for d in range(1, NY)]

    spread = pl.pallas_call(
        pack_queries_kernel,
        out_shape=jax.ShapeDtypeStruct((NQ, DH, BLK), bf16),
        in_specs=[VMEM],
        out_specs=VMEM,
        compiler_params=SMALL,
        cost_estimate=LIGHT,
    )(moved)
    spread, *pieces = lax.optimization_barrier((spread, *pieces))
    mine = lax.all_to_all(spread, ("x", "y"), 0, 0, tiled=True)

    here = jnp.stack(pieces)
    near = [here, lax.ppermute(here, "z", ring(NZ, 1)), lax.ppermute(here, "z", ring(NZ, -1))]
    near[0], near[1], block_pairs, doc_lengths, x, c, z, y = lax.optimization_barrier(
        (near[0], near[1], block_pairs, doc_lengths, x, c, z, y)
    )
    other = [lax.ppermute(b, "c", ring(NC, 1)) for b in near]

    slot = jnp.arange(NQ, dtype=jnp.int32)
    digits = [
        lax.shift_right_logical(jnp.where(c == 0, LIVES[n][0], LIVES[n][1]), 3 * z) & 7
        for n in range(NX)
    ]
    lives = functools.reduce(
        lambda rest, n: jnp.where(slot // NY == n, digits[n], rest), range(NX), slot
    )
    query_block = PLANE * lax.rem(z + 1, NZ) + NY * lives + slot % NY
    slot = jnp.arange(NK, dtype=jnp.int32)
    group = (slot // NY) % PLANES
    plane = lax.rem(z + jnp.where(group == 0, 0, jnp.where(group == 1, NZ - 1, 1)), NZ)
    row = lax.rem(y + NY - slot % NY, NY)
    core = jnp.where(slot < PLANES * NY, c, 1 - c)
    key_block = PLANE * plane + 8 * row + 2 * x + core
    ends = jnp.sum(
        jnp.where(
            jnp.arange(16)[:, None] <= jnp.arange(16)[None, :], doc_lengths[:, None], 0
        ),
        axis=0,
    )
    token = query_block[:, None] * BLK + jnp.arange(BLK, dtype=jnp.int32)[None, :]
    start = jnp.max(jnp.where(ends[:, None, None] <= token[None], ends[:, None, None], 0), axis=0)
    first = jnp.max(
        jnp.where(ends[:, None] <= query_block[None] * BLK, ends[:, None], 0), axis=0
    )
    hit_query = (block_pairs[:, 0][None, :] == query_block[:, None]).astype(bf16)
    hit_key = (block_pairs[:, 1][None, :] == key_block[:, None]).astype(bf16)
    listed = lax.dot_general(
        hit_query, hit_key, (((1,), (1,)), ((), ())), preferred_element_type=jnp.float32
    )
    need = (
        (listed > 0.5)
        & (key_block[None, :] * BLK + (BLK - 1) >= first[:, None])
        & (key_block[None, :] <= query_block[:, None])
    )
    bits = jnp.left_shift(jnp.int32(1), jnp.arange(NK, dtype=jnp.int32))
    need = jnp.sum(jnp.where(need, bits[None, :], 0), axis=1)

    plan = pl.pallas_call(
        plan_kernel,
        out_shape=jax.ShapeDtypeStruct((PLAN,), jnp.int32),
        in_specs=[SMEM] * 3,
        out_specs=SMEM,
        compiler_params=SMALL,
        cost_estimate=LIGHT,
    )(need, query_block, key_block)
    parts = pl.pallas_call(
        attend_kernel,
        out_shape=jax.ShapeDtypeStruct((NQ, ROWS, BLK), bf16),
        in_specs=[SMEM, VMEM, VMEM, VMEM],
        out_specs=VMEM,
        scratch_shapes=[
            pltpu.VMEM((NQ + 1, DH, BLK), jnp.float32),
            pltpu.VMEM((NQ + 8, BLK), jnp.float32),
            pltpu.VMEM((NQ + 8, BLK), jnp.float32),
        ],
        compiler_params=pltpu.CompilerParams(vmem_limit_bytes=24 << 20),
    )(plan, start, mine, join([*near, *other]))

    gathered = lax.all_to_all(parts, ("x", "y"), 0, 0, tiled=True)
    result = pl.pallas_call(
        combine_kernel,
        out_shape=jax.ShapeDtypeStruct((BLK, H * DH), bf16),
        in_specs=[VMEM],
        out_specs=VMEM,
        compiler_params=SMALL,
        cost_estimate=LIGHT,
    )(gathered)
    return lax.ppermute(result, ("x", "c", "z", "y"), transpose_pairs(True))


def solution(mesh):
    fine = Mesh(mesh.devices.reshape(NX, NC, NZ, NY), ("x", "c", "z", "y"))
    return jax.shard_map(
        on_device,
        mesh=fine,
        in_specs=(
            P(("x", "c", "z", "y"), None),
            P(("z", "y", "x", "c"), None),
            P(("z", "y", "x", "c"), None),
            P(),
            P(),
        ),
        out_specs=P(("x", "c", "z", "y"), None),
        check_vma=False,
    )
```

```python
import functools
import math

import jax
import jax.numpy as jnp
from jax import lax
from jax.experimental import pallas as pl
from jax.experimental.pallas import tpu as pltpu
from jax.sharding import Mesh
from jax.sharding import PartitionSpec as P

H = 4
DH = 128
BLK = 128
NX, NC, NZ, NY = 4, 2, 8, 4
PLANE = 32
NQ = NX * NY
PLANES = 3
NK = PLANES * NY * NC
STAT_ROWS = 16
ROWS = DH + STAT_ROWS
UNROLL = 8
COUNT_AT = NQ * NK // 2 + UNROLL
QUERY_AT = COUNT_AT + 1
KEY_AT = QUERY_AT + NQ
PLAN = KEY_AT + NK + 1
NOWHERE = 1 << 20
NEG = -1e30
SCALE = math.log2(math.e) / math.sqrt(DH)


def device(x, c, z, y):
    return ((x * NC + c) * NZ + z) * NY + y


PLACE = [
    [7, 3, 4, 0, 5, 6, 2, 1],
    [3, 5, 1, 2, 6, 0, 7, 4],
    [1, 6, 2, 5, 0, 3, 4, 7],
    [2, 7, 4, 6, 0, 5, 3, 1],
    [6, 2, 0, 5, 3, 7, 4, 1],
    [5, 4, 2, 0, 6, 1, 7, 3],
    [1, 6, 0, 7, 2, 4, 3, 5],
    [1, 7, 5, 3, 0, 6, 4, 2],
]
LIVES = [
    [
        sum(PLACE[(z + 1) % NZ].index(2 * x + c) << (3 * z) for z in range(NZ))
        for c in range(NC)
    ]
    for x in range(NX)
]


def transpose_pairs(back):
    pairs = []
    for x in range(NX):
        for c in range(NC):
            for z in range(NZ):
                for y in range(NY):
                    p = 2 * x + c
                    home = device(x, c, z, y)
                    work = device(PLACE[p][z] // 2, PLACE[p][z] % 2, (p - 1) % NZ, y)
                    pairs.append((work, home) if back else (home, work))
    return pairs


def ring(n, d):
    return [(i, (i + d) % n) for i in range(n)]


def pack_queries_kernel(q_ref, out_ref):
    for h in range(H):
        part = q_ref[:, h * DH : (h + 1) * DH].astype(jnp.float32).T.astype(jnp.bfloat16)
        for x in range(NX):
            out_ref[x * H + h] = part


def pack_keys_kernel(y_ref, k_ref, v_ref, *out_refs):
    for d, out_ref in enumerate(out_refs):
        at = pl.ds(pl.multiple_of(lax.rem(y_ref[0] + d, H) * DH, DH), DH)
        out_ref[0] = k_ref[:, at]
        out_ref[1] = v_ref[:, at].astype(jnp.float32).T.astype(jnp.bfloat16)


def join_kernel(*refs):
    at = 0
    for ref in refs[:-1]:
        refs[-1][at : at + ref.shape[0]] = ref[...]
        at += ref.shape[0]


def join(parts):
    count = sum(p.shape[0] for p in parts)
    return pl.pallas_call(
        join_kernel,
        out_shape=jax.ShapeDtypeStruct((count,) + parts[0].shape[1:], parts[0].dtype),
        in_specs=[VMEM] * len(parts),
        out_specs=VMEM,
        compiler_params=SMALL,
        cost_estimate=LIGHT,
    )(*parts)


def lowest_bit(mask):
    return 31 - lax.clz(mask & -mask)


def plan_kernel(need_ref, qblk_ref, kblk_ref, plan_ref):
    def list_row(j, count):
        plan_ref[QUERY_AT + j] = qblk_ref[j]

        def entry(carry):
            mask, count = carry
            rest = mask & (mask - 1)
            second = jnp.where(rest == 0, NK, lowest_bit(rest))
            plan_ref[count] = j * 1024 + lowest_bit(mask) * 32 + second
            return rest & (rest - 1), count + 1

        return lax.while_loop(lambda c: c[0] != 0, entry, (need_ref[j], count))[1]

    count = lax.fori_loop(0, NQ, list_row, jnp.int32(0))
    for u in range(UNROLL):
        plan_ref[count + u] = NQ * 1024 + NK * 32 + NK
    plan_ref[COUNT_AT] = count
    for s in range(NK):
        plan_ref[KEY_AT + s] = kblk_ref[s]
    plan_ref[KEY_AT + NK] = NOWHERE


def attend_kernel(plan_ref, start_ref, q_ref, kv_ref, out_ref, acc, top, total):
    acc[...] = jnp.zeros_like(acc)
    top[...] = jnp.full_like(top, NEG)
    total[...] = jnp.zeros_like(total)
    key_row = lax.broadcasted_iota(jnp.int32, (BLK, BLK), 0)
    lane = lax.broadcasted_iota(jnp.int32, (1, BLK), 1)

    def step(i, carry):
        done = []
        for u in range(UNROLL):
            entry = plan_ref[i * UNROLL + u]
            j = lax.shift_right_logical(entry, 10)
            jq = jnp.minimum(j, NQ - 1)
            slots = (lax.shift_right_logical(entry, 5) & 31, entry & 31)
            held = [jnp.minimum(s, NK - 1) for s in slots]
            scores = jnp.dot(
                jnp.concatenate([kv_ref[s, 0] for s in held], axis=0),
                q_ref[jq],
                preferred_element_type=jnp.float32,
            )
            masked = []
            for n, s in enumerate(slots):
                base = plan_ref[KEY_AT + s] * BLK
                low = start_ref[pl.ds(jq, 1), :] - base
                high = plan_ref[QUERY_AT + jq] * BLK + lane - base
                allowed = (key_row >= low) & (key_row <= high)
                part = scores[n * BLK : (n + 1) * BLK]
                masked.append(jnp.where(allowed, part * SCALE, NEG))
            scores = jnp.concatenate(masked, axis=0)
            peak = jnp.max(scores, axis=0, keepdims=True)
            weights = jnp.exp2(scores - peak)
            mass = jnp.sum(weights, axis=0, keepdims=True)
            part = jnp.dot(
                jnp.concatenate([kv_ref[s, 1] for s in held], axis=1),
                weights.astype(jnp.bfloat16),
                preferred_element_type=jnp.float32,
            )
            done.append((j, peak, mass, part))
        for j, peak, mass, part in done:
            at = pl.ds(j, 1)
            old = top[at, :]
            new = jnp.maximum(old, peak)
            keep = jnp.exp2(old - new)
            gain = jnp.exp2(peak - new)
            top[at, :] = new
            total[at, :] = total[at, :] * keep + mass * gain
            acc[j] = acc[j] * keep + part * gain
        return carry

    lax.fori_loop(0, (plan_ref[COUNT_AT] + UNROLL - 1) // UNROLL, step, 0)

    mass = total[:NQ, :]
    some = mass > 0.0
    safe = jnp.where(some, mass, 1.0)
    inverse = 1.0 / safe
    level = jnp.where(some, top[:NQ, :] + jnp.log2(safe), NEG)
    first = level.astype(jnp.bfloat16).astype(jnp.float32)
    second = (level - first).astype(jnp.bfloat16).astype(jnp.float32)
    third = level - first - second
    row = lax.broadcasted_iota(jnp.int32, (STAT_ROWS, BLK), 0)
    for j in range(NQ):
        one = slice(j, j + 1)
        out_ref[j, :DH, :] = (acc[j] * inverse[one]).astype(jnp.bfloat16)
        stat = jnp.where(
            row == 0, first[one], jnp.where(row == 1, second[one], third[one])
        )
        out_ref[j, DH:, :] = jnp.where(row < 3, stat, 0.0).astype(jnp.bfloat16)


def combine_kernel(parts_ref, out_ref):
    for h in range(H):
        levels = []
        for r in range(NX):
            stat = parts_ref[r * H + h, DH:, :].astype(jnp.float32)
            levels.append(stat[0:1] + stat[1:2] + stat[2:3])
        peak = functools.reduce(jnp.maximum, levels)
        shares = [jnp.exp2(level - peak) for level in levels]
        inverse = 1.0 / functools.reduce(jnp.add, shares)
        value = functools.reduce(
            jnp.add,
            [
                parts_ref[r * H + h, :DH, :].astype(jnp.float32) * (shares[r] * inverse)
                for r in range(NX)
            ],
        )
        out_ref[:, h * DH : (h + 1) * DH] = value.T.astype(jnp.bfloat16)


VMEM = pl.BlockSpec(memory_space=pltpu.VMEM)
SMEM = pl.BlockSpec(memory_space=pltpu.SMEM)
LIGHT = pl.CostEstimate(flops=1024, bytes_accessed=1024, transcendentals=0)
SMALL = pltpu.CompilerParams(vmem_limit_bytes=8 << 20)


def on_device(queries, keys, values, block_pairs, doc_lengths):
    x, c, z, y = (lax.axis_index(name) for name in ("x", "c", "z", "y"))
    bf16 = jnp.bfloat16

    piece = jax.ShapeDtypeStruct((2, BLK, DH), bf16)
    split = pl.pallas_call(
        pack_keys_kernel,
        out_shape=[piece] * NY,
        in_specs=[SMEM, VMEM, VMEM],
        out_specs=[VMEM] * NY,
        compiler_params=SMALL,
        cost_estimate=LIGHT,
    )(y.reshape(1), keys, values)
    moved = lax.ppermute(queries, ("x", "c", "z", "y"), transpose_pairs(False))
    pieces = [split[0]] + [lax.ppermute(split[d], "y", ring(NY, d)) for d in range(1, NY)]


    here = join([p[None] for p in pieces])
    moved, here = lax.optimization_barrier((moved, here))
    spread = pl.pallas_call(
        pack_queries_kernel,
        out_shape=jax.ShapeDtypeStruct((NQ, DH, BLK), bf16),
        in_specs=[VMEM],
        out_specs=VMEM,
        compiler_params=SMALL,
        cost_estimate=LIGHT,
    )(moved)
    mine = lax.all_to_all(spread, ("x", "y"), 0, 0, tiled=True)

    near = [here, lax.ppermute(here, "z", ring(NZ, 1)), lax.ppermute(here, "z", ring(NZ, -1))]
    near[0], near[1], block_pairs, doc_lengths, x, c, z, y = lax.optimization_barrier(
        (near[0], near[1], block_pairs, doc_lengths, x, c, z, y)
    )
    other = [lax.ppermute(b, "c", ring(NC, 1)) for b in near]

    slot = jnp.arange(NQ, dtype=jnp.int32)
    digits = [
        lax.shift_right_logical(jnp.where(c == 0, LIVES[n][0], LIVES[n][1]), 3 * z) & 7
        for n in range(NX)
    ]
    lives = functools.reduce(
        lambda rest, n: jnp.where(slot // NY == n, digits[n], rest), range(NX), slot
    )
    query_block = PLANE * lax.rem(z + 1, NZ) + NY * lives + slot % NY
    slot = jnp.arange(NK, dtype=jnp.int32)
    group = (slot // NY) % PLANES
    plane = lax.rem(z + jnp.where(group == 0, 0, jnp.where(group == 1, NZ - 1, 1)), NZ)
    row = lax.rem(y + NY - slot % NY, NY)
    core = jnp.where(slot < PLANES * NY, c, 1 - c)
    key_block = PLANE * plane + 8 * row + 2 * x + core
    ends = jnp.sum(
        jnp.where(
            jnp.arange(16)[:, None] <= jnp.arange(16)[None, :], doc_lengths[:, None], 0
        ),
        axis=0,
    )
    token = query_block[:, None] * BLK + jnp.arange(BLK, dtype=jnp.int32)[None, :]
    start = jnp.max(jnp.where(ends[:, None, None] <= token[None], ends[:, None, None], 0), axis=0)
    first = jnp.max(
        jnp.where(ends[:, None] <= query_block[None] * BLK, ends[:, None], 0), axis=0
    )
    hit_query = (block_pairs[:, 0][None, :] == query_block[:, None]).astype(bf16)
    hit_key = (block_pairs[:, 1][None, :] == key_block[:, None]).astype(bf16)
    listed = lax.dot_general(
        hit_query, hit_key, (((1,), (1,)), ((), ())), preferred_element_type=jnp.float32
    )
    need = (
        (listed > 0.5)
        & (key_block[None, :] * BLK + (BLK - 1) >= first[:, None])
        & (key_block[None, :] <= query_block[:, None])
    )
    bits = jnp.left_shift(jnp.int32(1), jnp.arange(NK, dtype=jnp.int32))
    need = jnp.sum(jnp.where(need, bits[None, :], 0), axis=1)

    plan = pl.pallas_call(
        plan_kernel,
        out_shape=jax.ShapeDtypeStruct((PLAN,), jnp.int32),
        in_specs=[SMEM] * 3,
        out_specs=SMEM,
        compiler_params=SMALL,
        cost_estimate=LIGHT,
    )(need, query_block, key_block)
    parts = pl.pallas_call(
        attend_kernel,
        out_shape=jax.ShapeDtypeStruct((NQ, ROWS, BLK), bf16),
        in_specs=[SMEM, VMEM, VMEM, VMEM],
        out_specs=VMEM,
        scratch_shapes=[
            pltpu.VMEM((NQ + 1, DH, BLK), jnp.float32),
            pltpu.VMEM((NQ + 8, BLK), jnp.float32),
            pltpu.VMEM((NQ + 8, BLK), jnp.float32),
        ],
        compiler_params=pltpu.CompilerParams(vmem_limit_bytes=24 << 20),
    )(plan, start, mine, join([*near, *other]))

    gathered = lax.all_to_all(parts, ("x", "y"), 0, 0, tiled=True)
    result = pl.pallas_call(
        combine_kernel,
        out_shape=jax.ShapeDtypeStruct((BLK, H * DH), bf16),
        in_specs=[VMEM],
        out_specs=VMEM,
        compiler_params=SMALL,
        cost_estimate=LIGHT,
    )(gathered)
    return lax.ppermute(result, ("x", "c", "z", "y"), transpose_pairs(True))


def solution(mesh):
    fine = Mesh(mesh.devices.reshape(NX, NC, NZ, NY), ("x", "c", "z", "y"))
    return jax.shard_map(
        on_device,
        mesh=fine,
        in_specs=(
            P(("x", "c", "z", "y"), None),
            P(("z", "y", "x", "c"), None),
            P(("z", "y", "x", "c"), None),
            P(),
            P(),
        ),
        out_specs=P(("x", "c", "z", "y"), None),
        check_vma=False,
    )
```

```python
import functools
import math

import jax
import jax.numpy as jnp
from jax import lax
from jax.experimental import pallas as pl
from jax.experimental.pallas import tpu as pltpu
from jax.sharding import Mesh
from jax.sharding import PartitionSpec as P

H = 4
DH = 128
BLK = 128
NX, NC, NZ, NY = 4, 2, 8, 4
PLANE = 32
NQ = NX * NY
PLANES = 3
NK = PLANES * NY * NC
STAT_ROWS = 16
ROWS = DH + STAT_ROWS
UNROLL = 8
COUNT_AT = NQ * NK // 2 + UNROLL
QUERY_AT = COUNT_AT + 1
KEY_AT = QUERY_AT + NQ
PLAN = KEY_AT + NK + 1
NOWHERE = 1 << 20
NEG = -1e30
SCALE = math.log2(math.e) / math.sqrt(DH)


def device(x, c, z, y):
    return ((x * NC + c) * NZ + z) * NY + y


PLACE = [
    [5, 3, 1, 0, 6, 2, 4, 7],
    [5, 4, 7, 3, 1, 0, 6, 2],
    [7, 5, 6, 1, 3, 2, 0, 4],
    [0, 6, 7, 4, 5, 1, 3, 2],
    [2, 7, 0, 1, 3, 6, 5, 4],
    [5, 3, 2, 7, 1, 0, 6, 4],
    [7, 6, 4, 5, 3, 2, 1, 0],
    [5, 1, 7, 6, 0, 3, 4, 2],
]
LIVES = [
    [
        sum(PLACE[(z + 1) % NZ].index(2 * x + c) << (3 * z) for z in range(NZ))
        for c in range(NC)
    ]
    for x in range(NX)
]


def transpose_pairs(back):
    pairs = []
    for x in range(NX):
        for c in range(NC):
            for z in range(NZ):
                for y in range(NY):
                    p = 2 * x + c
                    home = device(x, c, z, y)
                    work = device(PLACE[p][z] // 2, PLACE[p][z] % 2, (p - 1) % NZ, y)
                    pairs.append((work, home) if back else (home, work))
    return pairs


def ring(n, d):
    return [(i, (i + d) % n) for i in range(n)]


def pack_queries_kernel(q_ref, out_ref):
    for h in range(H):
        part = q_ref[:, h * DH : (h + 1) * DH].astype(jnp.float32).T.astype(jnp.bfloat16)
        for x in range(NX):
            out_ref[x * H + h] = part


def pack_keys_kernel(y_ref, k_ref, v_ref, *out_refs):
    for d, out_ref in enumerate(out_refs):
        at = pl.ds(pl.multiple_of(lax.rem(y_ref[0] + d, H) * DH, DH), DH)
        out_ref[0] = k_ref[:, at]
        out_ref[1] = v_ref[:, at].astype(jnp.float32).T.astype(jnp.bfloat16)


def join_kernel(*refs):
    at = 0
    for ref in refs[:-1]:
        refs[-1][at : at + ref.shape[0]] = ref[...]
        at += ref.shape[0]


def join(parts):
    count = sum(p.shape[0] for p in parts)
    return pl.pallas_call(
        join_kernel,
        out_shape=jax.ShapeDtypeStruct((count,) + parts[0].shape[1:], parts[0].dtype),
        in_specs=[VMEM] * len(parts),
        out_specs=VMEM,
        compiler_params=SMALL,
        cost_estimate=LIGHT,
    )(*parts)


def lowest_bit(mask):
    return 31 - lax.clz(mask & -mask)


def plan_kernel(need_ref, qblk_ref, kblk_ref, plan_ref):
    def list_row(j, count):
        plan_ref[QUERY_AT + j] = qblk_ref[j]

        def entry(carry):
            mask, count = carry
            rest = mask & (mask - 1)
            second = jnp.where(rest == 0, NK, lowest_bit(rest))
            plan_ref[count] = j * 1024 + lowest_bit(mask) * 32 + second
            return rest & (rest - 1), count + 1

        return lax.while_loop(lambda c: c[0] != 0, entry, (need_ref[j], count))[1]

    count = lax.fori_loop(0, NQ, list_row, jnp.int32(0))
    for u in range(UNROLL):
        plan_ref[count + u] = NQ * 1024 + NK * 32 + NK
    plan_ref[COUNT_AT] = count
    for s in range(NK):
        plan_ref[KEY_AT + s] = kblk_ref[s]
    plan_ref[KEY_AT + NK] = NOWHERE


def attend_kernel(plan_ref, start_ref, q_ref, kv_ref, out_ref, acc, top, total):
    acc[...] = jnp.zeros_like(acc)
    top[...] = jnp.full_like(top, NEG)
    total[...] = jnp.zeros_like(total)
    key_row = lax.broadcasted_iota(jnp.int32, (BLK, BLK), 0)
    lane = lax.broadcasted_iota(jnp.int32, (1, BLK), 1)

    def step(i, carry):
        done = []
        for u in range(UNROLL):
            entry = plan_ref[i * UNROLL + u]
            j = lax.shift_right_logical(entry, 10)
            jq = jnp.minimum(j, NQ - 1)
            slots = (lax.shift_right_logical(entry, 5) & 31, entry & 31)
            held = [jnp.minimum(s, NK - 1) for s in slots]
            scores = jnp.dot(
                jnp.concatenate([kv_ref[s, 0] for s in held], axis=0),
                q_ref[jq],
                preferred_element_type=jnp.float32,
            )
            masked = []
            for n, s in enumerate(slots):
                base = plan_ref[KEY_AT + s] * BLK
                low = start_ref[pl.ds(jq, 1), :] - base
                high = plan_ref[QUERY_AT + jq] * BLK + lane - base
                allowed = (key_row >= low) & (key_row <= high)
                part = scores[n * BLK : (n + 1) * BLK]
                masked.append(jnp.where(allowed, part * SCALE, NEG))
            scores = jnp.concatenate(masked, axis=0)
            peak = jnp.max(scores, axis=0, keepdims=True)
            weights = jnp.exp2(scores - peak)
            mass = jnp.sum(weights, axis=0, keepdims=True)
            part = jnp.dot(
                jnp.concatenate([kv_ref[s, 1] for s in held], axis=1),
                weights.astype(jnp.bfloat16),
                preferred_element_type=jnp.float32,
            )
            done.append((j, peak, mass, part))
        for j, peak, mass, part in done:
            at = pl.ds(j, 1)
            old = top[at, :]
            new = jnp.maximum(old, peak)
            keep = jnp.exp2(old - new)
            gain = jnp.exp2(peak - new)
            top[at, :] = new
            total[at, :] = total[at, :] * keep + mass * gain
            acc[j] = acc[j] * keep + part * gain
        return carry

    lax.fori_loop(0, (plan_ref[COUNT_AT] + UNROLL - 1) // UNROLL, step, 0)

    mass = total[:NQ, :]
    some = mass > 0.0
    safe = jnp.where(some, mass, 1.0)
    inverse = 1.0 / safe
    level = jnp.where(some, top[:NQ, :] + jnp.log2(safe), NEG)
    first = level.astype(jnp.bfloat16).astype(jnp.float32)
    second = (level - first).astype(jnp.bfloat16).astype(jnp.float32)
    third = level - first - second
    row = lax.broadcasted_iota(jnp.int32, (STAT_ROWS, BLK), 0)
    for j in range(NQ):
        one = slice(j, j + 1)
        out_ref[j, :DH, :] = (acc[j] * inverse[one]).astype(jnp.bfloat16)
        stat = jnp.where(
            row == 0, first[one], jnp.where(row == 1, second[one], third[one])
        )
        out_ref[j, DH:, :] = jnp.where(row < 3, stat, 0.0).astype(jnp.bfloat16)


def combine_kernel(parts_ref, out_ref):
    for h in range(H):
        levels = []
        for r in range(NX):
            stat = parts_ref[r * H + h, DH:, :].astype(jnp.float32)
            levels.append(stat[0:1] + stat[1:2] + stat[2:3])
        peak = functools.reduce(jnp.maximum, levels)
        shares = [jnp.exp2(level - peak) for level in levels]
        inverse = 1.0 / functools.reduce(jnp.add, shares)
        value = functools.reduce(
            jnp.add,
            [
                parts_ref[r * H + h, :DH, :].astype(jnp.float32) * (shares[r] * inverse)
                for r in range(NX)
            ],
        )
        out_ref[:, h * DH : (h + 1) * DH] = value.T.astype(jnp.bfloat16)


VMEM = pl.BlockSpec(memory_space=pltpu.VMEM)
SMEM = pl.BlockSpec(memory_space=pltpu.SMEM)
LIGHT = pl.CostEstimate(flops=1024, bytes_accessed=1024, transcendentals=0)
SMALL = pltpu.CompilerParams(vmem_limit_bytes=8 << 20)


def on_device(queries, keys, values, block_pairs, doc_lengths):
    x, c, z, y = (lax.axis_index(name) for name in ("x", "c", "z", "y"))
    bf16 = jnp.bfloat16

    piece = jax.ShapeDtypeStruct((2, BLK, DH), bf16)
    split = pl.pallas_call(
        pack_keys_kernel,
        out_shape=[piece] * NY,
        in_specs=[SMEM, VMEM, VMEM],
        out_specs=[VMEM] * NY,
        compiler_params=SMALL,
        cost_estimate=LIGHT,
    )(y.reshape(1), keys, values)
    moved = lax.ppermute(queries, ("x", "c", "z", "y"), transpose_pairs(False))
    pieces = [split[0]] + [lax.ppermute(split[d], "y", ring(NY, d)) for d in range(1, NY)]
    here = join([p[None] for p in pieces])
    moved, here = lax.optimization_barrier((moved, here))

    spread = pl.pallas_call(
        pack_queries_kernel,
        out_shape=jax.ShapeDtypeStruct((NQ, DH, BLK), bf16),
        in_specs=[VMEM],
        out_specs=VMEM,
        compiler_params=SMALL,
        cost_estimate=LIGHT,
    )(moved)
    mine = lax.all_to_all(spread, ("x", "y"), 0, 0, tiled=True)
    near = [here, lax.ppermute(here, "z", ring(NZ, 1)), lax.ppermute(here, "z", ring(NZ, -1))]
    near[0], near[1], block_pairs, doc_lengths, x, c, z, y = lax.optimization_barrier(
        (near[0], near[1], block_pairs, doc_lengths, x, c, z, y)
    )
    other = [lax.ppermute(b, "c", ring(NC, 1)) for b in near]

    slot = jnp.arange(NQ, dtype=jnp.int32)
    digits = [
        lax.shift_right_logical(jnp.where(c == 0, LIVES[n][0], LIVES[n][1]), 3 * z) & 7
        for n in range(NX)
    ]
    lives = functools.reduce(
        lambda rest, n: jnp.where(slot // NY == n, digits[n], rest), range(NX), slot
    )
    query_block = PLANE * lax.rem(z + 1, NZ) + NY * lives + slot % NY
    slot = jnp.arange(NK, dtype=jnp.int32)
    group = (slot // NY) % PLANES
    plane = lax.rem(z + jnp.where(group == 0, 0, jnp.where(group == 1, NZ - 1, 1)), NZ)
    row = lax.rem(y + NY - slot % NY, NY)
    core = jnp.where(slot < PLANES * NY, c, 1 - c)
    key_block = PLANE * plane + 8 * row + 2 * x + core
    ends = jnp.sum(
        jnp.where(
            jnp.arange(16)[:, None] <= jnp.arange(16)[None, :], doc_lengths[:, None], 0
        ),
        axis=0,
    )
    token = query_block[:, None] * BLK + jnp.arange(BLK, dtype=jnp.int32)[None, :]
    start = jnp.max(jnp.where(ends[:, None, None] <= token[None], ends[:, None, None], 0), axis=0)
    first = jnp.max(
        jnp.where(ends[:, None] <= query_block[None] * BLK, ends[:, None], 0), axis=0
    )
    hit_query = (block_pairs[:, 0][None, :] == query_block[:, None]).astype(bf16)
    hit_key = (block_pairs[:, 1][None, :] == key_block[:, None]).astype(bf16)
    listed = lax.dot_general(
        hit_query, hit_key, (((1,), (1,)), ((), ())), preferred_element_type=jnp.float32
    )
    need = (
        (listed > 0.5)
        & (key_block[None, :] * BLK + (BLK - 1) >= first[:, None])
        & (key_block[None, :] <= query_block[:, None])
    )
    bits = jnp.left_shift(jnp.int32(1), jnp.arange(NK, dtype=jnp.int32))
    need = jnp.sum(jnp.where(need, bits[None, :], 0), axis=1)

    plan = pl.pallas_call(
        plan_kernel,
        out_shape=jax.ShapeDtypeStruct((PLAN,), jnp.int32),
        in_specs=[SMEM] * 3,
        out_specs=SMEM,
        compiler_params=SMALL,
        cost_estimate=LIGHT,
    )(need, query_block, key_block)
    parts = pl.pallas_call(
        attend_kernel,
        out_shape=jax.ShapeDtypeStruct((NQ, ROWS, BLK), bf16),
        in_specs=[SMEM, VMEM, VMEM, VMEM],
        out_specs=VMEM,
        scratch_shapes=[
            pltpu.VMEM((NQ + 1, DH, BLK), jnp.float32),
            pltpu.VMEM((NQ + 8, BLK), jnp.float32),
            pltpu.VMEM((NQ + 8, BLK), jnp.float32),
        ],
        compiler_params=pltpu.CompilerParams(vmem_limit_bytes=24 << 20),
    )(plan, start, mine, join([*near, *other]))

    gathered = lax.all_to_all(parts, ("x", "y"), 0, 0, tiled=True)
    result = pl.pallas_call(
        combine_kernel,
        out_shape=jax.ShapeDtypeStruct((BLK, H * DH), bf16),
        in_specs=[VMEM],
        out_specs=VMEM,
        compiler_params=SMALL,
        cost_estimate=LIGHT,
    )(gathered)
    return lax.ppermute(result, ("x", "c", "z", "y"), transpose_pairs(True))


def solution(mesh):
    fine = Mesh(mesh.devices.reshape(NX, NC, NZ, NY), ("x", "c", "z", "y"))
    return jax.shard_map(
        on_device,
        mesh=fine,
        in_specs=(
            P(("x", "c", "z", "y"), None),
            P(("z", "y", "x", "c"), None),
            P(("z", "y", "x", "c"), None),
            P(),
            P(),
        ),
        out_specs=P(("x", "c", "z", "y"), None),
        check_vma=False,
    )
```

```python
import functools
import math

import jax
import jax.numpy as jnp
from jax import lax
from jax.experimental import pallas as pl
from jax.experimental.pallas import tpu as pltpu
from jax.sharding import Mesh
from jax.sharding import PartitionSpec as P

H = 4
DH = 128
BLK = 128
NX, NC, NZ, NY = 4, 2, 8, 4
PLANE = 32
NQ = NX * NY
PLANES = 3
NK = PLANES * NY * NC
STAT_ROWS = 16
ROWS = DH + STAT_ROWS
UNROLL = 16
COUNT_AT = NQ * NK // 2 + UNROLL
QUERY_AT = COUNT_AT + 1
KEY_AT = QUERY_AT + NQ
PLAN = KEY_AT + NK + 1
NOWHERE = 1 << 20
NEG = -1e30
SCALE = math.log2(math.e) / math.sqrt(DH)


def device(x, c, z, y):
    return ((x * NC + c) * NZ + z) * NY + y


PLACE = [
    [5, 3, 1, 0, 6, 2, 4, 7],
    [5, 4, 7, 3, 1, 0, 6, 2],
    [7, 5, 6, 1, 3, 2, 0, 4],
    [0, 6, 7, 4, 5, 1, 3, 2],
    [2, 7, 0, 1, 3, 6, 5, 4],
    [5, 3, 2, 7, 1, 0, 6, 4],
    [7, 6, 4, 5, 3, 2, 1, 0],
    [5, 1, 7, 6, 0, 3, 4, 2],
]
LIVES = [
    [
        sum(PLACE[(z + 1) % NZ].index(2 * x + c) << (3 * z) for z in range(NZ))
        for c in range(NC)
    ]
    for x in range(NX)
]


def transpose_pairs(back):
    pairs = []
    for x in range(NX):
        for c in range(NC):
            for z in range(NZ):
                for y in range(NY):
                    p = 2 * x + c
                    home = device(x, c, z, y)
                    work = device(PLACE[p][z] // 2, PLACE[p][z] % 2, (p - 1) % NZ, y)
                    pairs.append((work, home) if back else (home, work))
    return pairs


def ring(n, d):
    return [(i, (i + d) % n) for i in range(n)]


def pack_queries_kernel(q_ref, out_ref):
    for h in range(H):
        part = q_ref[:, h * DH : (h + 1) * DH].astype(jnp.float32).T.astype(jnp.bfloat16)
        for x in range(NX):
            out_ref[x * H + h] = part


def pack_keys_kernel(y_ref, k_hbm, v_hbm, *refs):
    out_refs, (k_ref, v_ref, sems) = refs[:NY], refs[NY:]
    copies = [
        pltpu.make_async_copy(v_hbm, v_ref, sems.at[0]),
        pltpu.make_async_copy(k_hbm, k_ref, sems.at[1]),
    ]
    for copy in copies:
        copy.start()
    for copy in copies:
        copy.wait()
    for d, out_ref in enumerate(out_refs):
        at = pl.ds(pl.multiple_of(lax.rem(y_ref[0] + d, H) * DH, DH), DH)
        out_ref[0] = k_ref[:, at]
        out_ref[1] = v_ref[:, at].astype(jnp.float32).T.astype(jnp.bfloat16)


def join_kernel(*refs):
    at = 0
    for ref in refs[:-1]:
        refs[-1][at : at + ref.shape[0]] = ref[...]
        at += ref.shape[0]


def join(parts):
    count = sum(p.shape[0] for p in parts)
    return pl.pallas_call(
        join_kernel,
        out_shape=jax.ShapeDtypeStruct((count,) + parts[0].shape[1:], parts[0].dtype),
        in_specs=[VMEM] * len(parts),
        out_specs=VMEM,
        compiler_params=SMALL,
        cost_estimate=LIGHT,
    )(*parts)


def lowest_bit(mask):
    return 31 - lax.clz(mask & -mask)


def plan_kernel(need_ref, qblk_ref, kblk_ref, plan_ref):
    def list_row(j, count):
        plan_ref[QUERY_AT + j] = qblk_ref[j]

        def entry(carry):
            mask, count = carry
            rest = mask & (mask - 1)
            second = jnp.where(rest == 0, NK, lowest_bit(rest))
            plan_ref[count] = j * 1024 + lowest_bit(mask) * 32 + second
            return rest & (rest - 1), count + 1

        return lax.while_loop(lambda c: c[0] != 0, entry, (need_ref[j], count))[1]

    count = lax.fori_loop(0, NQ, list_row, jnp.int32(0))
    for u in range(UNROLL):
        plan_ref[count + u] = NQ * 1024 + NK * 32 + NK
    plan_ref[COUNT_AT] = count
    for s in range(NK):
        plan_ref[KEY_AT + s] = kblk_ref[s]
    plan_ref[KEY_AT + NK] = NOWHERE


def attend_kernel(plan_ref, start_ref, q_ref, kv_ref, out_ref, acc, top, total):
    acc[...] = jnp.zeros_like(acc)
    top[...] = jnp.full_like(top, NEG)
    total[...] = jnp.zeros_like(total)
    key_row = lax.broadcasted_iota(jnp.int32, (BLK, BLK), 0)
    lane = lax.broadcasted_iota(jnp.int32, (1, BLK), 1)

    def step(i, carry):
        done = []
        for u in range(UNROLL):
            entry = plan_ref[i * UNROLL + u]
            j = lax.shift_right_logical(entry, 10)
            jq = jnp.minimum(j, NQ - 1)
            slots = (lax.shift_right_logical(entry, 5) & 31, entry & 31)
            held = [jnp.minimum(s, NK - 1) for s in slots]
            scores = jnp.dot(
                jnp.concatenate([kv_ref[s, 0] for s in held], axis=0),
                q_ref[jq],
                preferred_element_type=jnp.float32,
            )
            masked = []
            for n, s in enumerate(slots):
                base = plan_ref[KEY_AT + s] * BLK
                low = start_ref[pl.ds(jq, 1), :] - base
                high = plan_ref[QUERY_AT + jq] * BLK + lane - base
                allowed = (key_row >= low) & (key_row <= high)
                part = scores[n * BLK : (n + 1) * BLK]
                masked.append(jnp.where(allowed, part * SCALE, NEG))
            scores = jnp.concatenate(masked, axis=0)
            peak = jnp.max(scores, axis=0, keepdims=True)
            weights = jnp.exp2(scores - peak)
            mass = jnp.sum(weights, axis=0, keepdims=True)
            part = jnp.dot(
                jnp.concatenate([kv_ref[s, 1] for s in held], axis=1),
                weights.astype(jnp.bfloat16),
                preferred_element_type=jnp.float32,
            )
            done.append((j, peak, mass, part))
        for j, peak, mass, part in done:
            at = pl.ds(j, 1)
            old = top[at, :]
            new = jnp.maximum(old, peak)
            keep = jnp.exp2(old - new)
            gain = jnp.exp2(peak - new)
            top[at, :] = new
            total[at, :] = total[at, :] * keep + mass * gain
            acc[j] = acc[j] * keep + part * gain
        return carry

    lax.fori_loop(0, (plan_ref[COUNT_AT] + UNROLL - 1) // UNROLL, step, 0)

    mass = total[:NQ, :]
    some = mass > 0.0
    safe = jnp.where(some, mass, 1.0)
    inverse = 1.0 / safe
    level = jnp.where(some, top[:NQ, :] + jnp.log2(safe), NEG)
    first = level.astype(jnp.bfloat16).astype(jnp.float32)
    second = (level - first).astype(jnp.bfloat16).astype(jnp.float32)
    third = level - first - second
    row = lax.broadcasted_iota(jnp.int32, (STAT_ROWS, BLK), 0)
    for j in range(NQ):
        one = slice(j, j + 1)
        out_ref[j, :DH, :] = (acc[j] * inverse[one]).astype(jnp.bfloat16)
        stat = jnp.where(
            row == 0, first[one], jnp.where(row == 1, second[one], third[one])
        )
        out_ref[j, DH:, :] = jnp.where(row < 3, stat, 0.0).astype(jnp.bfloat16)


def combine_kernel(parts_ref, out_ref):
    for h in range(H):
        levels = []
        for r in range(NX):
            stat = parts_ref[r * H + h, DH:, :].astype(jnp.float32)
            levels.append(stat[0:1] + stat[1:2] + stat[2:3])
        peak = functools.reduce(jnp.maximum, levels)
        shares = [jnp.exp2(level - peak) for level in levels]
        inverse = 1.0 / functools.reduce(jnp.add, shares)
        value = functools.reduce(
            jnp.add,
            [
                parts_ref[r * H + h, :DH, :].astype(jnp.float32) * (shares[r] * inverse)
                for r in range(NX)
            ],
        )
        out_ref[:, h * DH : (h + 1) * DH] = value.T.astype(jnp.bfloat16)


VMEM = pl.BlockSpec(memory_space=pltpu.VMEM)
SMEM = pl.BlockSpec(memory_space=pltpu.SMEM)
LIGHT = pl.CostEstimate(flops=1024, bytes_accessed=1024, transcendentals=0)
HBM = pl.BlockSpec(memory_space=pltpu.HBM)
SMALL = pltpu.CompilerParams(vmem_limit_bytes=8 << 20)


def on_device(queries, keys, values, block_pairs, doc_lengths):
    x, c, z, y = (lax.axis_index(name) for name in ("x", "c", "z", "y"))
    bf16 = jnp.bfloat16

    piece = jax.ShapeDtypeStruct((2, BLK, DH), bf16)
    split = pl.pallas_call(
        pack_keys_kernel,
        out_shape=[piece] * NY,
        in_specs=[SMEM, HBM, HBM],
        out_specs=[VMEM] * NY,
        scratch_shapes=[pltpu.VMEM((BLK, H * DH), bf16)] * 2 + [pltpu.SemaphoreType.DMA((2,))],
        compiler_params=SMALL,
        cost_estimate=LIGHT,
    )(
        y.reshape(1),
        pltpu.with_memory_space_constraint(keys, pltpu.HBM),
        pltpu.with_memory_space_constraint(values, pltpu.HBM),
    )
    moved = lax.ppermute(queries, ("x", "c", "z", "y"), transpose_pairs(False))
    pieces = [split[0]] + [lax.ppermute(split[d], "y", ring(NY, d)) for d in range(1, NY)]
    here = join([p[None] for p in pieces])
    moved, here = lax.optimization_barrier((moved, here))

    spread = pl.pallas_call(
        pack_queries_kernel,
        out_shape=jax.ShapeDtypeStruct((NQ, DH, BLK), bf16),
        in_specs=[VMEM],
        out_specs=VMEM,
        compiler_params=SMALL,
        cost_estimate=LIGHT,
    )(moved)
    mine = lax.all_to_all(spread, ("x", "y"), 0, 0, tiled=True)
    near = [here, lax.ppermute(here, "z", ring(NZ, 1)), lax.ppermute(here, "z", ring(NZ, -1))]
    near[0], near[1], block_pairs, doc_lengths, x, c, z, y = lax.optimization_barrier(
        (near[0], near[1], block_pairs, doc_lengths, x, c, z, y)
    )
    other = [lax.ppermute(b, "c", ring(NC, 1)) for b in near]

    slot = jnp.arange(NQ, dtype=jnp.int32)
    digits = [
        lax.shift_right_logical(jnp.where(c == 0, LIVES[n][0], LIVES[n][1]), 3 * z) & 7
        for n in range(NX)
    ]
    lives = functools.reduce(
        lambda rest, n: jnp.where(slot // NY == n, digits[n], rest), range(NX), slot
    )
    query_block = PLANE * lax.rem(z + 1, NZ) + NY * lives + slot % NY
    slot = jnp.arange(NK, dtype=jnp.int32)
    group = (slot // NY) % PLANES
    plane = lax.rem(z + jnp.where(group == 0, 0, jnp.where(group == 1, NZ - 1, 1)), NZ)
    row = lax.rem(y + NY - slot % NY, NY)
    core = jnp.where(slot < PLANES * NY, c, 1 - c)
    key_block = PLANE * plane + 8 * row + 2 * x + core
    ends = jnp.sum(
        jnp.where(
            jnp.arange(16)[:, None] <= jnp.arange(16)[None, :], doc_lengths[:, None], 0
        ),
        axis=0,
    )
    token = query_block[:, None] * BLK + jnp.arange(BLK, dtype=jnp.int32)[None, :]
    start = jnp.max(jnp.where(ends[:, None, None] <= token[None], ends[:, None, None], 0), axis=0)
    first = jnp.max(
        jnp.where(ends[:, None] <= query_block[None] * BLK, ends[:, None], 0), axis=0
    )
    hit_query = (block_pairs[:, 0][None, :] == query_block[:, None]).astype(bf16)
    hit_key = (block_pairs[:, 1][None, :] == key_block[:, None]).astype(bf16)
    listed = lax.dot_general(
        hit_query, hit_key, (((1,), (1,)), ((), ())), preferred_element_type=jnp.float32
    )
    need = (
        (listed > 0.5)
        & (key_block[None, :] * BLK + (BLK - 1) >= first[:, None])
        & (key_block[None, :] <= query_block[:, None])
    )
    bits = jnp.left_shift(jnp.int32(1), jnp.arange(NK, dtype=jnp.int32))
    need = jnp.sum(jnp.where(need, bits[None, :], 0), axis=1)

    plan = pl.pallas_call(
        plan_kernel,
        out_shape=jax.ShapeDtypeStruct((PLAN,), jnp.int32),
        in_specs=[SMEM] * 3,
        out_specs=SMEM,
        compiler_params=SMALL,
        cost_estimate=LIGHT,
    )(need, query_block, key_block)
    parts = pl.pallas_call(
        attend_kernel,
        out_shape=jax.ShapeDtypeStruct((NQ, ROWS, BLK), bf16),
        in_specs=[SMEM, VMEM, VMEM, VMEM],
        out_specs=VMEM,
        scratch_shapes=[
            pltpu.VMEM((NQ + 1, DH, BLK), jnp.float32),
            pltpu.VMEM((NQ + 8, BLK), jnp.float32),
            pltpu.VMEM((NQ + 8, BLK), jnp.float32),
        ],
        compiler_params=pltpu.CompilerParams(vmem_limit_bytes=24 << 20),
    )(plan, start, mine, join([*near, *other]))

    gathered = lax.all_to_all(parts, ("x", "y"), 0, 0, tiled=True)
    result = pl.pallas_call(
        combine_kernel,
        out_shape=jax.ShapeDtypeStruct((BLK, H * DH), bf16),
        in_specs=[VMEM],
        out_specs=VMEM,
        compiler_params=SMALL,
        cost_estimate=LIGHT,
    )(gathered)
    return lax.ppermute(result, ("x", "c", "z", "y"), transpose_pairs(True))


def solution(mesh):
    fine = Mesh(mesh.devices.reshape(NX, NC, NZ, NY), ("x", "c", "z", "y"))
    return jax.shard_map(
        on_device,
        mesh=fine,
        in_specs=(
            P(("x", "c", "z", "y"), None),
            P(("z", "y", "x", "c"), None),
            P(("z", "y", "x", "c"), None),
            P(),
            P(),
        ),
        out_specs=P(("x", "c", "z", "y"), None),
        check_vma=False,
    )
```

```python
import functools
import math

import jax
import jax.numpy as jnp
from jax import lax
from jax.experimental import pallas as pl
from jax.experimental.pallas import tpu as pltpu
from jax.sharding import Mesh
from jax.sharding import PartitionSpec as P

H = 4
DH = 128
BLK = 128
NX, NC, NZ, NY = 4, 2, 8, 4
PLANE = 32
NQ = NX * NY
PLANES = 3
NK = PLANES * NY * NC
STAT_ROWS = 16
ROWS = DH + STAT_ROWS
UNROLL = 8
COUNT_AT = NQ * NK // 2 + UNROLL
QUERY_AT = COUNT_AT + 1
KEY_AT = QUERY_AT + NQ
PLAN = KEY_AT + NK + 1
NOWHERE = 1 << 20
NEG = -1e30
SCALE = math.log2(math.e) / math.sqrt(DH)


def device(x, c, z, y):
    return ((x * NC + c) * NZ + z) * NY + y


WORK = [(p - 2) % NZ if p % 2 == 0 else p for p in range(NZ)]
PLACE = [
    [7, 2, 0, 1, 6, 4, 3, 5],
    [4, 5, 6, 2, 3, 1, 0, 7],
    [1, 7, 0, 4, 2, 3, 5, 6],
    [2, 0, 7, 4, 6, 5, 1, 3],
    [7, 1, 3, 0, 2, 6, 4, 5],
    [4, 5, 3, 2, 0, 6, 1, 7],
    [6, 7, 1, 5, 3, 2, 4, 0],
    [3, 0, 1, 7, 6, 4, 2, 5],
]
LIVES = [
    [
        sum(PLACE[WORK.index(z)].index(2 * x + c) << (3 * z) for z in range(NZ))
        for c in range(NC)
    ]
    for x in range(NX)
]


def transpose_pairs(back):
    pairs = []
    for x in range(NX):
        for c in range(NC):
            for z in range(NZ):
                for y in range(NY):
                    p = 2 * x + c
                    home = device(x, c, z, y)
                    work = device(PLACE[p][z] // 2, PLACE[p][z] % 2, WORK[p], y)
                    pairs.append((work, home) if back else (home, work))
    return pairs


def ring(n, d):
    return [(i, (i + d) % n) for i in range(n)]


def pack_queries_kernel(q_ref, out_ref):
    for h in range(H):
        part = q_ref[:, h * DH : (h + 1) * DH].astype(jnp.float32).T.astype(jnp.bfloat16)
        for x in range(NX):
            out_ref[x * H + h] = part


def pack_keys_kernel(y_ref, k_hbm, v_hbm, *refs):
    out_refs, (k_ref, v_ref, sems) = refs[:NY], refs[NY:]
    copies = [
        pltpu.make_async_copy(v_hbm, v_ref, sems.at[0]),
        pltpu.make_async_copy(k_hbm, k_ref, sems.at[1]),
    ]
    for copy in copies:
        copy.start()
    for copy in copies:
        copy.wait()
    for d, out_ref in enumerate(out_refs):
        at = pl.ds(pl.multiple_of(lax.rem(y_ref[0] + d, H) * DH, DH), DH)
        out_ref[0] = k_ref[:, at]
        out_ref[1] = v_ref[:, at].astype(jnp.float32).T.astype(jnp.bfloat16)


def join_kernel(*refs):
    at = 0
    for ref in refs[:-1]:
        refs[-1][at : at + ref.shape[0]] = ref[...]
        at += ref.shape[0]


def join(parts):
    count = sum(p.shape[0] for p in parts)
    return pl.pallas_call(
        join_kernel,
        out_shape=jax.ShapeDtypeStruct((count,) + parts[0].shape[1:], parts[0].dtype),
        in_specs=[VMEM] * len(parts),
        out_specs=VMEM,
        compiler_params=SMALL,
        cost_estimate=LIGHT,
    )(*parts)


def lowest_bit(mask):
    return 31 - lax.clz(mask & -mask)


def plan_kernel(need_ref, qblk_ref, kblk_ref, plan_ref):
    def list_row(j, count):
        plan_ref[QUERY_AT + j] = qblk_ref[j]

        def entry(carry):
            mask, count = carry
            rest = mask & (mask - 1)
            second = jnp.where(rest == 0, NK, lowest_bit(rest))
            plan_ref[count] = j * 1024 + lowest_bit(mask) * 32 + second
            return rest & (rest - 1), count + 1

        return lax.while_loop(lambda c: c[0] != 0, entry, (need_ref[j], count))[1]

    count = lax.fori_loop(0, NQ, list_row, jnp.int32(0))
    for u in range(UNROLL):
        plan_ref[count + u] = NQ * 1024 + NK * 32 + NK
    plan_ref[COUNT_AT] = count
    for s in range(NK):
        plan_ref[KEY_AT + s] = kblk_ref[s]
    plan_ref[KEY_AT + NK] = NOWHERE


def attend_kernel(plan_ref, start_ref, q_ref, kv_ref, out_ref, acc, top, total):
    acc[...] = jnp.zeros_like(acc)
    top[...] = jnp.full_like(top, NEG)
    total[...] = jnp.zeros_like(total)
    key_row = lax.broadcasted_iota(jnp.int32, (BLK, BLK), 0)
    lane = lax.broadcasted_iota(jnp.int32, (1, BLK), 1)

    def step(i, carry):
        done = []
        for u in range(UNROLL):
            entry = plan_ref[i * UNROLL + u]
            j = lax.shift_right_logical(entry, 10)
            jq = jnp.minimum(j, NQ - 1)
            slots = (lax.shift_right_logical(entry, 5) & 31, entry & 31)
            held = [jnp.minimum(s, NK - 1) for s in slots]
            scores = jnp.dot(
                jnp.concatenate([kv_ref[s, 0] for s in held], axis=0),
                q_ref[jq],
                preferred_element_type=jnp.float32,
            )
            masked = []
            for n, s in enumerate(slots):
                base = plan_ref[KEY_AT + s] * BLK
                low = start_ref[pl.ds(jq, 1), :] - base
                high = plan_ref[QUERY_AT + jq] * BLK + lane - base
                allowed = (key_row >= low) & (key_row <= high)
                part = scores[n * BLK : (n + 1) * BLK]
                masked.append(jnp.where(allowed, part * SCALE, NEG))
            scores = jnp.concatenate(masked, axis=0)
            peak = jnp.max(scores, axis=0, keepdims=True)
            weights = jnp.exp2(scores - peak)
            mass = jnp.sum(weights, axis=0, keepdims=True)
            part = jnp.dot(
                jnp.concatenate([kv_ref[s, 1] for s in held], axis=1),
                weights.astype(jnp.bfloat16),
                preferred_element_type=jnp.float32,
            )
            done.append((j, peak, mass, part))
        for j, peak, mass, part in done:
            at = pl.ds(j, 1)
            old = top[at, :]
            new = jnp.maximum(old, peak)
            keep = jnp.exp2(old - new)
            gain = jnp.exp2(peak - new)
            top[at, :] = new
            total[at, :] = total[at, :] * keep + mass * gain
            acc[j] = acc[j] * keep + part * gain
        return carry

    lax.fori_loop(0, (plan_ref[COUNT_AT] + UNROLL - 1) // UNROLL, step, 0)

    mass = total[:NQ, :]
    some = mass > 0.0
    safe = jnp.where(some, mass, 1.0)
    inverse = 1.0 / safe
    level = jnp.where(some, top[:NQ, :] + jnp.log2(safe), NEG)
    first = level.astype(jnp.bfloat16).astype(jnp.float32)
    second = (level - first).astype(jnp.bfloat16).astype(jnp.float32)
    third = level - first - second
    row = lax.broadcasted_iota(jnp.int32, (STAT_ROWS, BLK), 0)
    for j in range(NQ):
        one = slice(j, j + 1)
        out_ref[j, :DH, :] = (acc[j] * inverse[one]).astype(jnp.bfloat16)
        stat = jnp.where(
            row == 0, first[one], jnp.where(row == 1, second[one], third[one])
        )
        out_ref[j, DH:, :] = jnp.where(row < 3, stat, 0.0).astype(jnp.bfloat16)


def combine_kernel(parts_ref, out_ref):
    for h in range(H):
        levels = []
        for r in range(NX):
            stat = parts_ref[r * H + h, DH:, :].astype(jnp.float32)
            levels.append(stat[0:1] + stat[1:2] + stat[2:3])
        peak = functools.reduce(jnp.maximum, levels)
        shares = [jnp.exp2(level - peak) for level in levels]
        inverse = 1.0 / functools.reduce(jnp.add, shares)
        value = functools.reduce(
            jnp.add,
            [
                parts_ref[r * H + h, :DH, :].astype(jnp.float32) * (shares[r] * inverse)
                for r in range(NX)
            ],
        )
        out_ref[:, h * DH : (h + 1) * DH] = value.T.astype(jnp.bfloat16)


VMEM = pl.BlockSpec(memory_space=pltpu.VMEM)
SMEM = pl.BlockSpec(memory_space=pltpu.SMEM)
LIGHT = pl.CostEstimate(flops=1024, bytes_accessed=1024, transcendentals=0)
HBM = pl.BlockSpec(memory_space=pltpu.HBM)
SMALL = pltpu.CompilerParams(vmem_limit_bytes=8 << 20)


def on_device(queries, keys, values, block_pairs, doc_lengths):
    x, c, z, y = (lax.axis_index(name) for name in ("x", "c", "z", "y"))
    bf16 = jnp.bfloat16

    piece = jax.ShapeDtypeStruct((2, BLK, DH), bf16)
    split = pl.pallas_call(
        pack_keys_kernel,
        out_shape=[piece] * NY,
        in_specs=[SMEM, HBM, HBM],
        out_specs=[VMEM] * NY,
        scratch_shapes=[pltpu.VMEM((BLK, H * DH), bf16)] * 2 + [pltpu.SemaphoreType.DMA((2,))],
        compiler_params=SMALL,
        cost_estimate=LIGHT,
    )(
        y.reshape(1),
        pltpu.with_memory_space_constraint(keys, pltpu.HBM),
        pltpu.with_memory_space_constraint(values, pltpu.HBM),
    )
    moved = lax.ppermute(queries, ("x", "c", "z", "y"), transpose_pairs(False))
    pieces = [split[0]] + [lax.ppermute(split[d], "y", ring(NY, d)) for d in range(1, NY)]
    here = join([p[None] for p in pieces])
    moved, here = lax.optimization_barrier((moved, here))

    spread = pl.pallas_call(
        pack_queries_kernel,
        out_shape=jax.ShapeDtypeStruct((NQ, DH, BLK), bf16),
        in_specs=[VMEM],
        out_specs=VMEM,
        compiler_params=SMALL,
        cost_estimate=LIGHT,
    )(moved)
    mine = lax.all_to_all(spread, ("x", "y"), 0, 0, tiled=True)
    near = [
        here,
        lax.ppermute(here, "z", [(i, i ^ 1) for i in range(NZ)]),
        lax.ppermute(here, "z", [(i, (i + (2 if i % 2 else -2)) % NZ) for i in range(NZ)]),
    ]
    near[0], near[1], block_pairs, doc_lengths, x, c, z, y = lax.optimization_barrier(
        (near[0], near[1], block_pairs, doc_lengths, x, c, z, y)
    )
    other = [lax.ppermute(b, "c", ring(NC, 1)) for b in near]

    slot = jnp.arange(NQ, dtype=jnp.int32)
    digits = [
        lax.shift_right_logical(jnp.where(c == 0, LIVES[n][0], LIVES[n][1]), 3 * z) & 7
        for n in range(NX)
    ]
    lives = functools.reduce(
        lambda rest, n: jnp.where(slot // NY == n, digits[n], rest), range(NX), slot
    )
    query_block = PLANE * jnp.where(z % 2 == 0, lax.rem(z + 2, NZ), z) + NY * lives + slot % NY
    slot = jnp.arange(NK, dtype=jnp.int32)
    group = (slot // NY) % PLANES
    plane = lax.rem(z + jnp.where(z % 2 == 0, group, (NZ - group) % NZ), NZ)
    row = lax.rem(y + NY - slot % NY, NY)
    core = jnp.where(slot < PLANES * NY, c, 1 - c)
    key_block = PLANE * plane + 8 * row + 2 * x + core
    ends = jnp.sum(
        jnp.where(
            jnp.arange(16)[:, None] <= jnp.arange(16)[None, :], doc_lengths[:, None], 0
        ),
        axis=0,
    )
    token = query_block[:, None] * BLK + jnp.arange(BLK, dtype=jnp.int32)[None, :]
    start = jnp.max(jnp.where(ends[:, None, None] <= token[None], ends[:, None, None], 0), axis=0)
    first = jnp.max(
        jnp.where(ends[:, None] <= query_block[None] * BLK, ends[:, None], 0), axis=0
    )
    hit_query = (block_pairs[:, 0][None, :] == query_block[:, None]).astype(bf16)
    hit_key = (block_pairs[:, 1][None, :] == key_block[:, None]).astype(bf16)
    listed = lax.dot_general(
        hit_query, hit_key, (((1,), (1,)), ((), ())), preferred_element_type=jnp.float32
    )
    need = (
        (listed > 0.5)
        & (key_block[None, :] * BLK + (BLK - 1) >= first[:, None])
        & (key_block[None, :] <= query_block[:, None])
    )
    bits = jnp.left_shift(jnp.int32(1), jnp.arange(NK, dtype=jnp.int32))
    need = jnp.sum(jnp.where(need, bits[None, :], 0), axis=1)

    plan = pl.pallas_call(
        plan_kernel,
        out_shape=jax.ShapeDtypeStruct((PLAN,), jnp.int32),
        in_specs=[SMEM] * 3,
        out_specs=SMEM,
        compiler_params=SMALL,
        cost_estimate=LIGHT,
    )(need, query_block, key_block)
    parts = pl.pallas_call(
        attend_kernel,
        out_shape=jax.ShapeDtypeStruct((NQ, ROWS, BLK), bf16),
        in_specs=[SMEM, VMEM, VMEM, VMEM],
        out_specs=VMEM,
        scratch_shapes=[
            pltpu.VMEM((NQ + 1, DH, BLK), jnp.float32),
            pltpu.VMEM((NQ + 8, BLK), jnp.float32),
            pltpu.VMEM((NQ + 8, BLK), jnp.float32),
        ],
        compiler_params=pltpu.CompilerParams(vmem_limit_bytes=24 << 20),
    )(plan, start, mine, join([*near, *other]))

    gathered = lax.all_to_all(parts, ("x", "y"), 0, 0, tiled=True)
    result = pl.pallas_call(
        combine_kernel,
        out_shape=jax.ShapeDtypeStruct((BLK, H * DH), bf16),
        in_specs=[VMEM],
        out_specs=VMEM,
        compiler_params=SMALL,
        cost_estimate=LIGHT,
    )(gathered)
    return lax.ppermute(result, ("x", "c", "z", "y"), transpose_pairs(True))


def solution(mesh):
    fine = Mesh(mesh.devices.reshape(NX, NC, NZ, NY), ("x", "c", "z", "y"))
    return jax.shard_map(
        on_device,
        mesh=fine,
        in_specs=(
            P(("x", "c", "z", "y"), None),
            P(("z", "y", "x", "c"), None),
            P(("z", "y", "x", "c"), None),
            P(),
            P(),
        ),
        out_specs=P(("x", "c", "z", "y"), None),
        check_vma=False,
    )
```

```python
import functools
import math

import jax
import jax.numpy as jnp
from jax import lax
from jax.experimental import pallas as pl
from jax.experimental.pallas import tpu as pltpu
from jax.sharding import Mesh
from jax.sharding import PartitionSpec as P

H = 4
DH = 128
BLK = 128
NX, NC, NZ, NY = 4, 2, 8, 4
PLANE = 32
NQ = NX * NY
PLANES = 3
NK = PLANES * NY * NC
STAT_ROWS = 16
ROWS = DH + STAT_ROWS
UNROLL = 8
COUNT_AT = NQ * NK // 2 + UNROLL
QUERY_AT = COUNT_AT + 1
KEY_AT = QUERY_AT + NQ
PLAN = KEY_AT + NK + 1
NOWHERE = 1 << 20
NEG = -1e30
SCALE = math.log2(math.e) / math.sqrt(DH)


def device(x, c, z, y):
    return ((x * NC + c) * NZ + z) * NY + y


PLACE = [
    [5, 3, 1, 0, 6, 2, 4, 7],
    [5, 4, 7, 3, 1, 0, 6, 2],
    [7, 5, 6, 1, 3, 2, 0, 4],
    [0, 6, 7, 4, 5, 1, 3, 2],
    [2, 7, 0, 1, 3, 6, 5, 4],
    [5, 3, 2, 7, 1, 0, 6, 4],
    [7, 6, 4, 5, 3, 2, 1, 0],
    [5, 1, 7, 6, 0, 3, 4, 2],
]
LIVES = [
    [
        sum(PLACE[(z + 1) % NZ].index(2 * x + c) << (3 * z) for z in range(NZ))
        for c in range(NC)
    ]
    for x in range(NX)
]


def transpose_pairs(back):
    pairs = []
    for x in range(NX):
        for c in range(NC):
            for z in range(NZ):
                for y in range(NY):
                    p = 2 * x + c
                    home = device(x, c, z, y)
                    work = device(PLACE[p][z] // 2, PLACE[p][z] % 2, (p - 1) % NZ, y)
                    pairs.append((work, home) if back else (home, work))
    return pairs


def ring(n, d):
    return [(i, (i + d) % n) for i in range(n)]


def pack_queries_kernel(q_ref, out_ref):
    for h in range(H):
        part = q_ref[:, h * DH : (h + 1) * DH].astype(jnp.float32).T.astype(jnp.bfloat16)
        for x in range(NX):
            out_ref[x * H + h] = part


def pack_keys_kernel(y_ref, k_hbm, v_hbm, *refs):
    out_refs, (k_ref, v_ref, sems) = refs[:NY], refs[NY:]
    copies = [
        pltpu.make_async_copy(v_hbm, v_ref, sems.at[0]),
        pltpu.make_async_copy(k_hbm, k_ref, sems.at[1]),
    ]
    for copy in copies:
        copy.start()
    for copy in copies:
        copy.wait()
    for d, out_ref in enumerate(out_refs):
        at = pl.ds(pl.multiple_of(lax.rem(y_ref[0] + d, H) * DH, DH), DH)
        out_ref[0] = k_ref[:, at]
        out_ref[1] = v_ref[:, at].astype(jnp.float32).T.astype(jnp.bfloat16)


def join_kernel(*refs):
    at = 0
    for ref in refs[:-1]:
        refs[-1][at : at + ref.shape[0]] = ref[...]
        at += ref.shape[0]


def join(parts):
    count = sum(p.shape[0] for p in parts)
    return pl.pallas_call(
        join_kernel,
        out_shape=jax.ShapeDtypeStruct((count,) + parts[0].shape[1:], parts[0].dtype),
        in_specs=[VMEM] * len(parts),
        out_specs=VMEM,
        compiler_params=SMALL,
        cost_estimate=LIGHT,
    )(*parts)


def lowest_bit(mask):
    return 31 - lax.clz(mask & -mask)


def plan_kernel(need_ref, qblk_ref, kblk_ref, plan_ref):
    def list_row(j, count):
        plan_ref[QUERY_AT + j] = qblk_ref[j]

        def entry(carry):
            mask, count = carry
            rest = mask & (mask - 1)
            second = jnp.where(rest == 0, NK, lowest_bit(rest))
            plan_ref[count] = j * 1024 + lowest_bit(mask) * 32 + second
            return rest & (rest - 1), count + 1

        return lax.while_loop(lambda c: c[0] != 0, entry, (need_ref[j], count))[1]

    count = lax.fori_loop(0, NQ, list_row, jnp.int32(0))
    for u in range(UNROLL):
        plan_ref[count + u] = NQ * 1024 + NK * 32 + NK
    plan_ref[COUNT_AT] = count
    for s in range(NK):
        plan_ref[KEY_AT + s] = kblk_ref[s]
    plan_ref[KEY_AT + NK] = NOWHERE


def attend_kernel(plan_ref, start_ref, q_ref, kv_ref, out_ref, acc, top, total):
    acc[...] = jnp.zeros_like(acc)
    top[...] = jnp.full_like(top, NEG)
    total[...] = jnp.zeros_like(total)
    key_row = lax.broadcasted_iota(jnp.int32, (BLK, BLK), 0)
    lane = lax.broadcasted_iota(jnp.int32, (1, BLK), 1)

    def step(i, carry):
        done = []
        for u in range(UNROLL):
            entry = plan_ref[i * UNROLL + u]
            j = lax.shift_right_logical(entry, 10)
            jq = jnp.minimum(j, NQ - 1)
            slots = (lax.shift_right_logical(entry, 5) & 31, entry & 31)
            held = [jnp.minimum(s, NK - 1) for s in slots]
            scores = jnp.dot(
                jnp.concatenate([kv_ref[s, 0] for s in held], axis=0),
                q_ref[jq],
                preferred_element_type=jnp.float32,
            )
            masked = []
            for n, s in enumerate(slots):
                base = plan_ref[KEY_AT + s] * BLK
                low = start_ref[pl.ds(jq, 1), :] - base
                high = plan_ref[QUERY_AT + jq] * BLK + lane - base
                allowed = (key_row >= low) & (key_row <= high)
                part = scores[n * BLK : (n + 1) * BLK]
                masked.append(jnp.where(allowed, part * SCALE, NEG))
            scores = jnp.concatenate(masked, axis=0)
            peak = jnp.max(scores, axis=0, keepdims=True)
            weights = jnp.exp2(scores - peak)
            mass = jnp.sum(weights, axis=0, keepdims=True)
            part = jnp.dot(
                jnp.concatenate([kv_ref[s, 1] for s in held], axis=1),
                weights.astype(jnp.bfloat16),
                preferred_element_type=jnp.float32,
            )
            done.append((j, peak, mass, part))
        for j, peak, mass, part in done:
            at = pl.ds(j, 1)
            old = top[at, :]
            new = jnp.maximum(old, peak)
            keep = jnp.exp2(old - new)
            gain = jnp.exp2(peak - new)
            top[at, :] = new
            total[at, :] = total[at, :] * keep + mass * gain
            acc[j] = acc[j] * keep + part * gain
        return carry

    lax.fori_loop(0, (plan_ref[COUNT_AT] + UNROLL - 1) // UNROLL, step, 0)

    mass = total[:NQ, :]
    some = mass > 0.0
    safe = jnp.where(some, mass, 1.0)
    inverse = 1.0 / safe
    level = jnp.where(some, top[:NQ, :] + jnp.log2(safe), NEG)
    first = level.astype(jnp.bfloat16).astype(jnp.float32)
    second = (level - first).astype(jnp.bfloat16).astype(jnp.float32)
    third = level - first - second
    row = lax.broadcasted_iota(jnp.int32, (STAT_ROWS, BLK), 0)
    for j in range(NQ):
        one = slice(j, j + 1)
        out_ref[j, :DH, :] = (acc[j] * inverse[one]).astype(jnp.bfloat16)
        stat = jnp.where(
            row == 0, first[one], jnp.where(row == 1, second[one], third[one])
        )
        out_ref[j, DH:, :] = jnp.where(row < 3, stat, 0.0).astype(jnp.bfloat16)


def combine_kernel(parts_ref, out_ref):
    for h in range(H):
        levels = []
        for r in range(NX):
            stat = parts_ref[r * H + h, DH:, :].astype(jnp.float32)
            levels.append(stat[0:1] + stat[1:2] + stat[2:3])
        peak = functools.reduce(jnp.maximum, levels)
        shares = [jnp.exp2(level - peak) for level in levels]
        inverse = 1.0 / functools.reduce(jnp.add, shares)
        value = functools.reduce(
            jnp.add,
            [
                parts_ref[r * H + h, :DH, :].astype(jnp.float32) * (shares[r] * inverse)
                for r in range(NX)
            ],
        )
        out_ref[:, h * DH : (h + 1) * DH] = value.T.astype(jnp.bfloat16)


VMEM = pl.BlockSpec(memory_space=pltpu.VMEM)
SMEM = pl.BlockSpec(memory_space=pltpu.SMEM)
LIGHT = pl.CostEstimate(flops=1024, bytes_accessed=1024, transcendentals=0)
HBM = pl.BlockSpec(memory_space=pltpu.HBM)
SMALL = pltpu.CompilerParams(vmem_limit_bytes=8 << 20)


def on_device(queries, keys, values, block_pairs, doc_lengths):
    x, c, z, y = (lax.axis_index(name) for name in ("x", "c", "z", "y"))
    bf16 = jnp.bfloat16

    piece = jax.ShapeDtypeStruct((2, BLK, DH), bf16)
    split = pl.pallas_call(
        pack_keys_kernel,
        out_shape=[piece] * NY,
        in_specs=[SMEM, HBM, HBM],
        out_specs=[VMEM] * NY,
        scratch_shapes=[pltpu.VMEM((BLK, H * DH), bf16)] * 2 + [pltpu.SemaphoreType.DMA((2,))],
        compiler_params=SMALL,
        cost_estimate=LIGHT,
    )(
        y.reshape(1),
        pltpu.with_memory_space_constraint(keys, pltpu.HBM),
        pltpu.with_memory_space_constraint(values, pltpu.HBM),
    )
    moved = lax.ppermute(queries, ("x", "c", "z", "y"), transpose_pairs(False))
    pieces = [split[0]] + [lax.ppermute(split[d], "y", ring(NY, d)) for d in range(1, NY)]
    here = join([p[None] for p in pieces])
    moved, here = lax.optimization_barrier((moved, here))

    spread = pl.pallas_call(
        pack_queries_kernel,
        out_shape=jax.ShapeDtypeStruct((NQ, DH, BLK), bf16),
        in_specs=[VMEM],
        out_specs=VMEM,
        compiler_params=SMALL,
        cost_estimate=LIGHT,
    )(moved)
    mine = lax.all_to_all(spread, ("x", "y"), 0, 0, tiled=True)
    near = [here, lax.ppermute(here, "z", ring(NZ, 1)), lax.ppermute(here, "z", ring(NZ, -1))]
    near[0], near[1], block_pairs, doc_lengths, x, c, z, y = lax.optimization_barrier(
        (near[0], near[1], block_pairs, doc_lengths, x, c, z, y)
    )
    other = [lax.ppermute(b, "c", ring(NC, 1)) for b in near]

    slot = jnp.arange(NQ, dtype=jnp.int32)
    digits = [
        lax.shift_right_logical(jnp.where(c == 0, LIVES[n][0], LIVES[n][1]), 3 * z) & 7
        for n in range(NX)
    ]
    lives = functools.reduce(
        lambda rest, n: jnp.where(slot // NY == n, digits[n], rest), range(NX), slot
    )
    query_block = PLANE * lax.rem(z + 1, NZ) + NY * lives + slot % NY
    slot = jnp.arange(NK, dtype=jnp.int32)
    group = (slot // NY) % PLANES
    plane = lax.rem(z + jnp.where(group == 0, 0, jnp.where(group == 1, NZ - 1, 1)), NZ)
    row = lax.rem(y + NY - slot % NY, NY)
    core = jnp.where(slot < PLANES * NY, c, 1 - c)
    key_block = PLANE * plane + 8 * row + 2 * x + core
    ends = jnp.sum(
        jnp.where(
            jnp.arange(16)[:, None] <= jnp.arange(16)[None, :], doc_lengths[:, None], 0
        ),
        axis=0,
    )
    token = query_block[:, None] * BLK + jnp.arange(BLK, dtype=jnp.int32)[None, :]
    start = jnp.max(jnp.where(ends[:, None, None] <= token[None], ends[:, None, None], 0), axis=0)
    first = jnp.max(
        jnp.where(ends[:, None] <= query_block[None] * BLK, ends[:, None], 0), axis=0
    )
    hit_query = (block_pairs[:, 0][None, :] == query_block[:, None]).astype(bf16)
    hit_key = (block_pairs[:, 1][None, :] == key_block[:, None]).astype(bf16)
    listed = lax.dot_general(
        hit_query, hit_key, (((1,), (1,)), ((), ())), preferred_element_type=jnp.float32
    )
    need = (
        (listed > 0.5)
        & (key_block[None, :] * BLK + (BLK - 1) >= first[:, None])
        & (key_block[None, :] <= query_block[:, None])
    )
    bits = jnp.left_shift(jnp.int32(1), jnp.arange(NK, dtype=jnp.int32))
    need = jnp.sum(jnp.where(need, bits[None, :], 0), axis=1)

    plan = pl.pallas_call(
        plan_kernel,
        out_shape=jax.ShapeDtypeStruct((PLAN,), jnp.int32),
        in_specs=[SMEM] * 3,
        out_specs=SMEM,
        compiler_params=SMALL,
        cost_estimate=LIGHT,
    )(need, query_block, key_block)
    parts = pl.pallas_call(
        attend_kernel,
        out_shape=jax.ShapeDtypeStruct((NQ, ROWS, BLK), bf16),
        in_specs=[SMEM, VMEM, VMEM, VMEM],
        out_specs=VMEM,
        scratch_shapes=[
            pltpu.VMEM((NQ + 1, DH, BLK), jnp.float32),
            pltpu.VMEM((NQ + 8, BLK), jnp.float32),
            pltpu.VMEM((NQ + 8, BLK), jnp.float32),
        ],
        compiler_params=pltpu.CompilerParams(vmem_limit_bytes=24 << 20),
    )(plan, start, mine, join([*near, *other]))

    gathered = lax.all_to_all(parts, ("x", "y"), 0, 0, tiled=True)
    result = pl.pallas_call(
        combine_kernel,
        out_shape=jax.ShapeDtypeStruct((BLK, H * DH), bf16),
        in_specs=[VMEM],
        out_specs=VMEM,
        compiler_params=SMALL,
        cost_estimate=LIGHT,
    )(gathered)
    return lax.ppermute(result, ("x", "c", "z", "y"), transpose_pairs(True))


def solution(mesh):
    fine = Mesh(mesh.devices.reshape(NX, NC, NZ, NY), ("x", "c", "z", "y"))
    return jax.shard_map(
        on_device,
        mesh=fine,
        in_specs=(
            P(("x", "c", "z", "y"), None),
            P(("z", "y", "x", "c"), None),
            P(("z", "y", "x", "c"), None),
            P(),
            P(),
        ),
        out_specs=P(("x", "c", "z", "y"), None),
        check_vma=False,
    )
```

```python
import functools
import math

import jax
import jax.numpy as jnp
from jax import lax
from jax.experimental import pallas as pl
from jax.experimental.pallas import tpu as pltpu
from jax.sharding import Mesh
from jax.sharding import PartitionSpec as P

H = 4
DH = 128
BLK = 128
NX, NC, NZ, NY = 4, 2, 8, 4
PLANE = 32
NQ = NX * NY
PLANES = 3
NK = PLANES * NY * NC
STAT_ROWS = 16
ROWS = DH + STAT_ROWS
UNROLL = 8
COUNT_AT = NQ * NK // 2 + UNROLL
QUERY_AT = COUNT_AT + 1
KEY_AT = QUERY_AT + NQ
PLAN = KEY_AT + NK + 1
NOWHERE = 1 << 20
NEG = -1e30
SCALE = math.log2(math.e) / math.sqrt(DH)


def device(x, c, z, y):
    return ((x * NC + c) * NZ + z) * NY + y


PLACE = [
    [5, 3, 1, 0, 6, 2, 4, 7],
    [5, 4, 7, 3, 1, 0, 6, 2],
    [7, 5, 6, 1, 3, 2, 0, 4],
    [0, 6, 7, 4, 5, 1, 3, 2],
    [2, 7, 0, 1, 3, 6, 5, 4],
    [5, 3, 2, 7, 1, 0, 6, 4],
    [7, 6, 4, 5, 3, 2, 1, 0],
    [5, 1, 7, 6, 0, 3, 4, 2],
]
LIVES = [
    [
        sum(PLACE[(z + 1) % NZ].index(2 * x + c) << (3 * z) for z in range(NZ))
        for c in range(NC)
    ]
    for x in range(NX)
]


def transpose_pairs(back):
    pairs = []
    for x in range(NX):
        for c in range(NC):
            for z in range(NZ):
                for y in range(NY):
                    p = 2 * x + c
                    home = device(x, c, z, y)
                    work = device(PLACE[p][z] // 2, PLACE[p][z] % 2, (p - 1) % NZ, y)
                    pairs.append((work, home) if back else (home, work))
    return pairs


def ring(n, d):
    return [(i, (i + d) % n) for i in range(n)]


def pack_queries_kernel(q_ref, out_ref):
    for h in range(H):
        part = q_ref[:, h * DH : (h + 1) * DH].astype(jnp.float32).T.astype(jnp.bfloat16)
        for x in range(NX):
            out_ref[x * H + h] = part


def pack_keys_kernel(y_ref, k_hbm, v_hbm, *refs):
    out_refs, (k_ref, v_ref, sems) = refs[:NY], refs[NY:]
    copies = [
        pltpu.make_async_copy(v_hbm, v_ref, sems.at[0]),
        pltpu.make_async_copy(k_hbm, k_ref, sems.at[1]),
    ]
    for copy in copies:
        copy.start()
    for copy in copies:
        copy.wait()
    for d, out_ref in enumerate(out_refs):
        at = pl.ds(pl.multiple_of(lax.rem(y_ref[0] + d, H) * DH, DH), DH)
        out_ref[0] = k_ref[:, at]
        out_ref[1] = v_ref[:, at].astype(jnp.float32).T.astype(jnp.bfloat16)


def join_kernel(*refs):
    at = 0
    for ref in refs[:-1]:
        refs[-1][at : at + ref.shape[0]] = ref[...]
        at += ref.shape[0]


def join(parts):
    count = sum(p.shape[0] for p in parts)
    return pl.pallas_call(
        join_kernel,
        out_shape=jax.ShapeDtypeStruct((count,) + parts[0].shape[1:], parts[0].dtype),
        in_specs=[VMEM] * len(parts),
        out_specs=VMEM,
        compiler_params=SMALL,
        cost_estimate=LIGHT,
    )(*parts)


def lowest_bit(mask):
    return 31 - lax.clz(mask & -mask)


def plan_kernel(need_ref, qblk_ref, kblk_ref, plan_ref):
    def list_row(j, count):
        plan_ref[QUERY_AT + j] = qblk_ref[j]

        def entry(carry):
            mask, count = carry
            rest = mask & (mask - 1)
            second = jnp.where(rest == 0, NK, lowest_bit(rest))
            plan_ref[count] = j * 1024 + lowest_bit(mask) * 32 + second
            return rest & (rest - 1), count + 1

        return lax.while_loop(lambda c: c[0] != 0, entry, (need_ref[j], count))[1]

    count = lax.fori_loop(0, NQ, list_row, jnp.int32(0))
    for u in range(UNROLL):
        plan_ref[count + u] = NQ * 1024 + NK * 32 + NK
    plan_ref[COUNT_AT] = count
    for s in range(NK):
        plan_ref[KEY_AT + s] = kblk_ref[s]
    plan_ref[KEY_AT + NK] = NOWHERE


def attend_kernel(plan_ref, start_ref, q_ref, kv_ref, out_ref, acc, top, total):
    acc[...] = jnp.zeros_like(acc)
    top[...] = jnp.full_like(top, NEG)
    total[...] = jnp.zeros_like(total)
    key_row = lax.broadcasted_iota(jnp.int32, (BLK, BLK), 0)
    lane = lax.broadcasted_iota(jnp.int32, (1, BLK), 1)

    def step(first, width):
        done = []
        for u in range(width):
            entry = plan_ref[first + u]
            j = lax.shift_right_logical(entry, 10)
            jq = jnp.minimum(j, NQ - 1)
            slots = (lax.shift_right_logical(entry, 5) & 31, entry & 31)
            held = [jnp.minimum(s, NK - 1) for s in slots]
            scores = jnp.dot(
                jnp.concatenate([kv_ref[s, 0] for s in held], axis=0),
                q_ref[jq],
                preferred_element_type=jnp.float32,
            )
            masked = []
            for n, s in enumerate(slots):
                base = plan_ref[KEY_AT + s] * BLK
                low = start_ref[pl.ds(jq, 1), :] - base
                high = plan_ref[QUERY_AT + jq] * BLK + lane - base
                allowed = (key_row >= low) & (key_row <= high)
                part = scores[n * BLK : (n + 1) * BLK]
                masked.append(jnp.where(allowed, part * SCALE, NEG))
            scores = jnp.concatenate(masked, axis=0)
            peak = jnp.max(scores, axis=0, keepdims=True)
            weights = jnp.exp2(scores - peak)
            mass = jnp.sum(weights, axis=0, keepdims=True)
            part = jnp.dot(
                jnp.concatenate([kv_ref[s, 1] for s in held], axis=1),
                weights.astype(jnp.bfloat16),
                preferred_element_type=jnp.float32,
            )
            done.append((j, peak, mass, part))
        for j, peak, mass, part in done:
            at = pl.ds(j, 1)
            old = top[at, :]
            new = jnp.maximum(old, peak)
            keep = jnp.exp2(old - new)
            gain = jnp.exp2(peak - new)
            top[at, :] = new
            total[at, :] = total[at, :] * keep + mass * gain
            acc[j] = acc[j] * keep + part * gain

    def wide(i, carry):
        step(i * (2 * UNROLL), 2 * UNROLL)
        return carry

    turns = (plan_ref[COUNT_AT] + UNROLL - 1) // UNROLL
    lax.fori_loop(0, turns // 2, wide, 0)

    @pl.when(turns % 2 == 1)
    def _():
        step((turns - 1) * UNROLL, UNROLL)

    mass = total[:NQ, :]
    some = mass > 0.0
    safe = jnp.where(some, mass, 1.0)
    inverse = 1.0 / safe
    level = jnp.where(some, top[:NQ, :] + jnp.log2(safe), NEG)
    first = level.astype(jnp.bfloat16).astype(jnp.float32)
    second = (level - first).astype(jnp.bfloat16).astype(jnp.float32)
    third = level - first - second
    row = lax.broadcasted_iota(jnp.int32, (STAT_ROWS, BLK), 0)
    for j in range(NQ):
        one = slice(j, j + 1)
        out_ref[j, :DH, :] = (acc[j] * inverse[one]).astype(jnp.bfloat16)
        stat = jnp.where(
            row == 0, first[one], jnp.where(row == 1, second[one], third[one])
        )
        out_ref[j, DH:, :] = jnp.where(row < 3, stat, 0.0).astype(jnp.bfloat16)


def combine_kernel(parts_ref, out_ref):
    for h in range(H):
        levels = []
        for r in range(NX):
            stat = parts_ref[r * H + h, DH:, :].astype(jnp.float32)
            levels.append(stat[0:1] + stat[1:2] + stat[2:3])
        peak = functools.reduce(jnp.maximum, levels)
        shares = [jnp.exp2(level - peak) for level in levels]
        inverse = 1.0 / functools.reduce(jnp.add, shares)
        value = functools.reduce(
            jnp.add,
            [
                parts_ref[r * H + h, :DH, :].astype(jnp.float32) * (shares[r] * inverse)
                for r in range(NX)
            ],
        )
        out_ref[:, h * DH : (h + 1) * DH] = value.T.astype(jnp.bfloat16)


VMEM = pl.BlockSpec(memory_space=pltpu.VMEM)
SMEM = pl.BlockSpec(memory_space=pltpu.SMEM)
LIGHT = pl.CostEstimate(flops=1024, bytes_accessed=1024, transcendentals=0)
HBM = pl.BlockSpec(memory_space=pltpu.HBM)
SMALL = pltpu.CompilerParams(vmem_limit_bytes=8 << 20)


def on_device(queries, keys, values, block_pairs, doc_lengths):
    x, c, z, y = (lax.axis_index(name) for name in ("x", "c", "z", "y"))
    bf16 = jnp.bfloat16

    piece = jax.ShapeDtypeStruct((2, BLK, DH), bf16)
    split = pl.pallas_call(
        pack_keys_kernel,
        out_shape=[piece] * NY,
        in_specs=[SMEM, HBM, HBM],
        out_specs=[VMEM] * NY,
        scratch_shapes=[pltpu.VMEM((BLK, H * DH), bf16)] * 2 + [pltpu.SemaphoreType.DMA((2,))],
        compiler_params=SMALL,
        cost_estimate=LIGHT,
    )(
        y.reshape(1),
        pltpu.with_memory_space_constraint(keys, pltpu.HBM),
        pltpu.with_memory_space_constraint(values, pltpu.HBM),
    )
    moved = lax.ppermute(queries, ("x", "c", "z", "y"), transpose_pairs(False))
    pieces = [split[0]] + [lax.ppermute(split[d], "y", ring(NY, d)) for d in range(1, NY)]
    here = join([p[None] for p in pieces])
    moved, here = lax.optimization_barrier((moved, here))

    spread = pl.pallas_call(
        pack_queries_kernel,
        out_shape=jax.ShapeDtypeStruct((NQ, DH, BLK), bf16),
        in_specs=[VMEM],
        out_specs=VMEM,
        compiler_params=SMALL,
        cost_estimate=LIGHT,
    )(moved)
    mine = lax.all_to_all(spread, ("x", "y"), 0, 0, tiled=True)
    near = [here, lax.ppermute(here, "z", ring(NZ, 1)), lax.ppermute(here, "z", ring(NZ, -1))]
    near[0], near[1], block_pairs, doc_lengths, x, c, z, y = lax.optimization_barrier(
        (near[0], near[1], block_pairs, doc_lengths, x, c, z, y)
    )
    other = [lax.ppermute(b, "c", ring(NC, 1)) for b in near]

    slot = jnp.arange(NQ, dtype=jnp.int32)
    digits = [
        lax.shift_right_logical(jnp.where(c == 0, LIVES[n][0], LIVES[n][1]), 3 * z) & 7
        for n in range(NX)
    ]
    lives = functools.reduce(
        lambda rest, n: jnp.where(slot // NY == n, digits[n], rest), range(NX), slot
    )
    query_block = PLANE * lax.rem(z + 1, NZ) + NY * lives + slot % NY
    slot = jnp.arange(NK, dtype=jnp.int32)
    group = (slot // NY) % PLANES
    plane = lax.rem(z + jnp.where(group == 0, 0, jnp.where(group == 1, NZ - 1, 1)), NZ)
    row = lax.rem(y + NY - slot % NY, NY)
    core = jnp.where(slot < PLANES * NY, c, 1 - c)
    key_block = PLANE * plane + 8 * row + 2 * x + core
    ends = jnp.sum(
        jnp.where(
            jnp.arange(16)[:, None] <= jnp.arange(16)[None, :], doc_lengths[:, None], 0
        ),
        axis=0,
    )
    token = query_block[:, None] * BLK + jnp.arange(BLK, dtype=jnp.int32)[None, :]
    start = jnp.max(jnp.where(ends[:, None, None] <= token[None], ends[:, None, None], 0), axis=0)
    first = jnp.max(
        jnp.where(ends[:, None] <= query_block[None] * BLK, ends[:, None], 0), axis=0
    )
    hit_query = (block_pairs[:, 0][None, :] == query_block[:, None]).astype(bf16)
    hit_key = (block_pairs[:, 1][None, :] == key_block[:, None]).astype(bf16)
    listed = lax.dot_general(
        hit_query, hit_key, (((1,), (1,)), ((), ())), preferred_element_type=jnp.float32
    )
    need = (
        (listed > 0.5)
        & (key_block[None, :] * BLK + (BLK - 1) >= first[:, None])
        & (key_block[None, :] <= query_block[:, None])
    )
    bits = jnp.left_shift(jnp.int32(1), jnp.arange(NK, dtype=jnp.int32))
    need = jnp.sum(jnp.where(need, bits[None, :], 0), axis=1)

    plan = pl.pallas_call(
        plan_kernel,
        out_shape=jax.ShapeDtypeStruct((PLAN,), jnp.int32),
        in_specs=[SMEM] * 3,
        out_specs=SMEM,
        compiler_params=SMALL,
        cost_estimate=LIGHT,
    )(need, query_block, key_block)
    parts = pl.pallas_call(
        attend_kernel,
        out_shape=jax.ShapeDtypeStruct((NQ, ROWS, BLK), bf16),
        in_specs=[SMEM, VMEM, VMEM, VMEM],
        out_specs=VMEM,
        scratch_shapes=[
            pltpu.VMEM((NQ + 1, DH, BLK), jnp.float32),
            pltpu.VMEM((NQ + 8, BLK), jnp.float32),
            pltpu.VMEM((NQ + 8, BLK), jnp.float32),
        ],
        compiler_params=pltpu.CompilerParams(vmem_limit_bytes=24 << 20),
    )(plan, start, mine, join([*near, *other]))

    gathered = lax.all_to_all(parts, ("x", "y"), 0, 0, tiled=True)
    result = pl.pallas_call(
        combine_kernel,
        out_shape=jax.ShapeDtypeStruct((BLK, H * DH), bf16),
        in_specs=[VMEM],
        out_specs=VMEM,
        compiler_params=SMALL,
        cost_estimate=LIGHT,
    )(gathered)
    return lax.ppermute(result, ("x", "c", "z", "y"), transpose_pairs(True))


def solution(mesh):
    fine = Mesh(mesh.devices.reshape(NX, NC, NZ, NY), ("x", "c", "z", "y"))
    return jax.shard_map(
        on_device,
        mesh=fine,
        in_specs=(
            P(("x", "c", "z", "y"), None),
            P(("z", "y", "x", "c"), None),
            P(("z", "y", "x", "c"), None),
            P(),
            P(),
        ),
        out_specs=P(("x", "c", "z", "y"), None),
        check_vma=False,
    )
```

```python
import functools
import math

import jax
import jax.numpy as jnp
from jax import lax
from jax.experimental import pallas as pl
from jax.experimental.pallas import tpu as pltpu
from jax.sharding import Mesh
from jax.sharding import PartitionSpec as P

H = 4
DH = 128
BLK = 128
NX, NC, NZ, NY = 4, 2, 8, 4
PLANE = 32
NQ = NX * NY
PLANES = 3
NK = PLANES * NY * NC
STAT_ROWS = 16
ROWS = DH + STAT_ROWS
UNROLL = 8
COUNT_AT = NQ * NK // 2 + UNROLL
QUERY_AT = COUNT_AT + 1
KEY_AT = QUERY_AT + NQ
PLAN = KEY_AT + NK + 1
NOWHERE = 1 << 20
NEG = -1e30
SCALE = math.log2(math.e) / math.sqrt(DH)


def device(x, c, z, y):
    return ((x * NC + c) * NZ + z) * NY + y


PLACE = [
    [5, 3, 1, 0, 6, 2, 4, 7],
    [5, 4, 7, 3, 1, 0, 6, 2],
    [7, 5, 6, 1, 3, 2, 0, 4],
    [0, 6, 7, 4, 5, 1, 3, 2],
    [2, 7, 0, 1, 3, 6, 5, 4],
    [5, 3, 2, 7, 1, 0, 6, 4],
    [7, 6, 4, 5, 3, 2, 1, 0],
    [5, 1, 7, 6, 0, 3, 4, 2],
]
LIVES = [
    [
        sum(PLACE[(z + 1) % NZ].index(2 * x + c) << (3 * z) for z in range(NZ))
        for c in range(NC)
    ]
    for x in range(NX)
]


def transpose_pairs(back):
    pairs = []
    for x in range(NX):
        for c in range(NC):
            for z in range(NZ):
                for y in range(NY):
                    p = 2 * x + c
                    home = device(x, c, z, y)
                    work = device(PLACE[p][z] // 2, PLACE[p][z] % 2, (p - 1) % NZ, y)
                    pairs.append((work, home) if back else (home, work))
    return pairs


def ring(n, d):
    return [(i, (i + d) % n) for i in range(n)]


def pack_queries_kernel(q_ref, out_ref):
    for h in range(H):
        part = q_ref[:, h * DH : (h + 1) * DH].astype(jnp.float32).T.astype(jnp.bfloat16)
        for x in range(NX):
            out_ref[x * H + h] = part


def pack_keys_kernel(y_ref, k_hbm, v_hbm, *refs):
    out_refs, (k_ref, v_ref, sems) = refs[:NY], refs[NY:]
    copies = [
        pltpu.make_async_copy(v_hbm, v_ref, sems.at[0]),
        pltpu.make_async_copy(k_hbm, k_ref, sems.at[1]),
    ]
    for copy in copies:
        copy.start()
    for copy in copies:
        copy.wait()
    for d, out_ref in enumerate(out_refs):
        at = pl.ds(pl.multiple_of(lax.rem(y_ref[0] + d, H) * DH, DH), DH)
        out_ref[0] = k_ref[:, at]
        out_ref[1] = v_ref[:, at].astype(jnp.float32).T.astype(jnp.bfloat16)


def join_kernel(*refs):
    at = 0
    for ref in refs[:-1]:
        refs[-1][at : at + ref.shape[0]] = ref[...]
        at += ref.shape[0]


def join(parts):
    count = sum(p.shape[0] for p in parts)
    return pl.pallas_call(
        join_kernel,
        out_shape=jax.ShapeDtypeStruct((count,) + parts[0].shape[1:], parts[0].dtype),
        in_specs=[VMEM] * len(parts),
        out_specs=VMEM,
        compiler_params=SMALL,
        cost_estimate=LIGHT,
    )(*parts)


def lowest_bit(mask):
    return 31 - lax.clz(mask & -mask)


def plan_kernel(need_ref, qblk_ref, kblk_ref, plan_ref):
    def list_row(j, count):
        plan_ref[QUERY_AT + j] = qblk_ref[j]

        def entry(carry):
            mask, count = carry
            rest = mask & (mask - 1)
            second = jnp.where(rest == 0, NK, lowest_bit(rest))
            plan_ref[count] = j * 1024 + lowest_bit(mask) * 32 + second
            return rest & (rest - 1), count + 1

        return lax.while_loop(lambda c: c[0] != 0, entry, (need_ref[j], count))[1]

    count = lax.fori_loop(0, NQ, list_row, jnp.int32(0))
    for u in range(UNROLL):
        plan_ref[count + u] = NQ * 1024 + NK * 32 + NK
    plan_ref[COUNT_AT] = count
    for s in range(NK):
        plan_ref[KEY_AT + s] = kblk_ref[s]
    plan_ref[KEY_AT + NK] = NOWHERE


def attend_kernel(plan_ref, start_ref, q_ref, kv_ref, out_ref, acc, top, total):
    acc[...] = jnp.zeros_like(acc)
    top[...] = jnp.full_like(top, NEG)
    total[...] = jnp.zeros_like(total)
    key_row = lax.broadcasted_iota(jnp.int32, (BLK, BLK), 0)
    lane = lax.broadcasted_iota(jnp.int32, (1, BLK), 1)

    def step(first, width):
        done = []
        for u in range(width):
            entry = plan_ref[first + u]
            j = lax.shift_right_logical(entry, 10)
            jq = jnp.minimum(j, NQ - 1)
            slots = (lax.shift_right_logical(entry, 5) & 31, entry & 31)
            held = [jnp.minimum(s, NK - 1) for s in slots]
            scores = jnp.dot(
                jnp.concatenate([kv_ref[s, 0] for s in held], axis=0),
                q_ref[jq],
                preferred_element_type=jnp.float32,
            )
            masked = []
            for n, s in enumerate(slots):
                base = plan_ref[KEY_AT + s] * BLK
                low = start_ref[pl.ds(jq, 1), :] - base
                high = plan_ref[QUERY_AT + jq] * BLK + lane - base
                allowed = (key_row >= low) & (key_row <= high)
                part = scores[n * BLK : (n + 1) * BLK]
                masked.append(jnp.where(allowed, part * SCALE, NEG))
            scores = jnp.concatenate(masked, axis=0)
            peak = jnp.max(scores, axis=0, keepdims=True)
            weights = jnp.exp2(scores - peak)
            mass = jnp.sum(weights, axis=0, keepdims=True)
            part = jnp.dot(
                jnp.concatenate([kv_ref[s, 1] for s in held], axis=1),
                weights.astype(jnp.bfloat16),
                preferred_element_type=jnp.float32,
            )
            done.append((j, peak, mass, part))
        for j, peak, mass, part in done:
            at = pl.ds(j, 1)
            old = top[at, :]
            new = jnp.maximum(old, peak)
            keep = jnp.exp2(old - new)
            gain = jnp.exp2(peak - new)
            top[at, :] = new
            total[at, :] = total[at, :] * keep + mass * gain
            acc[j] = acc[j] * keep + part * gain

    def wide(i, carry):
        step(i * (2 * UNROLL), 2 * UNROLL)
        return carry

    turns = (plan_ref[COUNT_AT] + UNROLL - 1) // UNROLL
    lax.fori_loop(0, turns // 2, wide, 0)

    @pl.when(turns % 2 == 1)
    def _():
        step((turns - 1) * UNROLL, UNROLL)

    mass = total[:NQ, :]
    some = mass > 0.0
    safe = jnp.where(some, mass, 1.0)
    inverse = 1.0 / safe
    level = jnp.where(some, top[:NQ, :] + jnp.log2(safe), NEG)
    first = level.astype(jnp.bfloat16).astype(jnp.float32)
    second = (level - first).astype(jnp.bfloat16).astype(jnp.float32)
    third = level - first - second
    row = lax.broadcasted_iota(jnp.int32, (STAT_ROWS, BLK), 0)
    for j in range(NQ):
        one = slice(j, j + 1)
        out_ref[j, :DH, :] = (acc[j] * inverse[one]).astype(jnp.bfloat16)
        stat = jnp.where(
            row == 0, first[one], jnp.where(row == 1, second[one], third[one])
        )
        out_ref[j, DH:, :] = jnp.where(row < 3, stat, 0.0).astype(jnp.bfloat16)


def combine_kernel(parts_ref, out_ref):
    for h in range(H):
        levels = []
        for r in range(NX):
            stat = parts_ref[r * H + h, DH:, :].astype(jnp.float32)
            levels.append(stat[0:1] + stat[1:2] + stat[2:3])
        peak = functools.reduce(jnp.maximum, levels)
        shares = [jnp.exp2(level - peak) for level in levels]
        inverse = 1.0 / functools.reduce(jnp.add, shares)
        value = functools.reduce(
            jnp.add,
            [
                parts_ref[r * H + h, :DH, :].astype(jnp.float32) * (shares[r] * inverse)
                for r in range(NX)
            ],
        )
        out_ref[:, h * DH : (h + 1) * DH] = value.T.astype(jnp.bfloat16)


VMEM = pl.BlockSpec(memory_space=pltpu.VMEM)
SMEM = pl.BlockSpec(memory_space=pltpu.SMEM)
LIGHT = pl.CostEstimate(flops=1024, bytes_accessed=1024, transcendentals=0)
HBM = pl.BlockSpec(memory_space=pltpu.HBM)
SMALL = pltpu.CompilerParams(vmem_limit_bytes=8 << 20)


def on_device(queries, keys, values, block_pairs, doc_lengths):
    x, c, z, y = (lax.axis_index(name) for name in ("x", "c", "z", "y"))
    bf16 = jnp.bfloat16

    piece = jax.ShapeDtypeStruct((2, BLK, DH), bf16)
    split = pl.pallas_call(
        pack_keys_kernel,
        out_shape=[piece] * NY,
        in_specs=[SMEM, HBM, HBM],
        out_specs=[VMEM] * NY,
        scratch_shapes=[pltpu.VMEM((BLK, H * DH), bf16)] * 2 + [pltpu.SemaphoreType.DMA((2,))],
        compiler_params=SMALL,
        cost_estimate=LIGHT,
    )(
        y.reshape(1),
        pltpu.with_memory_space_constraint(keys, pltpu.HBM),
        pltpu.with_memory_space_constraint(values, pltpu.HBM),
    )
    moved = lax.ppermute(queries, ("x", "c", "z", "y"), transpose_pairs(False))
    pieces = [split[0]] + [lax.ppermute(split[d], "y", ring(NY, d)) for d in range(1, NY)]
    here = join([p[None] for p in pieces])
    moved, here = lax.optimization_barrier((moved, here))

    spread = pl.pallas_call(
        pack_queries_kernel,
        out_shape=pltpu.VMEM((NQ, DH, BLK), bf16),
        in_specs=[VMEM],
        out_specs=VMEM,
        compiler_params=SMALL,
        cost_estimate=LIGHT,
    )(moved)
    mine = lax.all_to_all(spread, ("x", "y"), 0, 0, tiled=True)
    near = [here, lax.ppermute(here, "z", ring(NZ, 1)), lax.ppermute(here, "z", ring(NZ, -1))]
    near[0], near[1], block_pairs, doc_lengths, x, c, z, y = lax.optimization_barrier(
        (near[0], near[1], block_pairs, doc_lengths, x, c, z, y)
    )
    other = [lax.ppermute(b, "c", ring(NC, 1)) for b in near]

    slot = jnp.arange(NQ, dtype=jnp.int32)
    digits = [
        lax.shift_right_logical(jnp.where(c == 0, LIVES[n][0], LIVES[n][1]), 3 * z) & 7
        for n in range(NX)
    ]
    lives = functools.reduce(
        lambda rest, n: jnp.where(slot // NY == n, digits[n], rest), range(NX), slot
    )
    query_block = PLANE * lax.rem(z + 1, NZ) + NY * lives + slot % NY
    slot = jnp.arange(NK, dtype=jnp.int32)
    group = (slot // NY) % PLANES
    plane = lax.rem(z + jnp.where(group == 0, 0, jnp.where(group == 1, NZ - 1, 1)), NZ)
    row = lax.rem(y + NY - slot % NY, NY)
    core = jnp.where(slot < PLANES * NY, c, 1 - c)
    key_block = PLANE * plane + 8 * row + 2 * x + core
    ends = jnp.sum(
        jnp.where(
            jnp.arange(16)[:, None] <= jnp.arange(16)[None, :], doc_lengths[:, None], 0
        ),
        axis=0,
    )
    token = query_block[:, None] * BLK + jnp.arange(BLK, dtype=jnp.int32)[None, :]
    start = jnp.max(jnp.where(ends[:, None, None] <= token[None], ends[:, None, None], 0), axis=0)
    first = jnp.max(
        jnp.where(ends[:, None] <= query_block[None] * BLK, ends[:, None], 0), axis=0
    )
    hit_query = (block_pairs[:, 0][None, :] == query_block[:, None]).astype(bf16)
    hit_key = (block_pairs[:, 1][None, :] == key_block[:, None]).astype(bf16)
    listed = lax.dot_general(
        hit_query, hit_key, (((1,), (1,)), ((), ())), preferred_element_type=jnp.float32
    )
    need = (
        (listed > 0.5)
        & (key_block[None, :] * BLK + (BLK - 1) >= first[:, None])
        & (key_block[None, :] <= query_block[:, None])
    )
    bits = jnp.left_shift(jnp.int32(1), slot)
    need = jnp.sum(jnp.where(need, bits[None, :], 0), axis=1)

    plan = pl.pallas_call(
        plan_kernel,
        out_shape=jax.ShapeDtypeStruct((PLAN,), jnp.int32),
        in_specs=[SMEM] * 3,
        out_specs=SMEM,
        compiler_params=SMALL,
        cost_estimate=LIGHT,
    )(need, query_block, key_block)
    parts = pl.pallas_call(
        attend_kernel,
        out_shape=jax.ShapeDtypeStruct((NQ, ROWS, BLK), bf16),
        in_specs=[SMEM, VMEM, VMEM, VMEM],
        out_specs=VMEM,
        scratch_shapes=[
            pltpu.VMEM((NQ + 1, DH, BLK), jnp.float32),
            pltpu.VMEM((NQ + 8, BLK), jnp.float32),
            pltpu.VMEM((NQ + 8, BLK), jnp.float32),
        ],
        compiler_params=pltpu.CompilerParams(vmem_limit_bytes=24 << 20),
    )(plan, start, mine, join([*near, *other]))

    gathered = lax.all_to_all(parts, ("x", "y"), 0, 0, tiled=True)
    result = pl.pallas_call(
        combine_kernel,
        out_shape=jax.ShapeDtypeStruct((BLK, H * DH), bf16),
        in_specs=[VMEM],
        out_specs=VMEM,
        compiler_params=SMALL,
        cost_estimate=LIGHT,
    )(gathered)
    return lax.ppermute(result, ("x", "c", "z", "y"), transpose_pairs(True))


def solution(mesh):
    fine = Mesh(mesh.devices.reshape(NX, NC, NZ, NY), ("x", "c", "z", "y"))
    return jax.shard_map(
        on_device,
        mesh=fine,
        in_specs=(
            P(("x", "c", "z", "y"), None),
            P(("z", "y", "x", "c"), None),
            P(("z", "y", "x", "c"), None),
            P(),
            P(),
        ),
        out_specs=P(("x", "c", "z", "y"), None),
        check_vma=False,
    )
```

```python
import functools
import math

import jax
import jax.numpy as jnp
from jax import lax
from jax.experimental import pallas as pl
from jax.experimental.pallas import tpu as pltpu
from jax.sharding import Mesh
from jax.sharding import PartitionSpec as P

H = 4
DH = 128
BLK = 128
NX, NC, NZ, NY = 4, 2, 8, 4
PLANE = 32
NQ = NX * NY
PLANES = 3
NK = PLANES * NY * NC
STAT_ROWS = 16
ROWS = DH + STAT_ROWS
UNROLL = 8
COUNT_AT = NQ * NK // 2 + UNROLL
QUERY_AT = COUNT_AT + 1
KEY_AT = QUERY_AT + NQ
PLAN = KEY_AT + NK + 1
NOWHERE = 1 << 20
NEG = -1e30
SCALE = math.log2(math.e) / math.sqrt(DH)


def device(x, c, z, y):
    return ((x * NC + c) * NZ + z) * NY + y


PLACE = [
    [5, 3, 1, 0, 6, 2, 4, 7],
    [5, 4, 7, 3, 1, 0, 6, 2],
    [7, 5, 6, 1, 3, 2, 0, 4],
    [0, 6, 7, 4, 5, 1, 3, 2],
    [2, 7, 0, 1, 3, 6, 5, 4],
    [5, 3, 2, 7, 1, 0, 6, 4],
    [7, 6, 4, 5, 3, 2, 1, 0],
    [5, 1, 7, 6, 0, 3, 4, 2],
]
LIVES = [
    [
        sum(PLACE[(z + 1) % NZ].index(2 * x + c) << (3 * z) for z in range(NZ))
        for c in range(NC)
    ]
    for x in range(NX)
]


def transpose_pairs(back):
    pairs = []
    for x in range(NX):
        for c in range(NC):
            for z in range(NZ):
                for y in range(NY):
                    p = 2 * x + c
                    home = device(x, c, z, y)
                    work = device(PLACE[p][z] // 2, PLACE[p][z] % 2, (p - 1) % NZ, y)
                    pairs.append((work, home) if back else (home, work))
    return pairs


def ring(n, d):
    return [(i, (i + d) % n) for i in range(n)]


def pack_queries_kernel(q_ref, out_ref):
    for h in range(H):
        part = q_ref[:, h * DH : (h + 1) * DH].T
        for x in range(NX):
            out_ref[x * H + h] = part


def pack_keys_kernel(y_ref, k_hbm, v_hbm, *refs):
    out_refs, (k_ref, v_ref, sems) = refs[:NY], refs[NY:]
    copies = [
        pltpu.make_async_copy(v_hbm, v_ref, sems.at[0]),
        pltpu.make_async_copy(k_hbm, k_ref, sems.at[1]),
    ]
    for copy in copies:
        copy.start()
    for copy in copies:
        copy.wait()
    for d, out_ref in enumerate(out_refs):
        at = pl.ds(pl.multiple_of(lax.rem(y_ref[0] + d, H) * DH, DH), DH)
        out_ref[0] = k_ref[:, at]
        out_ref[1] = v_ref[:, at].astype(jnp.float32).T.astype(jnp.bfloat16)


def join_kernel(*refs):
    at = 0
    for ref in refs[:-1]:
        refs[-1][at : at + ref.shape[0]] = ref[...]
        at += ref.shape[0]


def join(parts):
    count = sum(p.shape[0] for p in parts)
    return pl.pallas_call(
        join_kernel,
        out_shape=jax.ShapeDtypeStruct((count,) + parts[0].shape[1:], parts[0].dtype),
        in_specs=[VMEM] * len(parts),
        out_specs=VMEM,
        compiler_params=SMALL,
        cost_estimate=LIGHT,
    )(*parts)


def lowest_bit(mask):
    return 31 - lax.clz(mask & -mask)


def plan_kernel(need_ref, qblk_ref, kblk_ref, plan_ref):
    def list_row(j, count):
        plan_ref[QUERY_AT + j] = qblk_ref[j]

        def entry(carry):
            mask, count = carry
            rest = mask & (mask - 1)
            second = jnp.where(rest == 0, NK, lowest_bit(rest))
            plan_ref[count] = j * 1024 + lowest_bit(mask) * 32 + second
            return rest & (rest - 1), count + 1

        return lax.while_loop(lambda c: c[0] != 0, entry, (need_ref[j], count))[1]

    count = lax.fori_loop(0, NQ, list_row, jnp.int32(0))
    for u in range(UNROLL):
        plan_ref[count + u] = NQ * 1024 + NK * 32 + NK
    plan_ref[COUNT_AT] = count
    for s in range(NK):
        plan_ref[KEY_AT + s] = kblk_ref[s]
    plan_ref[KEY_AT + NK] = NOWHERE


def attend_kernel(plan_ref, start_ref, q_ref, kv_ref, out_ref, acc, top, total):
    acc[...] = jnp.zeros_like(acc)
    top[...] = jnp.full_like(top, NEG)
    total[...] = jnp.zeros_like(total)
    key_row = lax.broadcasted_iota(jnp.int32, (BLK, BLK), 0)
    lane = lax.broadcasted_iota(jnp.int32, (1, BLK), 1)

    def step(first, width):
        done = []
        for u in range(width):
            entry = plan_ref[first + u]
            j = lax.shift_right_logical(entry, 10)
            jq = jnp.minimum(j, NQ - 1)
            slots = (lax.shift_right_logical(entry, 5) & 31, entry & 31)
            held = [jnp.minimum(s, NK - 1) for s in slots]
            scores = jnp.dot(
                jnp.concatenate([kv_ref[s, 0] for s in held], axis=0),
                q_ref[jq],
                preferred_element_type=jnp.float32,
            )
            masked = []
            for n, s in enumerate(slots):
                base = plan_ref[KEY_AT + s] * BLK
                low = start_ref[pl.ds(jq, 1), :] - base
                high = plan_ref[QUERY_AT + jq] * BLK + lane - base
                allowed = (key_row >= low) & (key_row <= high)
                part = scores[n * BLK : (n + 1) * BLK]
                masked.append(jnp.where(allowed, part * SCALE, NEG))
            scores = jnp.concatenate(masked, axis=0)
            peak = jnp.max(scores, axis=0, keepdims=True)
            weights = jnp.exp2(scores - peak)
            mass = jnp.sum(weights, axis=0, keepdims=True)
            part = jnp.dot(
                jnp.concatenate([kv_ref[s, 1] for s in held], axis=1),
                weights.astype(jnp.bfloat16),
                preferred_element_type=jnp.float32,
            )
            done.append((j, peak, mass, part))
        for j, peak, mass, part in done:
            at = pl.ds(j, 1)
            old = top[at, :]
            new = jnp.maximum(old, peak)
            keep = jnp.exp2(old - new)
            gain = jnp.exp2(peak - new)
            top[at, :] = new
            total[at, :] = total[at, :] * keep + mass * gain
            acc[j] = acc[j] * keep + part * gain

    def wide(i, carry):
        step(i * (2 * UNROLL), 2 * UNROLL)
        return carry

    turns = (plan_ref[COUNT_AT] + UNROLL - 1) // UNROLL
    lax.fori_loop(0, turns // 2, wide, 0)

    @pl.when(turns % 2 == 1)
    def _():
        step((turns - 1) * UNROLL, UNROLL)

    mass = total[:NQ, :]
    some = mass > 0.0
    safe = jnp.where(some, mass, 1.0)
    inverse = 1.0 / safe
    level = jnp.where(some, top[:NQ, :] + jnp.log2(safe), NEG)
    first = level.astype(jnp.bfloat16).astype(jnp.float32)
    second = (level - first).astype(jnp.bfloat16).astype(jnp.float32)
    third = level - first - second
    row = lax.broadcasted_iota(jnp.int32, (STAT_ROWS, BLK), 0)
    for j in range(NQ):
        one = slice(j, j + 1)
        out_ref[j, :DH, :] = (acc[j] * inverse[one]).astype(jnp.bfloat16)
        stat = jnp.where(
            row == 0, first[one], jnp.where(row == 1, second[one], third[one])
        )
        out_ref[j, DH:, :] = jnp.where(row < 3, stat, 0.0).astype(jnp.bfloat16)


def combine_kernel(parts_ref, out_ref):
    for h in range(H):
        levels = []
        for r in range(NX):
            stat = parts_ref[r * H + h, DH:, :].astype(jnp.float32)
            levels.append(stat[0:1] + stat[1:2] + stat[2:3])
        peak = functools.reduce(jnp.maximum, levels)
        shares = [jnp.exp2(level - peak) for level in levels]
        inverse = 1.0 / functools.reduce(jnp.add, shares)
        value = functools.reduce(
            jnp.add,
            [
                parts_ref[r * H + h, :DH, :].astype(jnp.float32) * (shares[r] * inverse)
                for r in range(NX)
            ],
        )
        out_ref[:, h * DH : (h + 1) * DH] = value.T.astype(jnp.bfloat16)


VMEM = pl.BlockSpec(memory_space=pltpu.VMEM)
SMEM = pl.BlockSpec(memory_space=pltpu.SMEM)
LIGHT = pl.CostEstimate(flops=1024, bytes_accessed=1024, transcendentals=0)
HBM = pl.BlockSpec(memory_space=pltpu.HBM)
SMALL = pltpu.CompilerParams(vmem_limit_bytes=8 << 20)


def on_device(queries, keys, values, block_pairs, doc_lengths):
    x, c, z, y = (lax.axis_index(name) for name in ("x", "c", "z", "y"))
    bf16 = jnp.bfloat16

    piece = jax.ShapeDtypeStruct((2, BLK, DH), bf16)
    split = pl.pallas_call(
        pack_keys_kernel,
        out_shape=[piece] * NY,
        in_specs=[SMEM, HBM, HBM],
        out_specs=[VMEM] * NY,
        scratch_shapes=[pltpu.VMEM((BLK, H * DH), bf16)] * 2 + [pltpu.SemaphoreType.DMA((2,))],
        compiler_params=SMALL,
        cost_estimate=LIGHT,
    )(
        y.reshape(1),
        pltpu.with_memory_space_constraint(keys, pltpu.HBM),
        pltpu.with_memory_space_constraint(values, pltpu.HBM),
    )
    moved = lax.ppermute(queries, ("x", "c", "z", "y"), transpose_pairs(False))
    pieces = [split[0]] + [lax.ppermute(split[d], "y", ring(NY, d)) for d in range(1, NY)]
    here = join([p[None] for p in pieces])
    moved, here = lax.optimization_barrier((moved, here))

    spread = pl.pallas_call(
        pack_queries_kernel,
        out_shape=jax.ShapeDtypeStruct((NQ, DH, BLK), bf16),
        in_specs=[VMEM],
        out_specs=VMEM,
        compiler_params=SMALL,
        cost_estimate=LIGHT,
    )(moved)
    mine = lax.all_to_all(spread, ("x", "y"), 0, 0, tiled=True)
    near = [here, lax.ppermute(here, "z", ring(NZ, 1)), lax.ppermute(here, "z", ring(NZ, -1))]
    near[0], near[1], block_pairs, doc_lengths, x, c, z, y = lax.optimization_barrier(
        (near[0], near[1], block_pairs, doc_lengths, x, c, z, y)
    )
    other = [lax.ppermute(b, "c", ring(NC, 1)) for b in near]

    slot = jnp.arange(NQ, dtype=jnp.int32)
    digits = [
        lax.shift_right_logical(jnp.where(c == 0, LIVES[n][0], LIVES[n][1]), 3 * z) & 7
        for n in range(NX)
    ]
    lives = functools.reduce(
        lambda rest, n: jnp.where(slot // NY == n, digits[n], rest), range(NX), slot
    )
    query_block = PLANE * lax.rem(z + 1, NZ) + NY * lives + slot % NY
    slot = jnp.arange(NK, dtype=jnp.int32)
    group = (slot // NY) % PLANES
    plane = lax.rem(z + jnp.where(group == 0, 0, jnp.where(group == 1, NZ - 1, 1)), NZ)
    row = lax.rem(y + NY - slot % NY, NY)
    core = jnp.where(slot < PLANES * NY, c, 1 - c)
    key_block = PLANE * plane + 8 * row + 2 * x + core
    ends = jnp.sum(
        jnp.where(
            jnp.arange(16)[:, None] <= jnp.arange(16)[None, :], doc_lengths[:, None], 0
        ),
        axis=0,
    )
    token = query_block[:, None] * BLK + jnp.arange(BLK, dtype=jnp.int32)[None, :]
    start = jnp.max(jnp.where(ends[:, None, None] <= token[None], ends[:, None, None], 0), axis=0)
    first = jnp.max(
        jnp.where(ends[:, None] <= query_block[None] * BLK, ends[:, None], 0), axis=0
    )
    hit_query = (block_pairs[:, 0][None, :] == query_block[:, None]).astype(bf16)
    hit_key = (block_pairs[:, 1][None, :] == key_block[:, None]).astype(bf16)
    listed = lax.dot_general(
        hit_query, hit_key, (((1,), (1,)), ((), ())), preferred_element_type=jnp.float32
    )
    need = (
        (listed > 0.5)
        & (key_block[None, :] * BLK + (BLK - 1) >= first[:, None])
        & (key_block[None, :] <= query_block[:, None])
    )
    bits = jnp.left_shift(jnp.int32(1), jnp.arange(NK, dtype=jnp.int32))
    need = jnp.sum(jnp.where(need, bits[None, :], 0), axis=1)

    plan = pl.pallas_call(
        plan_kernel,
        out_shape=jax.ShapeDtypeStruct((PLAN,), jnp.int32),
        in_specs=[SMEM] * 3,
        out_specs=SMEM,
        compiler_params=SMALL,
        cost_estimate=LIGHT,
    )(need, query_block, key_block)
    parts = pl.pallas_call(
        attend_kernel,
        out_shape=jax.ShapeDtypeStruct((NQ, ROWS, BLK), bf16),
        in_specs=[SMEM, VMEM, VMEM, VMEM],
        out_specs=VMEM,
        scratch_shapes=[
            pltpu.VMEM((NQ + 1, DH, BLK), jnp.float32),
            pltpu.VMEM((NQ + 8, BLK), jnp.float32),
            pltpu.VMEM((NQ + 8, BLK), jnp.float32),
        ],
        compiler_params=pltpu.CompilerParams(vmem_limit_bytes=24 << 20),
    )(plan, start, mine, join([*near, *other]))

    gathered = lax.all_to_all(parts, ("x", "y"), 0, 0, tiled=True)
    result = pl.pallas_call(
        combine_kernel,
        out_shape=jax.ShapeDtypeStruct((BLK, H * DH), bf16),
        in_specs=[VMEM],
        out_specs=VMEM,
        compiler_params=SMALL,
        cost_estimate=LIGHT,
    )(gathered)
    return lax.ppermute(result, ("x", "c", "z", "y"), transpose_pairs(True))


def solution(mesh):
    fine = Mesh(mesh.devices.reshape(NX, NC, NZ, NY), ("x", "c", "z", "y"))
    return jax.shard_map(
        on_device,
        mesh=fine,
        in_specs=(
            P(("x", "c", "z", "y"), None),
            P(("z", "y", "x", "c"), None),
            P(("z", "y", "x", "c"), None),
            P(),
            P(),
        ),
        out_specs=P(("x", "c", "z", "y"), None),
        check_vma=False,
    )
```
